32 devices in a mesh: dp: 8 (over z, x), tensor: 4 (over y, core).
Axes of the slice: x: 2, y: 2, z: 4, core: 2. Of those that a mesh axis runs over, the one named last changes fastest.
Arguments:
- inputs: bfloat16 [8, 2048, 768], P('dp', 'tensor'), may hold values from -6 to 6
- cotangent: bfloat16 [8, 2048, 768], P('dp', 'tensor'), may hold values from -6 to 6
- lengths: int32 [8], P('dp'), may hold values from 512 to 2048, as said below
- query_index: int32 [8, 256], P('dp'), may hold values from 0 to 2047, as said below
- key_index: int32 [8, 256], P('dp'), may hold values from 0 to 2047, as said below
- token_index: int32 [8, 256], P('dp'), may hold values from 0 to 2047, as said below
- light_qkv: bfloat16 [3, 768, 512], P(None, 'dp', 'tensor'), may hold values from -0.21875 to 0.21875
- light_out: bfloat16 [512, 768], P('tensor', 'dp'), may hold values from -2 to 2
- heavy_qkv: bfloat16 [3, 768, 768], P(None, 'dp', 'tensor'), may hold values from -0.21875 to 0.21875
- heavy_out: bfloat16 [768, 768], P('tensor', 'dp'), may hold values from -3 to 3
- light_in: bfloat16 [2, 768, 1024], P(None, 'dp', 'tensor'), may hold values from -0.21875 to 0.21875
- light_down: bfloat16 [1024, 768], P('tensor', 'dp'), may hold values from -0.375 to 0.375
- heavy_in: bfloat16 [2, 768, 4096], P(None, 'dp', 'tensor'), may hold values from -0.21875 to 0.21875
- heavy_down: bfloat16 [4096, 768], P('tensor', 'dp'), may hold values from -0.25 to 0.25
- norm_gains: bfloat16 [2, 768], P(None, ('dp', 'tensor')), may hold values from 0.5 to 1.5
- routers: bfloat16 [3, 768], P(None, ('dp', 'tensor')), may hold values from -0.21875 to 0.21875
Outputs:
- output: bfloat16 [8, 2048, 768], P('dp', 'tensor')
- input_grad: float32 [8, 2048, 768], P('dp', 'tensor')
- light_qkv_grad: float32 [3, 768, 512], P(None, 'dp', 'tensor')
- light_out_grad: float32 [512, 768], P('tensor', 'dp')
- heavy_qkv_grad: float32 [3, 768, 768], P(None, 'dp', 'tensor')
- heavy_out_grad: float32 [768, 768], P('tensor', 'dp')
- light_in_grad: float32 [2, 768, 1024], P(None, 'dp', 'tensor')
- light_down_grad: float32 [1024, 768], P('tensor', 'dp')
- heavy_in_grad: float32 [2, 768, 4096], P(None, 'dp', 'tensor')
- heavy_down_grad: float32 [4096, 768], P('tensor', 'dp')
- gains_grad: float32 [2, 768], P(None, ('dp', 'tensor'))
- routers_grad: float32 [3, 768], P(None, ('dp', 'tensor'))
The draws below stay inside these ranges and needn't reach their ends.
Inputs may be any that keep to these rules, and one draw needn't show every extreme that they name: `lengths`: number of real positions of each slot; positions at or past it are padding; the first slot is full. `query_index`: each row holds 256 distinct positions of its slot in increasing order, all below the slot's length, among them position 0 and the slot's last real position. `key_index`: each row holds 256 distinct positions of its slot in increasing order, all below the slot's length, among them position 0 and the slot's last real position. `token_index`: each row holds 256 distinct positions of its slot in increasing order, all below the slot's length, among them position 0 and the slot's last real position.
All inputs are finite; a program needn't handle non-finite values.
Results may differ from the reference program's by a relative error of at most 0.023.
Values may be sent and summed in bfloat16 or wider, within the bound.
No kernel may reach another device: no remote copies, remote signals or barrier semaphores. Data moves between devices by JAX's collectives and lax.ppermute only.
A program may use at most 128 MiB of HBM per device.

```python
import jax
import jax.numpy as jnp
from jax import lax

D = 768
HEAD = 64
HEAVY_HEADS = 12
FL = 1024
FH = 4096
SLOT = 2048
WINDOW = 128
QBLOCK = 512
ROUTED = 256
HL = 512
HH = 768
SLOTS = 8


def slot_lengths(key):
    subkey = jax.random.fold_in(key, 7)
    drawn = jax.random.randint(subkey, (SLOTS,), SLOT // 4, SLOT + 1)
    drawn = drawn.at[0].set(SLOT)
    drawn = drawn.at[SLOTS - 1].set(SLOT // 4)
    return drawn.astype(jnp.int32)


def routed_rows(key, salt):
    limits = slot_lengths(key)
    subkey = jax.random.fold_in(key, salt)
    ranks = jax.random.randint(subkey, (SLOTS, SLOT), 0, 4096)
    positions = jnp.arange(SLOT, dtype=jnp.int32)
    ranks = jnp.where(positions[None, :] < limits[:, None], ranks, ranks + 8192)
    forced = (positions[None, :] == 0) | (positions[None, :] == limits[:, None] - 1)
    ranks = jnp.where(forced, -1, ranks)
    ordered = jnp.argsort(ranks * SLOT + positions[None, :], axis=1)
    chosen = jnp.sort(ordered[:, :ROUTED], axis=1)
    return chosen.astype(jnp.int32)


def draw_lengths(key, part):
    return slot_lengths(key)


def draw_query_index(key, part):
    return routed_rows(key, 11)


def draw_key_index(key, part):
    return routed_rows(key, 13)


def draw_token_index(key, part):
    return routed_rows(key, 17)


def strengthened(array, key, source, target, blocks, factor):
    def block_of(axis_at):
        return (jnp.arange(array.shape[axis_at]) // (array.shape[axis_at] // blocks)).reshape((-1,) + (1,) * (array.ndim - 1 - axis_at))

    first = jax.random.permutation(key, blocks)[block_of(target)]
    other_side = (block_of(target) + blocks // 2) % blocks
    return jnp.where((block_of(source) == first) | (block_of(source) == other_side), factor * array, array)


def block_levels(stream_key, extent, pieces, least, high):
    level, own = 1.0, jax.random.fold_in(stream_key, 6)
    for axis_at, blocks in pieces:
        draws = jnp.exp(jax.random.uniform(jax.random.fold_in(own, axis_at), (blocks,), jnp.float32, least / len(pieces), high / len(pieces)))
        level = level * jnp.repeat(draws, extent[axis_at] // blocks).reshape([-1 if axis == axis_at else 1 for axis in range(len(extent))])
    return level


def gaussian(stream_key, shape, deviation, most, shards=(), kind=jnp.bfloat16):
    values = deviation * jax.random.normal(stream_key, shape, jnp.float32)
    if shards:
        values = values * block_levels(stream_key, shape, shards, -0.22, 0.18)
    return jnp.clip(values, -most, most).astype(kind)


def noise_with(stream_key, shape, width, most, split, heavy, kind=jnp.bfloat16):
    values = width * jax.random.normal(stream_key, shape, jnp.float32)
    if split:
        values = values * block_levels(stream_key, shape, split, -0.22, 0.18)
    return jnp.clip(strengthened(values, jax.random.fold_in(stream_key, 3), *heavy), -most, most).astype(kind)


def setup_inputs(seed: int = 0) -> dict:
    arg_keys = jax.random.split(jax.random.key(seed), 17)
    inputs = gaussian(arg_keys[0], (SLOTS, SLOT, D), 1.0, 6.0, ((0, 8), (1, 4)))
    cotangent = noise_with(arg_keys[1], (SLOTS, SLOT, D), 1.0, 6.0, ((0, 8), (1, 4)), (0, 2, 8, 2.0))
    lengths = draw_lengths(jax.random.fold_in(arg_keys[16], 71), 0)
    query_index = draw_query_index(jax.random.fold_in(arg_keys[16], 71), 0)
    key_index = draw_key_index(jax.random.fold_in(arg_keys[16], 71), 0)
    token_index = draw_token_index(jax.random.fold_in(arg_keys[16], 71), 0)
    light_qkv = gaussian(arg_keys[6], (3, D, HL), D ** -0.5, 0.21875, ((1, 8), (2, 4)))
    light_out = gaussian(arg_keys[7], (HL, D), 8 ** -0.5, 2.0, ((0, 4), (1, 8)))
    heavy_qkv = gaussian(arg_keys[8], (3, D, HH), D ** -0.5, 0.21875, ((1, 8), (2, 4)))
    heavy_out = gaussian(arg_keys[9], (HH, D), 4 ** -0.5, 3.0, ((0, 4), (1, 8)))
    light_in = gaussian(arg_keys[10], (2, D, FL), D ** -0.5, 0.21875, ((1, 8), (2, 4)))
    light_down = gaussian(arg_keys[11], (FL, D), (FL // 4) ** -0.5, 0.375, ((0, 4), (1, 8)))
    heavy_in = gaussian(arg_keys[12], (2, D, FH), D ** -0.5, 0.21875, ((1, 8), (2, 4)))
    heavy_down = gaussian(arg_keys[13], (FH, D), (FH // 8) ** -0.5, 0.25, ((0, 4), (1, 8)))
    norm_gains = jnp.clip(1.0 + 0.1 * jax.random.normal(arg_keys[14], (2, D), jnp.float32), 0.5, 1.5).astype(jnp.bfloat16)
    routers = gaussian(arg_keys[15], (3, D), D ** -0.5, 0.21875, ((1, 32),))
    return dict(inputs=inputs, cotangent=cotangent, lengths=lengths, query_index=query_index, key_index=key_index, token_index=token_index, light_qkv=light_qkv, light_out=light_out, heavy_qkv=heavy_qkv, heavy_out=heavy_out, light_in=light_in, light_down=light_down, heavy_in=heavy_in, heavy_down=heavy_down, norm_gains=norm_gains, routers=routers)


HIGHEST = lax.Precision.HIGHEST
NORM_EPS = 1e-06
SCORE_SCALE = 0.125
MASKED = -1e+30

@jax.custom_vjp
def low(v):
    return lax.optimization_barrier(v.astype(jnp.bfloat16)).astype(jnp.float32)

@jax.custom_vjp
def low_back(v):
    return v

def low_keep(v):
    return (low(v), None)

def low_pass(kept, grad):
    return (grad,)

def back_keep(v):
    return (v, None)

def back_low(kept, grad):
    return (low(grad),)
low.defvjp(low_keep, low_pass)
low_back.defvjp(back_keep, back_low)

def matmul_high(left, right):
    return jnp.dot(left, right, precision=HIGHEST, preferred_element_type=jnp.float32)

def rms_norm(values, gain):
    return values * lax.rsqrt(lax.optimization_barrier(jnp.mean(values * values, axis=-1, keepdims=True)) + NORM_EPS) * gain

def gelu_product(gate, upper):
    return jax.nn.gelu(gate, approximate=True) * upper

def attend_scores(q_block, k_block, v_block, mask):
    scores = low_back(jnp.einsum('qhe,khe->hqk', q_block, k_block, precision=HIGHEST) * SCORE_SCALE)
    scores = jnp.where(mask[None, :, :], scores, MASKED)
    row_max = lax.optimization_barrier(jnp.max(scores, axis=-1, keepdims=True))
    exp_terms = jnp.exp(scores - row_max)
    probs = low(exp_terms / lax.optimization_barrier(jnp.sum(exp_terms, axis=-1, keepdims=True)))
    return jnp.einsum('hqk,khe->qhe', probs, v_block, precision=HIGHEST)

def band_mask(block_start, length):
    q_pos = block_start + jnp.arange(QBLOCK, dtype=jnp.int32)
    k_pos = block_start - WINDOW + jnp.arange(QBLOCK + 2 * WINDOW, dtype=jnp.int32)
    near = jnp.abs(q_pos[:, None] - k_pos[None, :]) < WINDOW
    inside = (k_pos[None, :] >= 0) & (k_pos[None, :] < SLOT)
    allowed = (k_pos[None, :] < length) | (q_pos[:, None] >= length)
    return near & inside & allowed

def local_attention(queries, keys, values, length):
    head_count = queries.shape[1] // HEAD
    q_heads = queries.reshape(SLOT, head_count, HEAD)
    padding = ((WINDOW, WINDOW), (0, 0), (0, 0))
    k_padded = jnp.pad(keys.reshape(SLOT, head_count, HEAD), padding)
    v_padded = jnp.pad(values.reshape(SLOT, head_count, HEAD), padding)

    def block(block_index):
        block_start = block_index * QBLOCK
        q_block = lax.dynamic_slice_in_dim(q_heads, block_start, QBLOCK, 0)
        k_block = lax.dynamic_slice_in_dim(k_padded, block_start, QBLOCK + 2 * WINDOW, 0)
        v_block = lax.dynamic_slice_in_dim(v_padded, block_start, QBLOCK + 2 * WINDOW, 0)
        return attend_scores(q_block, k_block, v_block, band_mask(block_start, length))
    blocks = lax.map(jax.checkpoint(block), jnp.arange(SLOT // QBLOCK, dtype=jnp.int32))
    return blocks.reshape(SLOT, head_count * HEAD)

def slot_forward(params, slot_inputs, length, q_index, k_index, f_index):
    light_qkv, light_out, heavy_qkv, heavy_out, light_in, light_down, heavy_in, heavy_down, norm_gains, routers = params
    positions = jnp.arange(SLOT, dtype=jnp.int32)
    valid_mask = (positions < length).astype(jnp.float32)[:, None]
    first = low(rms_norm(slot_inputs, norm_gains[0]))
    light_q = low_back(low(matmul_high(first, light_qkv[0])))
    light_k = low_back(low(matmul_high(first, light_qkv[1])))
    light_v = low_back(low(matmul_high(first, light_qkv[2])))
    light_heads = low_back(low(local_attention(light_q, light_k, light_v, length)))
    attn_sum = matmul_high(light_heads, light_out)
    q_rows = first[q_index]
    k_rows = first[k_index]
    q_score = jax.nn.sigmoid(matmul_high(q_rows, routers[0]))
    k_score = jax.nn.sigmoid(matmul_high(k_rows, routers[1]))
    key_value_rows = low(k_score[:, None] * k_rows)
    heavy_q = low_back(low(matmul_high(q_rows, heavy_qkv[0])))
    heavy_k = low_back(low(matmul_high(key_value_rows, heavy_qkv[1])))
    heavy_v = low_back(low(matmul_high(key_value_rows, heavy_qkv[2])))
    head_shape = (ROUTED, HEAVY_HEADS, HEAD)
    full_mask = jnp.ones((ROUTED, ROUTED), dtype=bool)
    heavy_heads = attend_scores(heavy_q.reshape(head_shape), heavy_k.reshape(head_shape), heavy_v.reshape(head_shape), full_mask)
    heavy_heads = low_back(low(heavy_heads.reshape(ROUTED, HH)))
    heavy_proj = low_back(matmul_high(heavy_heads, heavy_out))
    attn_sum = low_back(attn_sum + jnp.zeros_like(attn_sum).at[q_index].add(q_score[:, None] * heavy_proj))
    middle = slot_inputs + valid_mask * attn_sum
    second = low(rms_norm(middle, norm_gains[1]))
    gate = low_back(matmul_high(second, light_in[0]))
    upper = low_back(matmul_high(second, light_in[1]))
    light_hidden = low_back(low(gelu_product(gate, upper)))
    feed_sum = matmul_high(light_hidden, light_down)
    f_rows = second[f_index]
    f_score = jax.nn.sigmoid(matmul_high(f_rows, routers[2]))
    heavy_gate = low_back(matmul_high(f_rows, heavy_in[0]))
    heavy_up = low_back(matmul_high(f_rows, heavy_in[1]))
    heavy_hidden = low_back(low(gelu_product(heavy_gate, heavy_up)))
    heavy_feed = low_back(matmul_high(heavy_hidden, heavy_down))
    feed_sum = low_back(feed_sum + jnp.zeros_like(feed_sum).at[f_index].add(f_score[:, None] * heavy_feed))
    return middle + valid_mask * feed_sum

def reference(inputs, cotangent, lengths, query_index, key_index, token_index, light_qkv, light_out, heavy_qkv, heavy_out, light_in, light_down, heavy_in, heavy_down, norm_gains, routers):
    params = (light_qkv.astype(jnp.float32), light_out.astype(jnp.float32), heavy_qkv.astype(jnp.float32), heavy_out.astype(jnp.float32), light_in.astype(jnp.float32), light_down.astype(jnp.float32), heavy_in.astype(jnp.float32), heavy_down.astype(jnp.float32), norm_gains.astype(jnp.float32), routers.astype(jnp.float32))

    def forward(weights, acts):

        def per_slot(item):
            return slot_forward(weights, item[0], item[1], item[2], item[3], item[4])
        return lax.map(jax.checkpoint(per_slot), (acts, lengths, query_index, key_index, token_index))
    result, pull = jax.vjp(forward, params, inputs.astype(jnp.float32))
    positions = jnp.arange(SLOT, dtype=jnp.int32)
    valid_mask = (positions[None, :] < lengths[:, None]).astype(jnp.float32)[:, :, None]
    weight_grads, input_grad = pull(valid_mask * cotangent.astype(jnp.float32))
    return (result.astype(jnp.bfloat16), input_grad, weight_grads[0], weight_grads[1], weight_grads[2], weight_grads[3], weight_grads[4], weight_grads[5], weight_grads[6], weight_grads[7], weight_grads[8], weight_grads[9])
```

```python
import jax
import jax.numpy as jnp
from jax import lax
from jax.sharding import PartitionSpec as P

HEAD = 64
SLOT = 2048
WINDOW = 128
ROUTED = 256
NORM_EPS = 1e-06
SCALE = 0.125
MASKED = -1e30
F32 = jnp.float32
BF16 = jnp.bfloat16


def rms_norm(values, gain):
    return values * lax.rsqrt(jnp.mean(values * values, axis=-1, keepdims=True) + NORM_EPS) * gain


def gelu_product(gate, upper):
    return jax.nn.gelu(gate, approximate=True) * upper


def mm(left, right, dims):
    return lax.dot_general(left, right, (dims, ((), ())), preferred_element_type=F32)


def nn(left, right):
    return mm(left, right, ((1,), (0,)))


def nt(left, right):
    return mm(left, right, ((1,), (1,)))


def tn(left, right):
    return mm(left, right, ((0,), (0,)))


def swap(values, axis, bit):
    size = lax.axis_size(axis)
    return lax.ppermute(values, axis, [(i, i ^ bit) for i in range(size)])


def bits_of(axis):
    size = lax.axis_size(axis)
    bits = []
    bit = 1
    while bit < size:
        bits.append(bit)
        bit *= 2
    return bits


def gather(block, axis):
    index = lax.axis_index(axis)
    have = block[None]
    for bit in reversed(bits_of(axis)):
        got = swap(have, axis, bit)
        high = (index & bit) != 0
        first = jnp.where(high, got, have)
        second = jnp.where(high, have, got)
        have = jnp.stack([first, second], axis=1).reshape((-1,) + block.shape)
    return have


def scatter(blocks, axis, last=None):
    index = lax.axis_index(axis)
    bits = bits_of(axis)
    for bit in bits:
        pairs = blocks.reshape((-1, 2) + blocks.shape[1:])
        high = ((index & bit) != 0).astype(jnp.int32)
        keep = lax.dynamic_index_in_dim(pairs, high, 1, keepdims=False)
        send = lax.dynamic_index_in_dim(pairs, 1 - high, 1, keepdims=False)
        got = swap(send, axis, bit)
        kind = last if (last is not None and bit == bits[-1]) else blocks.dtype
        blocks = (keep.astype(F32) + got.astype(F32)).astype(kind)
    return blocks[0]


def tensor_sum(halves):
    core = lax.axis_index("tensor") & 1
    mine = lax.dynamic_index_in_dim(halves, core, 0, keepdims=False)
    other = lax.dynamic_index_in_dim(halves, 1 - core, 0, keepdims=False)

    def add(left, right):
        return (left.astype(F32) + right.astype(F32)).astype(left.dtype)

    mine = add(mine, swap(other, "tensor", 1))
    mine = add(mine, swap(mine, "tensor", 2))
    other = swap(mine, "tensor", 1)
    high = core == 1
    return jnp.stack([jnp.where(high, other, mine), jnp.where(high, mine, other)])


def sum_rows(rows):
    half = rows.shape[0] // 2
    return tensor_sum(rows.reshape((2, half) + rows.shape[1:])).reshape(rows.shape)


def neighbours(values_first, values_last):
    size = lax.axis_size("tensor")
    before = lax.ppermute(values_last, "tensor", [(i, i + 1) for i in range(size - 1)])
    after = lax.ppermute(values_first, "tensor", [(i + 1, i) for i in range(size - 1)])
    return before, after


def local_mask(start, length, blocks):
    q_pos = start + WINDOW * jnp.arange(blocks)[:, None, None] + jnp.arange(WINDOW)[None, :, None]
    k_pos = start + WINDOW * (jnp.arange(blocks)[:, None, None] - 1) + jnp.arange(3 * WINDOW)[None, None, :]
    near = jnp.abs(q_pos - k_pos) < WINDOW
    inside = (k_pos >= 0) & (k_pos < SLOT)
    allowed = (k_pos < length) | (q_pos >= length)
    return near & inside & allowed


def split_blocks(qkv):
    rows = qkv.shape[0]
    parts = qkv.reshape(rows // WINDOW, WINDOW, 4, 3, 2, HEAD)
    blocks = rows // WINDOW - 2
    q = parts[1:-1, :, :, 0]
    windows = jnp.concatenate([parts[0:blocks], parts[1 : blocks + 1], parts[2 : blocks + 2]], axis=1)
    return q, windows[:, :, :, 1], windows[:, :, :, 2]


def local_forward(qkv, start, length):
    q, k, v = split_blocks(qkv)
    blocks = q.shape[0]
    mask = local_mask(start, length, blocks)[:, None, None]
    s = jnp.einsum("bqthe,bkthe->bthqk", q, k, preferred_element_type=F32) * SCALE
    s = jnp.where(mask, s, MASKED)
    top = jnp.max(s, axis=-1, keepdims=True)
    e = jnp.exp(s - top)
    total = jnp.sum(e, axis=-1, keepdims=True)
    p = (e / total).astype(BF16)
    lse = top + jnp.log(total)
    o = jnp.einsum("bthqk,bkthe->bqthe", p, v, preferred_element_type=F32).astype(BF16)
    return o.reshape(blocks * WINDOW, -1), lse


def local_backward(qkv, lse, grad_o, start, length):
    q, k, v = split_blocks(qkv)
    blocks = q.shape[0]
    g = grad_o.reshape(blocks, WINDOW, 4, 2, HEAD)
    mask = local_mask(start, length, blocks)[:, None, None]
    s = jnp.einsum("bqthe,bkthe->bthqk", q, k, preferred_element_type=F32) * SCALE
    p = jnp.where(mask, jnp.exp(jnp.where(mask, s, MASKED) - lse), 0.0)
    dv = jnp.einsum("bthqk,bqthe->bkthe", p.astype(BF16), g, preferred_element_type=F32)
    dp = jnp.einsum("bqthe,bkthe->bthqk", g, v, preferred_element_type=F32)
    ds = (p * (dp - jnp.sum(p * dp, axis=-1, keepdims=True))).astype(BF16)
    dq = jnp.einsum("bthqk,bkthe->bqthe", ds, k, preferred_element_type=F32) * SCALE
    dk = jnp.einsum("bthqk,bqthe->bkthe", ds, q, preferred_element_type=F32) * SCALE

    def spread(x):
        x = x.reshape(blocks, 3, WINDOW, 4, 128)
        out = jnp.zeros((blocks + 2, WINDOW, 4, 128), F32)
        for j in range(3):
            out = out.at[j : j + blocks].add(x[:, j])
        return out.reshape(-1, 4, 128)

    return dq.reshape(blocks * WINDOW, 4, 128), spread(dk), spread(dv)


def heavy_forward(hq, hk, hv):
    outs = []
    lses = []
    for h in range(hq.shape[1] // HEAD):
        cut = slice(h * HEAD, (h + 1) * HEAD)
        s = nt(hq[:, cut], hk[:, cut]) * SCALE
        top = jnp.max(s, axis=-1, keepdims=True)
        e = jnp.exp(s - top)
        total = jnp.sum(e, axis=-1, keepdims=True)
        outs.append(nn((e / total).astype(BF16), hv[:, cut]))
        lses.append(top + jnp.log(total))
    return jnp.concatenate(outs, axis=1).astype(BF16), lses


def heavy_backward(hq, hk, hv, lses, grad_o):
    dqs, dks, dvs = [], [], []
    for h in range(hq.shape[1] // HEAD):
        cut = slice(h * HEAD, (h + 1) * HEAD)
        q, k, v, g = hq[:, cut], hk[:, cut], hv[:, cut], grad_o[:, cut]
        p = jnp.exp(nt(q, k) * SCALE - lses[h])
        dvs.append(tn(p.astype(BF16), g))
        dp = nt(g, v)
        ds = (p * (dp - jnp.sum(p * dp, axis=-1, keepdims=True))).astype(BF16)
        dqs.append(nn(ds, k) * SCALE)
        dks.append(tn(ds, q) * SCALE)
    return [jnp.concatenate(parts, axis=1).astype(BF16) for parts in (dqs, dks, dvs)]


def local(
    inputs, cotangent, lengths, query_index, key_index, token_index,
    light_qkv, light_out, heavy_qkv, heavy_out, light_in, light_down, heavy_in, heavy_down,
    norm_gains, routers,
):
    rows, width = inputs.shape[1], inputs.shape[2]
    shard = light_qkv.shape[1]
    dp = lax.axis_size("dp")
    tensor = lax.axis_size("tensor")
    length = lengths[0]
    start = lax.axis_index("tensor") * rows
    own_pos = start + jnp.arange(rows, dtype=jnp.int32)
    valid = (own_pos < length).astype(F32)[:, None]

    def one_hot(index):
        return (index[:, None] == own_pos[None, :]).astype(BF16)

    hot_q, hot_k, hot_f = one_hot(query_index[0]), one_hot(key_index[0]), one_hot(token_index[0])

    small = jnp.concatenate([norm_gains, routers], axis=0)
    small = gather(gather(small, "tensor"), "dp")
    small = small.transpose(2, 0, 1, 3).reshape(5, width).astype(F32)
    gains, router = small[:2], small[2:]

    def flat(w):
        return w.transpose(1, 0, 2).reshape(shard, -1)

    def dp_gather(parts):
        packed = jnp.concatenate(parts, axis=1)
        return gather(packed, "dp").reshape(dp * shard, -1)

    c_lqkv, c_hqkv = 3 * light_qkv.shape[2], heavy_qkv.shape[2]
    c_lout, c_hout = light_out.shape[0], heavy_out.shape[0]
    c_lin, c_ldown = light_in.shape[2], light_down.shape[0]
    c_hin = heavy_in.shape[2]
    w1 = dp_gather([flat(light_qkv), flat(heavy_qkv)])
    w_lqkv = gather(w1[:, :c_lqkv], "tensor")
    w_hqkv = w1[:, c_lqkv:]
    w2 = dp_gather([light_out.T, flat(light_in), light_down.T, heavy_out.T])
    w_light = gather(w2[:, : c_lout + 2 * c_lin + c_ldown], "tensor")
    w_hout = w2[:, c_lout + 2 * c_lin + c_ldown :]
    w_hin = dp_gather([flat(heavy_in)])
    w_hdown = dp_gather([heavy_down.T])
    w_lout = w_light[:, :, :c_lout]
    w_lin = w_light[:, :, c_lout : c_lout + 2 * c_lin]
    w_ldown = w_light[:, :, c_lout + 2 * c_lin :]

    own = inputs[0]
    before, after = neighbours(own[:WINDOW], own[rows - WINDOW :])
    x = own.astype(F32)
    wide = jnp.concatenate([before, own, after], axis=0).astype(F32)
    a1_wide = rms_norm(wide, gains[0]).astype(BF16)
    a1 = a1_wide[WINDOW : WINDOW + rows]
    picked = jnp.stack([nn(hot_q, a1), nn(hot_k, a1)]).astype(BF16)
    picked = tensor_sum(picked)
    q_rows, k_rows = picked[0], picked[1]
    q_rows32, k_rows32 = q_rows.astype(F32), k_rows.astype(F32)
    sq = jax.nn.sigmoid(jnp.sum(q_rows32 * router[0], axis=-1, keepdims=True))
    sk = jax.nn.sigmoid(jnp.sum(k_rows32 * router[1], axis=-1, keepdims=True))
    kvin = (sk * k_rows32).astype(BF16)
    hq = nn(q_rows, w_hqkv[:, :c_hqkv]).astype(BF16)
    hk = nn(kvin, w_hqkv[:, c_hqkv : 2 * c_hqkv]).astype(BF16)
    hv = nn(kvin, w_hqkv[:, 2 * c_hqkv :]).astype(BF16)
    ho, hlse = heavy_forward(hq, hk, hv)
    hy = nt(ho, w_hout)
    routed = sum_rows((sq * hy).astype(BF16))

    qkv = jnp.concatenate([nn(a1_wide, w_lqkv[t]) for t in range(tensor)], axis=1).astype(BF16)
    lo, lse = local_forward(qkv, start, length)
    attn = sum(nt(lo[:, t * c_lout : (t + 1) * c_lout], w_lout[t]) for t in range(tensor))
    attn = attn + tn(hot_q, routed)
    mid = x + valid * attn

    a2 = rms_norm(mid, gains[1]).astype(BF16)
    gfeed = (valid * cotangent[0].astype(F32)).astype(BF16)
    f_rows = sum_rows(nn(hot_f, a2).astype(BF16))
    gf = sum_rows(nn(hot_f, gfeed).astype(BF16)).astype(F32)
    feed = 0.0
    da2 = 0.0
    light_grads = []
    for t in range(tensor):
        gu = nn(a2, w_lin[t])
        gate, up = gu[:, :c_lin], gu[:, c_lin:]
        lh, pull = jax.vjp(gelu_product, gate, up)
        lh = lh.astype(BF16)
        feed = feed + nt(lh, w_ldown[t])
        dlh = nn(gfeed, w_ldown[t]).astype(BF16)
        dgate, dup = pull(dlh.astype(F32))
        dgu = jnp.concatenate([dgate, dup], axis=1).astype(BF16)
        da2 = da2 + nt(dgu, w_lin[t])
        light_grads.append(jnp.concatenate([tn(a2, dgu), tn(gfeed, lh)], axis=1).astype(BF16))
    f_rows32 = f_rows.astype(F32)
    sf = jax.nn.sigmoid(jnp.sum(f_rows32 * router[2], axis=-1, keepdims=True))
    hgu = nn(f_rows, w_hin)
    hh, pull = jax.vjp(gelu_product, hgu[:, :c_hin], hgu[:, c_hin:])
    hh = hh.astype(BF16)
    hf = nt(hh, w_hdown)
    feed = feed + tn(hot_f, sum_rows((sf * hf).astype(BF16)))
    output = mid + valid * feed
    dsf = jnp.sum(gf * hf, axis=-1, keepdims=True)
    tf = (sf * gf).astype(BF16)
    dhh = nn(tf, w_hdown).astype(BF16)
    dhgate, dhup = pull(dhh.astype(F32))
    dhgu = jnp.concatenate([dhgate, dhup], axis=1).astype(BF16)
    wf = dsf * sf * (1.0 - sf)
    daf = nt(dhgu, w_hin) + wf * router[2]
    da2 = da2 + tn(hot_f, sum_rows(daf.astype(BF16)))
    grad_router_f = jnp.sum(wf * f_rows32, axis=0)
    g_hff = jnp.concatenate([tn(f_rows, dhgu), tn(tf, hh)], axis=1).astype(BF16)
    g_hff = scatter(g_hff.reshape(dp, shard, -1), "dp", F32)
    g_lff = scatter(jnp.stack(light_grads), "tensor")
    g_lff = scatter(g_lff.reshape(dp, shard, -1), "dp", F32)

    _, pull_norm2 = jax.vjp(rms_norm, mid, gains[1])
    dmid_norm, grad_gain2 = pull_norm2(da2)
    dmid = gfeed.astype(F32) + dmid_norm
    gattn = (valid * dmid).astype(BF16)

    ga = sum_rows(nn(hot_q, gattn).astype(BF16)).astype(F32)
    dsq = jnp.sum(ga * hy, axis=-1, keepdims=True)
    tq = (sq * ga).astype(BF16)
    dho = nn(tq, w_hout).astype(BF16)
    dhq, dhk, dhv = heavy_backward(hq, hk, hv, hlse, dho)
    dkv = nt(dhk, w_hqkv[:, c_hqkv : 2 * c_hqkv]) + nt(dhv, w_hqkv[:, 2 * c_hqkv :])
    wq = dsq * sq * (1.0 - sq)
    wk = jnp.sum(dkv * k_rows32, axis=-1, keepdims=True) * sk * (1.0 - sk)
    dq_rows = nt(dhq, w_hqkv[:, :c_hqkv]) + wq * router[0]
    dk_rows = sk * dkv + wk * router[1]
    routed_grads = tensor_sum(jnp.stack([dq_rows, dk_rows]).astype(BF16))
    grad_router_q = jnp.sum(wq * q_rows32, axis=0)
    grad_router_k = jnp.sum(wk * k_rows32, axis=0)
    g_hattn = jnp.concatenate([tn(q_rows, dhq), tn(kvin, dhk), tn(kvin, dhv), tn(tq, ho)], axis=1).astype(BF16)
    g_hattn = scatter(g_hattn.reshape(dp, shard, -1), "dp", F32)

    dlo = jnp.concatenate([nn(gattn, w_lout[t]) for t in range(tensor)], axis=1).astype(BF16)
    dlq, dlk, dlv = local_backward(qkv, lse, dlo, start, length)
    edge = jnp.stack([dlk, dlv]).astype(F32)
    first, last = edge[:, :WINDOW].astype(BF16), edge[:, rows + WINDOW :].astype(BF16)
    from_before, from_after = neighbours(first, last)
    body = edge[:, WINDOW : WINDOW + rows]
    body = jnp.concatenate(
        [
            body[:, :WINDOW] + from_before.astype(F32),
            body[:, WINDOW : rows - WINDOW],
            body[:, rows - WINDOW :] + from_after.astype(F32),
        ],
        axis=1,
    )
    dqkv = jnp.stack([dlq, body[0], body[1]], axis=2).astype(BF16).reshape(rows, tensor, c_lqkv)
    da1 = sum(nt(dqkv[:, t], w_lqkv[t]) for t in range(tensor))
    g_lattn = jnp.stack(
        [
            jnp.concatenate([tn(a1, dqkv[:, t]), tn(gattn, lo[:, t * c_lout : (t + 1) * c_lout])], axis=1)
            for t in range(tensor)
        ]
    ).astype(BF16)
    g_lattn = scatter(g_lattn, "tensor")
    g_lattn = scatter(g_lattn.reshape(dp, shard, -1), "dp", F32)
    da1 = da1 + tn(hot_q, routed_grads[0]) + tn(hot_k, routed_grads[1])
    _, pull_norm1 = jax.vjp(rms_norm, x, gains[0])
    dx_norm, grad_gain1 = pull_norm1(da1)
    input_grad = dmid + dx_norm

    small_grads = jnp.stack([grad_gain1, grad_gain2, grad_router_q, grad_router_k, grad_router_f])
    small_grads = small_grads.reshape(5, dp, tensor, -1).transpose(1, 2, 0, 3)
    small_grads = scatter(scatter(small_grads, "dp"), "tensor")

    def unflat(grad, count):
        return grad.reshape(shard, count, -1).transpose(1, 0, 2)

    return (
        output[None].astype(BF16),
        input_grad[None],
        unflat(g_lattn[:, :c_lqkv], 3),
        g_lattn[:, c_lqkv:].T,
        unflat(g_hattn[:, : 3 * c_hqkv], 3),
        g_hattn[:, 3 * c_hqkv :].T,
        unflat(g_lff[:, : 2 * c_lin], 2),
        g_lff[:, 2 * c_lin :].T,
        unflat(g_hff[:, : 2 * c_hin], 2),
        g_hff[:, 2 * c_hin :].T,
        small_grads[:2],
        small_grads[2:],
    )


def solution(mesh):
    rows = P("dp", "tensor", None)
    index = P("dp", None)
    cols = P(None, "dp", "tensor")
    back = P("tensor", "dp")
    both = P(None, ("dp", "tensor"))
    weights = (cols, back) * 4
    return jax.shard_map(
        local,
        mesh=mesh,
        in_specs=(rows, rows, P("dp"), index, index, index) + weights + (both, both),
        out_specs=(rows, rows) + weights + (both, both),
        check_vma=False,
    )
```

```python
import jax
import jax.numpy as jnp
import numpy as np
from jax import lax
from jax.experimental import pallas as pl
from jax.experimental.pallas import tpu as pltpu
from jax.sharding import PartitionSpec as P

HEAD = 64
SLOT = 2048
WINDOW = 128
ROUTED = 256
NORM_EPS = 1e-06
SCALE = 0.125
MASKED = -1e30
F32 = jnp.float32
BF16 = jnp.bfloat16


def rms_norm(values, gain):
    return values * lax.rsqrt(jnp.mean(values * values, axis=-1, keepdims=True) + NORM_EPS) * gain


def gelu_product(gate, upper):
    return jax.nn.gelu(gate, approximate=True) * upper


def mm(left, right, dims):
    return lax.dot_general(left, right, (dims, ((), ())), preferred_element_type=F32)


def nn(left, right):
    return mm(left, right, ((1,), (0,)))


def nt(left, right):
    return mm(left, right, ((1,), (1,)))


def tn(left, right):
    return mm(left, right, ((0,), (0,)))


def swap(values, axis, bit):
    size = lax.axis_size(axis)
    return lax.ppermute(values, axis, [(i, i ^ bit) for i in range(size)])


def bits_of(axis):
    size = lax.axis_size(axis)
    bits = []
    bit = 1
    while bit < size:
        bits.append(bit)
        bit *= 2
    return bits


def gather(block, axis):
    index = lax.axis_index(axis)
    have = block[None]
    for bit in reversed(bits_of(axis)):
        got = swap(have, axis, bit)
        high = (index & bit) != 0
        first = jnp.where(high, got, have)
        second = jnp.where(high, have, got)
        have = jnp.stack([first, second], axis=1).reshape((-1,) + block.shape)
    return have


def scatter(blocks, axis, last=None):
    index = lax.axis_index(axis)
    bits = bits_of(axis)
    for bit in bits:
        pairs = blocks.reshape((-1, 2) + blocks.shape[1:])
        high = ((index & bit) != 0).astype(jnp.int32)
        keep = lax.dynamic_index_in_dim(pairs, high, 1, keepdims=False)
        send = lax.dynamic_index_in_dim(pairs, 1 - high, 1, keepdims=False)
        got = swap(send, axis, bit)
        kind = last if (last is not None and bit == bits[-1]) else blocks.dtype
        blocks = (keep.astype(F32) + got.astype(F32)).astype(kind)
    return blocks[0]


def tensor_sum(halves):
    core = lax.axis_index("tensor") & 1
    mine = lax.dynamic_index_in_dim(halves, core, 0, keepdims=False)
    other = lax.dynamic_index_in_dim(halves, 1 - core, 0, keepdims=False)

    def add(left, right):
        return (left.astype(F32) + right.astype(F32)).astype(left.dtype)

    mine = add(mine, swap(other, "tensor", 1))
    mine = add(mine, swap(mine, "tensor", 2))
    other = swap(mine, "tensor", 1)
    high = core == 1
    return jnp.stack([jnp.where(high, other, mine), jnp.where(high, mine, other)])


def sum_rows(rows):
    half = rows.shape[0] // 2
    return tensor_sum(rows.reshape((2, half) + rows.shape[1:])).reshape(rows.shape)


def neighbours(values_first, values_last):
    size = lax.axis_size("tensor")
    before = lax.ppermute(values_last, "tensor", [(i, i + 1) for i in range(size - 1)])
    after = lax.ppermute(values_first, "tensor", [(i + 1, i) for i in range(size - 1)])
    return before, after


def resident(shape):
    return pl.BlockSpec(shape, lambda *_: (0,) * len(shape))


def call(body, grid, in_specs, outs, flops, *args, scratch=()):
    nbytes = sum(a.size * a.dtype.itemsize for a in args)
    nbytes += sum(int(np.prod(shape)) * jnp.dtype(dtype).itemsize for shape, dtype, _ in outs)
    return pl.pallas_call(
        body,
        grid=grid,
        in_specs=in_specs,
        out_specs=[spec for _, _, spec in outs],
        out_shape=[jax.ShapeDtypeStruct(shape, dtype) for shape, dtype, _ in outs],
        scratch_shapes=scratch,
        compiler_params=pltpu.CompilerParams(vmem_limit_bytes=48 << 20),
        cost_estimate=pl.CostEstimate(flops=flops, bytes_accessed=nbytes, transcendentals=0),
    )(*args)


def gelu_parts(v):
    root = 0.7978845608028654
    th = jnp.tanh(root * (v + 0.044715 * v * v * v))
    value = 0.5 * v * (1.0 + th)
    slope = 0.5 * (1.0 + th) + 0.5 * v * (1.0 - th * th) * root * (1.0 + 3 * 0.044715 * v * v)
    return value, slope


def lane_masks(width):
    lane = lax.broadcasted_iota(jnp.int32, (1, width), 1) // HEAD
    return [(lane == h).astype(F32) for h in range(width // HEAD)]


def stack_heads(values, masks):
    return jnp.concatenate([values * m.astype(values.dtype) for m in masks], axis=0)


def join_heads(values, masks):
    size = values.shape[0] // len(masks)
    return sum(values[h * size : (h + 1) * size] * m for h, m in enumerate(masks))


def band(i, where_ref):
    start, length = where_ref[0], where_ref[1]
    shape = (2 * WINDOW, 3 * WINDOW)
    q_off = lax.broadcasted_iota(jnp.int32, shape, 0) % WINDOW
    k_off = lax.broadcasted_iota(jnp.int32, shape, 1)
    q_pos = start + i * WINDOW + q_off
    k_pos = start + (i - 1) * WINDOW + k_off
    ahead = k_off - q_off
    near = (ahead >= 1) & (ahead <= 2 * WINDOW - 1)
    inside = (k_pos >= 0) & (k_pos < SLOT)
    return near & inside & ((k_pos < length) | (q_pos >= length))


def local_forward_body(where_ref, a1_ref, w_ref, wout_ref, qkv_ref, lo_ref, lse_ref, attn_ref):
    t = pl.program_id(0)
    qkv_ref[...] = nn(a1_ref[...], w_ref[0]).astype(BF16)
    masks = lane_masks(2 * HEAD)

    @pl.loop(0, lo_ref.shape[0] // WINDOW)
    def _(i):
        base = pl.multiple_of(i * WINDOW, WINDOW)
        q = qkv_ref[pl.ds(base + WINDOW, WINDOW), 0:128]
        k = qkv_ref[pl.ds(base, 3 * WINDOW), 128:256]
        v = qkv_ref[pl.ds(base, 3 * WINDOW), 256:384]
        s = nt(stack_heads(q, masks), k) * SCALE
        s = jnp.where(band(i, where_ref), s, MASKED)
        top = jnp.max(s, axis=-1, keepdims=True)
        e = jnp.exp(s - top)
        total = jnp.sum(e, axis=-1, keepdims=True)
        o = nn((e / total).astype(BF16), v)
        lo_ref[pl.ds(base, WINDOW), :] = join_heads(o, masks).astype(BF16)
        lse_ref[pl.ds(base, WINDOW), :] = join_heads(top + jnp.log(total), masks)

    part = nt(lo_ref[...], wout_ref[0])

    @pl.when(t == 0)
    def _():
        attn_ref[...] = part

    @pl.when(t != 0)
    def _():
        attn_ref[...] += part


def local_backward_body(
    where_ref, g_ref, a1_ref, qkv_ref, lo_ref, lse_ref, w_ref, wout_ref, da1_ref, grad_ref, dq_ref, dkv_ref, dlo_ref
):
    t = pl.program_id(0)
    rows = g_ref.shape[0]
    masks = lane_masks(2 * HEAD)
    dlo_ref[...] = nn(g_ref[...], wout_ref[0]).astype(BF16)
    dkv_ref[...] = jnp.zeros_like(dkv_ref)

    @pl.loop(0, rows // WINDOW)
    def _(i):
        base = pl.multiple_of(i * WINDOW, WINDOW)
        q = stack_heads(qkv_ref[pl.ds(base + WINDOW, WINDOW), 0:128], masks)
        k = qkv_ref[pl.ds(base, 3 * WINDOW), 128:256]
        v = qkv_ref[pl.ds(base, 3 * WINDOW), 256:384]
        g = stack_heads(dlo_ref[pl.ds(base, WINDOW), :], masks)
        lse = lse_ref[pl.ds(base, WINDOW), :]
        lse = jnp.concatenate([lse[:, 0:1], lse[:, HEAD : HEAD + 1]], axis=0)
        s = jnp.where(band(i, where_ref), nt(q, k) * SCALE, MASKED)
        p = jnp.exp(s - lse)
        dp = nt(g, v)
        ds = (p * (dp - jnp.sum(p * dp, axis=-1, keepdims=True))).astype(BF16)
        dq_ref[pl.ds(base, WINDOW), :] = (join_heads(nn(ds, k), masks) * SCALE).astype(BF16)
        dkv_ref[pl.ds(base, 3 * WINDOW), 0:128] += tn(ds, q) * SCALE
        dkv_ref[pl.ds(base, 3 * WINDOW), 128:256] += tn(p.astype(BF16), g)

    dq = dq_ref[...]
    dkv = dkv_ref[...].astype(BF16)
    part = nt(dkv, w_ref[0, :, 128:384])
    part_q = nt(dq, w_ref[0, :, 0:128])

    @pl.when(t == 0)
    def _():
        da1_ref[...] = part

    @pl.when(t != 0)
    def _():
        da1_ref[...] += part

    da1_ref[WINDOW : WINDOW + rows, :] += part_q
    grad_ref[0, :, 0:128] = tn(a1_ref[WINDOW : WINDOW + rows, :], dq).astype(BF16)
    grad_ref[0, :, 128:384] = tn(a1_ref[...], dkv).astype(BF16)
    grad_ref[0, :, 384:512] = tn(g_ref[...], lo_ref[...]).astype(BF16)


def light_feed_body(a2_ref, g_ref, win_ref, wdown_ref, feed_ref, da2_ref, grad_ref):
    t = pl.program_id(0)
    hidden = wdown_ref.shape[2]
    gu = nn(a2_ref[...], win_ref[0])
    up = gu[:, hidden:]
    value, slope = gelu_parts(gu[:, :hidden])
    lh = (value * up).astype(BF16)
    dlh = nn(g_ref[...], wdown_ref[0]).astype(BF16).astype(F32)
    dgu = jnp.concatenate([dlh * up * slope, dlh * value], axis=1).astype(BF16)
    feed = nt(lh, wdown_ref[0])
    da2 = nt(dgu, win_ref[0])

    @pl.when(t == 0)
    def _():
        feed_ref[...] = feed
        da2_ref[...] = da2

    @pl.when(t != 0)
    def _():
        feed_ref[...] += feed
        da2_ref[...] += da2

    grad_ref[0, :, : 2 * hidden] = tn(a2_ref[...], dgu).astype(BF16)
    grad_ref[0, :, 2 * hidden :] = tn(g_ref[...], lh).astype(BF16)


def heavy_feed_body(
    f_ref, g_ref, router_ref, wgate_ref, wup_ref, wdown_ref,
    back_ref, daf_ref, drouter_ref, ggate_ref, gup_ref, gdown_ref, hf_acc, daf_acc
):
    j = pl.program_id(0)
    f = f_ref[...]
    f32 = f.astype(F32)
    sf = jax.nn.sigmoid(jnp.sum(f32 * router_ref[2:3, :], axis=-1, keepdims=True))
    g32 = g_ref[...].astype(F32)
    tf = (sf * g32).astype(BF16)
    up = nn(f, wup_ref[...])
    value, slope = gelu_parts(nn(f, wgate_ref[...]))
    hh = (value * up).astype(BF16)
    dhh = nn(tf, wdown_ref[...]).astype(BF16).astype(F32)
    dgate = (dhh * up * slope).astype(BF16)
    dup = (dhh * value).astype(BF16)
    hf = nt(hh, wdown_ref[...])
    daf = nt(dgate, wgate_ref[...]) + nt(dup, wup_ref[...])

    @pl.when(j == 0)
    def _():
        hf_acc[...] = hf
        daf_acc[...] = daf

    @pl.when(j != 0)
    def _():
        hf_acc[...] += hf
        daf_acc[...] += daf

    ggate_ref[...] = tn(f, dgate).astype(BF16)
    gup_ref[...] = tn(f, dup).astype(BF16)
    gdown_ref[...] = tn(tf, hh).astype(BF16)

    @pl.when(j == pl.num_programs(0) - 1)
    def _():
        whole = hf_acc[...]
        back_ref[...] = (sf * whole).astype(BF16)
        wf = jnp.sum(g32 * whole, axis=-1, keepdims=True) * sf * (1.0 - sf)
        daf_ref[...] = (daf_acc[...] + wf * router_ref[2:3, :]).astype(BF16)
        drouter_ref[...] = jnp.sum(wf * f32, axis=0, keepdims=True)


def heavy_forward_body(
    rows_ref, router_ref, w_ref, wout_ref, hqkv_ref, ho_ref, lse_ref, hy_ref, routed_ref, kvin_ref
):
    width = wout_ref.shape[1]
    masks = lane_masks(width)
    q_rows = rows_ref[0]
    q32, k32 = q_rows.astype(F32), rows_ref[1].astype(F32)
    sq = jax.nn.sigmoid(jnp.sum(q32 * router_ref[0:1, :], axis=-1, keepdims=True))
    sk = jax.nn.sigmoid(jnp.sum(k32 * router_ref[1:2, :], axis=-1, keepdims=True))
    kvin = (sk * k32).astype(BF16)
    kvin_ref[...] = kvin
    hq = nn(q_rows, w_ref[:, 0:width]).astype(BF16)
    hk = nn(kvin, w_ref[:, width : 2 * width]).astype(BF16)
    hv = nn(kvin, w_ref[:, 2 * width : 3 * width]).astype(BF16)
    hqkv_ref[0] = hq
    hqkv_ref[1] = hk
    hqkv_ref[2] = hv
    s = nt(stack_heads(hq, masks), hk) * SCALE
    top = jnp.max(s, axis=-1, keepdims=True)
    e = jnp.exp(s - top)
    total = jnp.sum(e, axis=-1, keepdims=True)
    ho = join_heads(nn((e / total).astype(BF16), hv), masks).astype(BF16)
    ho_ref[...] = ho
    lse_ref[...] = join_heads(top + jnp.log(total), masks)
    hy = nt(ho, wout_ref[...])
    hy_ref[...] = hy
    routed_ref[...] = (sq * hy).astype(BF16)


def heavy_backward_body(
    ga_ref, hy_ref, rows_ref, kvin_ref, router_ref, hqkv_ref, ho_ref, lse_ref, w_ref, wout_ref,
    drows_ref, grad_ref, drouter_ref
):
    width = wout_ref.shape[1]
    masks = lane_masks(width)
    q_rows = rows_ref[0]
    q32, k32 = q_rows.astype(F32), rows_ref[1].astype(F32)
    sq = jax.nn.sigmoid(jnp.sum(q32 * router_ref[0:1, :], axis=-1, keepdims=True))
    sk = jax.nn.sigmoid(jnp.sum(k32 * router_ref[1:2, :], axis=-1, keepdims=True))
    kvin = kvin_ref[...]
    ga = ga_ref[...].astype(F32)
    dsq = jnp.sum(ga * hy_ref[...], axis=-1, keepdims=True)
    tq = (sq * ga).astype(BF16)
    dho = nn(tq, wout_ref[...]).astype(BF16)
    q3 = stack_heads(hqkv_ref[0], masks)
    hk, hv = hqkv_ref[1], hqkv_ref[2]
    g3 = stack_heads(dho, masks)
    lse = lse_ref[...]
    lse3 = jnp.concatenate([lse[:, h * HEAD : h * HEAD + 1] for h in range(len(masks))], axis=0)
    p = jnp.exp(nt(q3, hk) * SCALE - lse3)
    dp = nt(g3, hv)
    ds = (p * (dp - jnp.sum(p * dp, axis=-1, keepdims=True))).astype(BF16)
    dhq = (join_heads(nn(ds, hk), masks) * SCALE).astype(BF16)
    dhk = (tn(ds, q3) * SCALE).astype(BF16)
    dhv = tn(p.astype(BF16), g3).astype(BF16)
    dkv = nt(dhk, w_ref[:, width : 2 * width]) + nt(dhv, w_ref[:, 2 * width : 3 * width])
    wq = dsq * sq * (1.0 - sq)
    wk = jnp.sum(dkv * k32, axis=-1, keepdims=True) * sk * (1.0 - sk)
    drows_ref[0] = (nt(dhq, w_ref[:, 0:width]) + wq * router_ref[0:1, :]).astype(BF16)
    drows_ref[1] = (sk * dkv + wk * router_ref[1:2, :]).astype(BF16)
    drouter_ref[0:1, :] = jnp.sum(wq * q32, axis=0, keepdims=True)
    drouter_ref[1:2, :] = jnp.sum(wk * k32, axis=0, keepdims=True)
    grad_ref[:, 0:width] = tn(q_rows, dhq).astype(BF16)
    grad_ref[:, width : 2 * width] = tn(kvin, dhk).astype(BF16)
    grad_ref[:, 2 * width : 3 * width] = tn(kvin, dhv).astype(BF16)
    grad_ref[:, 3 * width :] = tn(tq, ho_ref[...]).astype(BF16)


def local(
    inputs, cotangent, lengths, query_index, key_index, token_index,
    light_qkv, light_out, heavy_qkv, heavy_out, light_in, light_down, heavy_in, heavy_down,
    norm_gains, routers,
):
    rows, width = inputs.shape[1], inputs.shape[2]
    shard = light_qkv.shape[1]
    dp = lax.axis_size("dp")
    tensor = lax.axis_size("tensor")
    length = lengths[0]
    start = lax.axis_index("tensor") * rows
    own_pos = start + jnp.arange(rows, dtype=jnp.int32)
    valid = (own_pos < length).astype(F32)[:, None]

    def one_hot(index):
        return (index[:, None] == own_pos[None, :]).astype(BF16)

    hot_q, hot_k, hot_f = one_hot(query_index[0]), one_hot(key_index[0]), one_hot(token_index[0])

    small = jnp.concatenate([norm_gains, routers], axis=0)
    small = gather(gather(small, "tensor"), "dp")
    small = small.transpose(2, 0, 1, 3).reshape(5, width).astype(F32)
    gains, router = small[:2], small[2:]

    def flat(w):
        return w.transpose(1, 0, 2).reshape(shard, -1)

    def dp_gather(parts):
        packed = jnp.concatenate(parts, axis=1)
        return gather(packed, "dp").reshape(dp * shard, -1)

    c_lqkv, c_hqkv = 3 * light_qkv.shape[2], heavy_qkv.shape[2]
    c_lout, c_hout = light_out.shape[0], heavy_out.shape[0]
    c_lin, c_ldown = light_in.shape[2], light_down.shape[0]
    c_hin = heavy_in.shape[2]
    w1 = dp_gather([flat(light_qkv), flat(heavy_qkv)])
    w_lqkv = gather(w1[:, :c_lqkv], "tensor")
    w_hqkv = w1[:, c_lqkv:]
    w2 = dp_gather([light_out.T, flat(light_in), light_down.T, heavy_out.T])
    w_light = gather(w2[:, : c_lout + 2 * c_lin + c_ldown], "tensor")
    w_hout = w2[:, c_lout + 2 * c_lin + c_ldown :]
    w_hin = dp_gather([flat(heavy_in)])
    w_hdown = dp_gather([heavy_down.T])
    w_lout = w_light[:, :, :c_lout]
    w_lin = w_light[:, :, c_lout : c_lout + 2 * c_lin]
    w_ldown = w_light[:, :, c_lout + 2 * c_lin :]

    own = inputs[0]
    before, after = neighbours(own[:WINDOW], own[rows - WINDOW :])
    x = own.astype(F32)
    wide = jnp.concatenate([before, own, after], axis=0).astype(F32)
    a1_wide = rms_norm(wide, gains[0]).astype(BF16)
    a1 = a1_wide[WINDOW : WINDOW + rows]
    picked = jnp.stack([nn(hot_q, a1), nn(hot_k, a1)]).astype(BF16)
    picked = tensor_sum(picked)
    spots = jnp.stack([start, length]).astype(jnp.int32)
    smem = pl.BlockSpec(memory_space=pltpu.SMEM)
    whole = pl.BlockSpec(memory_space=pltpu.VMEM)

    def full(*shape_dtypes):
        return [(shape, dtype, whole) for shape, dtype in shape_dtypes]

    hw = heavy_out.shape[0]
    hqkv, ho, hlse, hy, routed, kvin = call(
        heavy_forward_body, (), [whole] * 4,
        full(
            ((3, ROUTED, hw), BF16), ((ROUTED, hw), BF16), ((ROUTED, hw), F32),
            ((ROUTED, width), F32), ((ROUTED, width), BF16), ((ROUTED, width), BF16),
        ),
        2 * ROUTED * width * hw * 4 + 4 * ROUTED * ROUTED * hw * 3,
        picked, router, w_hqkv, w_hout,
    )
    routed = sum_rows(routed)

    extent = rows + 2 * WINDOW
    qkv, lo, lse, attn = call(
        local_forward_body, (tensor,),
        [
            smem, resident((extent, width)),
            pl.BlockSpec((1, width, c_lqkv), lambda t: (t, 0, 0)),
            pl.BlockSpec((1, width, c_lout), lambda t: (t, 0, 0)),
        ],
        [
            ((extent, tensor * c_lqkv), BF16, pl.BlockSpec((extent, c_lqkv), lambda t: (0, t))),
            ((rows, tensor * c_lout), BF16, pl.BlockSpec((rows, c_lout), lambda t: (0, t))),
            ((rows, tensor * c_lout), F32, pl.BlockSpec((rows, c_lout), lambda t: (0, t))),
            ((rows, width), F32, resident((rows, width))),
        ],
        2 * extent * width * c_lqkv * tensor + 2 * rows * width * c_lout * tensor + 8 * rows * 384 * 128 * tensor,
        spots, a1_wide, w_lqkv, w_lout,
    )
    attn = attn + tn(hot_q, routed)
    mid = x + valid * attn

    a2 = rms_norm(mid, gains[1]).astype(BF16)
    gfeed = (valid * cotangent[0].astype(F32)).astype(BF16)
    f_rows = sum_rows(nn(hot_f, a2).astype(BF16))
    gf = sum_rows(nn(hot_f, gfeed).astype(BF16))
    feed, da2, g_lff = call(
        light_feed_body, (tensor,),
        [
            resident((rows, width)), resident((rows, width)),
            pl.BlockSpec((1, width, 2 * c_lin), lambda t: (t, 0, 0)),
            pl.BlockSpec((1, width, c_ldown), lambda t: (t, 0, 0)),
        ],
        [
            ((rows, width), F32, resident((rows, width))),
            ((rows, width), F32, resident((rows, width))),
            ((tensor, width, 3 * c_lin), BF16, pl.BlockSpec((1, width, 3 * c_lin), lambda t: (t, 0, 0))),
        ],
        2 * rows * width * c_lin * 9 * tensor,
        a2, gfeed, w_lin, w_ldown,
    )
    step = min(c_hin, 256)
    steps = c_hin // step
    col = pl.BlockSpec((width, step), lambda j: (0, j))
    next_col = pl.BlockSpec((width, step), lambda j: (0, j + steps))
    fixed = resident((ROUTED, width))
    back, daf, grad_router_f, g_hgate, g_hup, g_hdown = call(
        heavy_feed_body, (steps,),
        [fixed, fixed, resident((3, width)), col, next_col, col],
        [
            ((ROUTED, width), BF16, fixed), ((ROUTED, width), BF16, fixed), ((1, width), F32, resident((1, width))),
            ((width, c_hin), BF16, col), ((width, c_hin), BF16, col), ((width, c_hin), BF16, col),
        ],
        2 * ROUTED * width * c_hin * 9,
        f_rows, gf, router, w_hin, w_hin, w_hdown,
        scratch=[pltpu.VMEM((ROUTED, width), F32)] * 2,
    )
    output = mid + valid * (feed + tn(hot_f, sum_rows(back)))
    da2 = da2 + tn(hot_f, sum_rows(daf))
    g_hff = jnp.concatenate([g_hgate, g_hup, g_hdown], axis=1)
    g_hff = scatter(g_hff.reshape(dp, shard, -1), "dp", F32)
    g_lff = scatter(g_lff, "tensor")
    g_lff = scatter(g_lff.reshape(dp, shard, -1), "dp", F32)

    _, pull_norm2 = jax.vjp(rms_norm, mid, gains[1])
    dmid_norm, grad_gain2 = pull_norm2(da2)
    dmid = gfeed.astype(F32) + dmid_norm
    gattn = (valid * dmid).astype(BF16)

    ga = sum_rows(nn(hot_q, gattn).astype(BF16))
    routed_grads, g_hattn, grad_router_qk = call(
        heavy_backward_body, (), [whole] * 10,
        full(((2, ROUTED, width), BF16), ((width, 4 * hw), BF16), ((2, width), F32)),
        2 * ROUTED * width * hw * 8 + 10 * ROUTED * ROUTED * hw * 3,
        ga, hy, picked, kvin, router, hqkv, ho, hlse, w_hqkv, w_hout,
    )
    routed_grads = tensor_sum(routed_grads)
    g_hattn = scatter(g_hattn.reshape(dp, shard, -1), "dp", F32)

    da1_wide, g_lattn = call(
        local_backward_body, (tensor,),
        [
            smem, resident((rows, width)), resident((extent, width)),
            pl.BlockSpec((extent, c_lqkv), lambda t: (0, t)),
            pl.BlockSpec((rows, c_lout), lambda t: (0, t)),
            pl.BlockSpec((rows, c_lout), lambda t: (0, t)),
            pl.BlockSpec((1, width, c_lqkv), lambda t: (t, 0, 0)),
            pl.BlockSpec((1, width, c_lout), lambda t: (t, 0, 0)),
        ],
        [
            ((extent, width), F32, resident((extent, width))),
            ((tensor, width, c_lqkv + c_lout), BF16, pl.BlockSpec((1, width, c_lqkv + c_lout), lambda t: (t, 0, 0))),
        ],
        4 * extent * width * (c_lqkv + c_lout) * tensor + 20 * rows * 384 * 128 * tensor,
        spots, gattn, a1_wide, qkv, lo, lse, w_lqkv, w_lout,
        scratch=[pltpu.VMEM((rows, 128), BF16), pltpu.VMEM((extent, 256), F32), pltpu.VMEM((rows, 128), BF16)],
    )
    from_before, from_after = neighbours(
        da1_wide[:WINDOW].astype(BF16), da1_wide[rows + WINDOW :].astype(BF16)
    )
    da1 = da1_wide[WINDOW : WINDOW + rows]
    da1 = jnp.concatenate(
        [
            da1[:WINDOW] + from_before.astype(F32),
            da1[WINDOW : rows - WINDOW],
            da1[rows - WINDOW :] + from_after.astype(F32),
        ],
        axis=0,
    )
    g_lattn = scatter(g_lattn, "tensor")
    g_lattn = scatter(g_lattn.reshape(dp, shard, -1), "dp", F32)
    da1 = da1 + tn(hot_q, routed_grads[0]) + tn(hot_k, routed_grads[1])
    _, pull_norm1 = jax.vjp(rms_norm, x, gains[0])
    dx_norm, grad_gain1 = pull_norm1(da1)
    input_grad = dmid + dx_norm

    small_grads = jnp.concatenate([grad_gain1[None], grad_gain2[None], grad_router_qk, grad_router_f], axis=0)
    small_grads = small_grads.reshape(5, dp, tensor, -1).transpose(1, 2, 0, 3)
    small_grads = scatter(scatter(small_grads, "dp"), "tensor")

    def unflat(grad, count):
        return grad.reshape(shard, count, -1).transpose(1, 0, 2)

    return (
        output[None].astype(BF16),
        input_grad[None],
        unflat(g_lattn[:, :c_lqkv], 3),
        g_lattn[:, c_lqkv:].T,
        unflat(g_hattn[:, : 3 * c_hqkv], 3),
        g_hattn[:, 3 * c_hqkv :].T,
        unflat(g_lff[:, : 2 * c_lin], 2),
        g_lff[:, 2 * c_lin :].T,
        unflat(g_hff[:, : 2 * c_hin], 2),
        g_hff[:, 2 * c_hin :].T,
        small_grads[:2],
        small_grads[2:],
    )


def solution(mesh):
    rows = P("dp", "tensor", None)
    index = P("dp", None)
    cols = P(None, "dp", "tensor")
    back = P("tensor", "dp")
    both = P(None, ("dp", "tensor"))
    weights = (cols, back) * 4
    return jax.shard_map(
        local,
        mesh=mesh,
        in_specs=(rows, rows, P("dp"), index, index, index) + weights + (both, both),
        out_specs=(rows, rows) + weights + (both, both),
        check_vma=False,
    )
```

```python
import functools

import jax
import jax.numpy as jnp
import numpy as np
from jax import lax
from jax.experimental import pallas as pl
from jax.experimental.pallas import tpu as pltpu
from jax.sharding import PartitionSpec as P

HEAD = 64
SLOT = 2048
WINDOW = 128
ROUTED = 256
NORM_EPS = 1e-06
SCALE = 0.125
MASKED = -1e30
F32 = jnp.float32
BF16 = jnp.bfloat16


def mm(left, right, dims):
    return lax.dot_general(left, right, (dims, ((), ())), preferred_element_type=F32)


def nn(left, right):
    return mm(left, right, ((1,), (0,)))


def nt(left, right):
    return mm(left, right, ((1,), (1,)))


def tn(left, right):
    return mm(left, right, ((0,), (0,)))


def low(values):
    return values.astype(BF16)


def swap(values, axis, bit):
    size = lax.axis_size(axis)
    return lax.ppermute(values, axis, [(i, i ^ bit) for i in range(size)])


def bits_of(axis):
    size = lax.axis_size(axis)
    return [1 << b for b in range(size.bit_length() - 1)]


def relative_order(axis):
    order = [0]
    for bit in reversed(bits_of(axis)):
        order = order + [r ^ bit for r in order]
    return order


def after(values, *others):
    return lax.optimization_barrier((values,) + others)[0]


def gather_halves(block, axis):
    have = block
    bits = list(reversed(bits_of(axis)))
    for bit in bits[:-1]:
        have = jnp.concatenate([have, swap(have, axis, bit)], axis=0)
    return have, swap(have, axis, bits[-1])


def add(left, right, kind=BF16):
    return (left.astype(F32) + right.astype(F32)).astype(kind)


def reduce_halves(keep, send, axis, kind=F32):
    bits = bits_of(axis)
    for bit in bits:
        got = swap(send, axis, bit)
        if bit == bits[-1]:
            return add(keep, got, kind)
        half = keep.shape[0] // 2
        send = add(keep[half:], got[half:], keep.dtype)
        keep = add(keep[:half], got[:half], keep.dtype)


def tensor_sum(mine, other):
    mine = add(mine, swap(other, "tensor", 1))
    mine = add(mine, swap(mine, "tensor", 2))
    return mine, swap(mine, "tensor", 1)


def neighbours(first, last):
    size = lax.axis_size("tensor")
    before = lax.ppermute(last, "tensor", [(i, i + 1) for i in range(size - 1)])
    behind = lax.ppermute(first, "tensor", [(i + 1, i) for i in range(size - 1)])
    return before, behind


VMEM = pl.BlockSpec(memory_space=pltpu.VMEM)
SMEM = pl.BlockSpec(memory_space=pltpu.SMEM)


def call(body, flops, args, outs, grid=(), in_specs=None, out_specs=None, scratch=()):
    nbytes = sum(a.size * a.dtype.itemsize for a in args)
    nbytes += sum(int(np.prod(shape)) * jnp.dtype(dtype).itemsize for shape, dtype in outs)
    return pl.pallas_call(
        body,
        grid=grid,
        in_specs=in_specs or [SMEM if a.ndim == 1 else VMEM for a in args],
        out_specs=out_specs or [VMEM] * len(outs),
        out_shape=[jax.ShapeDtypeStruct(shape, dtype) for shape, dtype in outs],
        scratch_shapes=scratch,
        compiler_params=pltpu.CompilerParams(vmem_limit_bytes=48 << 20),
        cost_estimate=pl.CostEstimate(flops=int(flops), bytes_accessed=nbytes, transcendentals=0),
    )(*args)


def mul(x, first, second):
    half = first.shape[0]
    return nn(x[:, :half], first) + nn(x[:, half:], second)


def mul_t(y, first, second):
    return jnp.concatenate([nt(y, first), nt(y, second)], axis=1)


def sigmoid(v):
    return 1.0 / (1.0 + jnp.exp(-v))


def rms(v, gain):
    return v * lax.rsqrt(jnp.mean(v * v, axis=-1, keepdims=True) + NORM_EPS) * gain


def rms_back(v, gain, grad):
    r = lax.rsqrt(jnp.mean(v * v, axis=-1, keepdims=True) + NORM_EPS)
    n = v * r
    h = grad * gain
    return r * (h - n * jnp.mean(h * n, axis=-1, keepdims=True)), jnp.sum(grad * n, axis=0, keepdims=True)


def gelu_parts(v):
    root = 0.7978845608028654
    th = jnp.tanh(root * (v + 0.044715 * v * v * v))
    value = 0.5 * v * (1.0 + th)
    slope = 0.5 * (1.0 + th) + 0.5 * v * (1.0 - th * th) * root * (1.0 + 3 * 0.044715 * v * v)
    return value, slope


def iota(shape, axis):
    return lax.broadcasted_iota(jnp.int32, shape, axis)


def ones_where(mask):
    return low(jnp.where(mask, 1.0, 0.0))


def permutation(src_ref):
    size = src_ref.shape[1]
    return ones_where(iota((size, size), 0) == src_ref[...])


def valid_rows(where_ref, rows):
    return where_ref[0] + iota((rows, 1), 0) < where_ref[1]


def pick(cols_ref, which, where_ref, rows):
    index = cols_ref[:, which : which + 1]
    return ones_where(index == where_ref[0] + iota((index.shape[0], rows), 1))


def place(rows_ref, which, where_ref, rows):
    index = rows_ref[which : which + 1, :]
    return ones_where(index == where_ref[0] + iota((rows, index.shape[1]), 0))


def split(values, *refs):
    size = values.shape[0] // len(refs)
    for i, ref in enumerate(refs):
        ref[...] = values[i * size : (i + 1) * size].astype(ref.dtype)


def both(mine_ref, other_ref):
    return jnp.concatenate([mine_ref[...], other_ref[...]], axis=0)


def start_body(where_ref, src_ref, cols_ref, x_ref, cot_ref, xr_ref, g_ref, qm_ref, qo_ref, km_ref, ko_ref, fm_ref, fo_ref):
    rows = x_ref.shape[0]
    perm = permutation(src_ref)
    xr = low(nn(x_ref[...], perm))
    xr_ref[...] = xr
    g = low(jnp.where(valid_rows(where_ref, rows), nn(cot_ref[...], perm), 0.0))
    g_ref[...] = g
    split(nn(pick(cols_ref, 0, where_ref, rows), xr), qm_ref, qo_ref)
    split(nn(pick(cols_ref, 1, where_ref, rows), xr), km_ref, ko_ref)
    split(nn(pick(cols_ref, 2, where_ref, rows), g), fm_ref, fo_ref)


def norm_body(src_ref, gains_ref, before_ref, x_ref, after_ref, a1_ref):
    edge, rows = before_ref.shape[0], x_ref.shape[0]
    perm = permutation(src_ref)
    gain = gains_ref[0:1, :]
    a1_ref[0:edge, :] = low(rms(nn(before_ref[...], perm), gain))
    a1_ref[edge : edge + rows, :] = low(rms(x_ref[...].astype(F32), gain))
    a1_ref[edge + rows :, :] = low(rms(nn(after_ref[...], perm), gain))


def lane_masks(width):
    lane = iota((1, width), 1) // HEAD
    return [(lane == h).astype(F32) for h in range(width // HEAD)]


def stack_heads(values, masks):
    return jnp.concatenate([values * m.astype(values.dtype) for m in masks], axis=0)


def join_heads(values, masks):
    size = values.shape[0] // len(masks)
    return sum(values[h * size : (h + 1) * size] * m for h, m in enumerate(masks))


def band(i, where_ref):
    start, length = where_ref[0], where_ref[1]
    shape = (2 * WINDOW, 3 * WINDOW)
    q_off = iota(shape, 0) % WINDOW
    k_off = iota(shape, 1)
    q_pos = start + i * WINDOW + q_off
    k_pos = start + (i - 1) * WINDOW + k_off
    ahead = k_off - q_off
    near = (ahead >= 1) & (ahead <= 2 * WINDOW - 1)
    inside = (k_pos >= 0) & (k_pos < SLOT)
    return near & inside & ((k_pos < length) | (q_pos >= length))


def local_forward_body(where_ref, a1_ref, c_ref, d_ref, qkv_ref, lo_ref, lse_ref):
    qkv_ref[...] = low(mul(a1_ref[...], c_ref[...], d_ref[...]))
    masks = lane_masks(2 * HEAD)

    @pl.loop(0, lo_ref.shape[0] // WINDOW)
    def _(i):
        base = pl.multiple_of(i * WINDOW, WINDOW)
        q = qkv_ref[pl.ds(base + WINDOW, WINDOW), 0:128]
        k = qkv_ref[pl.ds(base, 3 * WINDOW), 128:256]
        v = qkv_ref[pl.ds(base, 3 * WINDOW), 256:384]
        s = nt(stack_heads(q, masks), k) * SCALE
        s = jnp.where(band(i, where_ref), s, MASKED)
        top = jnp.max(s, axis=-1, keepdims=True)
        e = jnp.exp(s - top)
        total = jnp.sum(e, axis=-1, keepdims=True)
        o = nn(low(e / total), v)
        lo_ref[pl.ds(base, WINDOW), :] = low(join_heads(o, masks))
        lse_ref[pl.ds(base, WINDOW), :] = join_heads(top + jnp.log(total), masks)


def local_backward_body(count, where_ref, g_ref, a1_ref, *refs):
    per = 5
    ins = [refs[i * per : (i + 1) * per] for i in range(count)]
    outs = [refs[count * per + i * 3 : count * per + (i + 1) * 3] for i in range(count)]
    dkv_acc, dlo_ref = refs[count * (per + 3) :]
    rows = g_ref.shape[0]
    masks = lane_masks(2 * HEAD)
    for (qkv_ref, lo_ref, lse_ref, c_ref, d_ref), (dq_ref, dkv_ref, grad_ref) in zip(ins, outs):
        dlo_ref[...] = low(mul(g_ref[...], c_ref[...], d_ref[...]))
        dkv_acc[...] = jnp.zeros_like(dkv_acc)

        @pl.loop(0, rows // WINDOW)
        def _(i, qkv_ref=qkv_ref, lse_ref=lse_ref, dq_ref=dq_ref):
            base = pl.multiple_of(i * WINDOW, WINDOW)
            q = stack_heads(qkv_ref[pl.ds(base + WINDOW, WINDOW), 0:128], masks)
            k = qkv_ref[pl.ds(base, 3 * WINDOW), 128:256]
            v = qkv_ref[pl.ds(base, 3 * WINDOW), 256:384]
            g = stack_heads(dlo_ref[pl.ds(base, WINDOW), :], masks)
            lse = lse_ref[pl.ds(base, WINDOW), :]
            lse = jnp.concatenate([lse[:, 0:1], lse[:, HEAD : HEAD + 1]], axis=0)
            s = jnp.where(band(i, where_ref), nt(q, k) * SCALE, MASKED)
            p = jnp.exp(s - lse)
            dp = nt(g, v)
            ds = low(p * (dp - jnp.sum(p * dp, axis=-1, keepdims=True)))
            dq_ref[pl.ds(base, WINDOW), :] = low(join_heads(nn(ds, k), masks) * SCALE)
            dkv_acc[pl.ds(base, 3 * WINDOW), 0:128] += tn(ds, q) * SCALE
            dkv_acc[pl.ds(base, 3 * WINDOW), 128:256] += tn(low(p), g)

        dkv_ref[...] = low(dkv_acc[...])
        grad_ref[:, 0:128] = low(tn(a1_ref[WINDOW : WINDOW + rows, :], dq_ref[...]))
        grad_ref[:, 128:384] = low(tn(a1_ref[...], dkv_ref[...]))
        grad_ref[:, 384:512] = low(tn(g_ref[...], lo_ref[...]))


def local_input_body(count, *refs):
    ins = [refs[i * 4 : (i + 1) * 4] for i in range(count)]
    da1_ref, first_ref, last_ref = refs[count * 4 :]
    rows, edge = da1_ref.shape[0], first_ref.shape[0]
    half = ins[0][2].shape[0]
    dkv = jnp.concatenate([r[1][...] for r in ins], axis=1)
    dq = jnp.concatenate([r[0][...] for r in ins], axis=1)
    for side in range(2):
        cut = slice(side * half, (side + 1) * half)
        w_kv = jnp.concatenate([r[2 + side][:, 128:384] for r in ins], axis=1)
        w_q = jnp.concatenate([r[2 + side][:, 0:128] for r in ins], axis=1)
        part = nt(dkv, w_kv)
        first_ref[:, cut] = low(part[:edge])
        da1_ref[:, cut] = part[edge : edge + rows] + nt(dq, w_q)
        last_ref[:, cut] = low(part[edge + rows :])


def light_feed_body(first, *refs):
    if first:
        a2_ref, g_ref, *refs = refs
    else:
        a2_ref, g_ref, feed_in, da2_in, *refs = refs
    weights = [refs[0:2], refs[2:4]]
    feed_ref, da2_ref, *grads = refs[4:]
    hidden = weights[0][0].shape[1] // 3
    feed = da2 = None
    a2, g = a2_ref[...], g_ref[...]
    for (c_ref, d_ref), grad_ref in zip(weights, grads):
        cin, din = c_ref[:, : 2 * hidden], d_ref[:, : 2 * hidden]
        cdown, ddown = c_ref[:, 2 * hidden :], d_ref[:, 2 * hidden :]
        gu = mul(a2, cin, din)
        up = gu[:, hidden:]
        value, slope = gelu_parts(gu[:, :hidden])
        lh = low(value * up)
        dlh = low(mul(g, cdown, ddown)).astype(F32)
        dgu = jnp.concatenate([low(dlh * up * slope), low(dlh * value)], axis=1)
        new_feed = mul_t(lh, cdown, ddown)
        new_da2 = mul_t(dgu, cin, din)
        feed = new_feed if feed is None else feed + new_feed
        da2 = new_da2 if da2 is None else da2 + new_da2
        grad_ref[:, : 2 * hidden] = low(tn(a2, dgu))
        grad_ref[:, 2 * hidden :] = low(tn(g, lh))
    if first:
        feed_ref[...] = feed
        da2_ref[...] = da2
    else:
        feed_ref[...] = feed_in[...] + feed
        da2_ref[...] = da2_in[...] + da2


def heavy_feed_body(
    gains_ref, fm_ref, fo_ref, gm_ref, go_ref, cg_ref, dg_ref, cu_ref, du_ref, cd_ref, dd_ref,
    bm_ref, bo_ref, am_ref, ao_ref, drouter_ref, g0, g1, u0, u1, w0, w1, hf_acc, daf_acc
):
    j = pl.program_id(0)
    half = cg_ref.shape[0]
    f = both(fm_ref, fo_ref)
    f32 = f.astype(F32)
    router = gains_ref[4:5, :]
    sf = sigmoid(jnp.sum(f32 * router, axis=-1, keepdims=True))
    g32 = both(gm_ref, go_ref).astype(F32)
    tf = low(sf * g32)
    up = mul(f, cu_ref[...], du_ref[...])
    value, slope = gelu_parts(mul(f, cg_ref[...], dg_ref[...]))
    hh = low(value * up)
    dhh = low(mul(tf, cd_ref[...], dd_ref[...])).astype(F32)
    dgate = low(dhh * up * slope)
    dup = low(dhh * value)
    hf = mul_t(hh, cd_ref[...], dd_ref[...])
    daf = mul_t(dgate, cg_ref[...], dg_ref[...]) + mul_t(dup, cu_ref[...], du_ref[...])

    @pl.when(j == 0)
    def _():
        hf_acc[...] = hf
        daf_acc[...] = daf

    @pl.when(j != 0)
    def _():
        hf_acc[...] += hf
        daf_acc[...] += daf

    for x, dy, refs in ((f, dgate, (g0, g1)), (f, dup, (u0, u1)), (tf, hh, (w0, w1))):
        refs[0][...] = low(tn(x[:, :half], dy))
        refs[1][...] = low(tn(x[:, half:], dy))

    @pl.when(j == pl.num_programs(0) - 1)
    def _():
        whole = hf_acc[...]
        split(sf * whole, bm_ref, bo_ref)
        wf = jnp.sum(g32 * whole, axis=-1, keepdims=True) * sf * (1.0 - sf)
        split(daf_acc[...] + wf * router, am_ref, ao_ref)
        drouter_ref[...] = jnp.sum(wf * f32, axis=0, keepdims=True)


def scores(rows, router):
    return sigmoid(jnp.sum(rows.astype(F32) * router, axis=-1, keepdims=True))


def heavy_forward_body(
    gains_ref, qm_ref, qo_ref, km_ref, ko_ref, c_ref, d_ref,
    rows_ref, hqkv_ref, ho_ref, lse_ref, hy_ref, rm_ref, ro_ref
):
    width = c_ref.shape[1] // 4
    masks = lane_masks(width)
    gain = gains_ref[0:1, :]
    q_rows = low(rms(both(qm_ref, qo_ref).astype(F32), gain))
    k_rows = low(rms(both(km_ref, ko_ref).astype(F32), gain))
    sq = scores(q_rows, gains_ref[2:3, :])
    kvin = low(scores(k_rows, gains_ref[3:4, :]) * k_rows.astype(F32))
    rows_ref[0] = q_rows
    rows_ref[1] = k_rows
    rows_ref[2] = kvin
    hq = low(mul(q_rows, c_ref[:, 0:width], d_ref[:, 0:width]))
    hk = low(mul(kvin, c_ref[:, width : 2 * width], d_ref[:, width : 2 * width]))
    hv = low(mul(kvin, c_ref[:, 2 * width : 3 * width], d_ref[:, 2 * width : 3 * width]))
    hqkv_ref[0] = hq
    hqkv_ref[1] = hk
    hqkv_ref[2] = hv
    s = nt(stack_heads(hq, masks), hk) * SCALE
    top = jnp.max(s, axis=-1, keepdims=True)
    e = jnp.exp(s - top)
    total = jnp.sum(e, axis=-1, keepdims=True)
    ho = low(join_heads(nn(low(e / total), hv), masks))
    ho_ref[...] = ho
    lse_ref[...] = join_heads(top + jnp.log(total), masks)
    hy = mul_t(ho, c_ref[:, 3 * width :], d_ref[:, 3 * width :])
    hy_ref[...] = hy
    split(sq * hy, rm_ref, ro_ref)


def heavy_backward_body(
    gains_ref, gm_ref, go_ref, hy_ref, rows_ref, hqkv_ref, ho_ref, lse_ref, c_ref, d_ref,
    qm_ref, qo_ref, km_ref, ko_ref, keep_ref, send_ref, drouter_ref
):
    width, half = c_ref.shape[1] // 4, c_ref.shape[0]
    masks = lane_masks(width)
    q_rows, k_rows, kvin = rows_ref[0], rows_ref[1], rows_ref[2]
    q32, k32 = q_rows.astype(F32), k_rows.astype(F32)
    sq = scores(q_rows, gains_ref[2:3, :])
    sk = scores(k_rows, gains_ref[3:4, :])
    ga = both(gm_ref, go_ref).astype(F32)
    dsq = jnp.sum(ga * hy_ref[...], axis=-1, keepdims=True)
    tq = low(sq * ga)
    cuts = [slice(i * width, (i + 1) * width) for i in range(4)]
    dho = low(mul(tq, c_ref[:, cuts[3]], d_ref[:, cuts[3]]))
    q3 = stack_heads(hqkv_ref[0], masks)
    hk, hv = hqkv_ref[1], hqkv_ref[2]
    g3 = stack_heads(dho, masks)
    lse = lse_ref[...]
    lse3 = jnp.concatenate([lse[:, h * HEAD : h * HEAD + 1] for h in range(len(masks))], axis=0)
    p = jnp.exp(nt(q3, hk) * SCALE - lse3)
    dp = nt(g3, hv)
    ds = low(p * (dp - jnp.sum(p * dp, axis=-1, keepdims=True)))
    dhq = low(join_heads(nn(ds, hk), masks) * SCALE)
    dhk = low(tn(ds, q3) * SCALE)
    dhv = low(tn(low(p), g3))
    dkv = mul_t(dhk, c_ref[:, cuts[1]], d_ref[:, cuts[1]]) + mul_t(dhv, c_ref[:, cuts[2]], d_ref[:, cuts[2]])
    wq = dsq * sq * (1.0 - sq)
    wk = jnp.sum(dkv * k32, axis=-1, keepdims=True) * sk * (1.0 - sk)
    split(mul_t(dhq, c_ref[:, cuts[0]], d_ref[:, cuts[0]]) + wq * gains_ref[2:3, :], qm_ref, qo_ref)
    split(sk * dkv + wk * gains_ref[3:4, :], km_ref, ko_ref)
    drouter_ref[0:1, :] = jnp.sum(wq * q32, axis=0, keepdims=True)
    drouter_ref[1:2, :] = jnp.sum(wk * k32, axis=0, keepdims=True)
    for cut, x, dy in zip(cuts, (q_rows, kvin, kvin, tq), (dhq, dhk, dhv, ho_ref[...])):
        keep_ref[:, cut] = low(tn(x[:, :half], dy))
        send_ref[:, cut] = low(tn(x[:, half:], dy))


def middle_body(where_ref, gains_ref, cols_ref, rows_ref, x_ref, rm_ref, ro_ref, *refs):
    ins = [refs[i * 3 : (i + 1) * 3] for i in range(4)]
    mid_ref, a2_ref, fm_ref, fo_ref = refs[12:]
    rows = x_ref.shape[0]
    lo = jnp.concatenate([r[0][...] for r in ins], axis=1)
    c = jnp.concatenate([r[1][...] for r in ins], axis=1)
    d = jnp.concatenate([r[2][...] for r in ins], axis=1)
    attn = mul_t(lo, c, d) + nn(place(rows_ref, 0, where_ref, rows), both(rm_ref, ro_ref))
    mid = x_ref[...].astype(F32) + jnp.where(valid_rows(where_ref, rows), attn, 0.0)
    mid_ref[...] = mid
    a2 = low(rms(mid, gains_ref[1:2, :]))
    a2_ref[...] = a2
    split(nn(pick(cols_ref, 2, where_ref, rows), a2), fm_ref, fo_ref)


def output_body(where_ref, src_ref, rows_ref, mid_ref, feed_ref, bm_ref, bo_ref, out_ref):
    rows = mid_ref.shape[0]
    feed = feed_ref[...] + nn(place(rows_ref, 2, where_ref, rows), both(bm_ref, bo_ref))
    out = low(mid_ref[...] + jnp.where(valid_rows(where_ref, rows), feed, 0.0))
    out_ref[...] = low(nt(out, permutation(src_ref)))


def turn_body(
    where_ref, gains_ref, cols_ref, rows_ref, mid_ref, da2_ref, g_ref, am_ref, ao_ref,
    dmid_ref, gattn_ref, dgain_ref, gm_ref, go_ref
):
    rows = mid_ref.shape[0]
    da2 = da2_ref[...] + nn(place(rows_ref, 2, where_ref, rows), both(am_ref, ao_ref))
    back, dgain_ref[...] = rms_back(mid_ref[...], gains_ref[1:2, :], da2)
    dmid = g_ref[...].astype(F32) + back
    dmid_ref[...] = dmid
    gattn = low(jnp.where(valid_rows(where_ref, rows), dmid, 0.0))
    gattn_ref[...] = gattn
    split(nn(pick(cols_ref, 0, where_ref, rows), gattn), gm_ref, go_ref)


def finish_body(
    where_ref, src_ref, gains_ref, rows_ref, x_ref, dmid_ref, da1_ref, before_ref, after_ref,
    qm_ref, qo_ref, km_ref, ko_ref, grad_ref, dgain_ref
):
    rows, edge = x_ref.shape[0], before_ref.shape[0]
    da1 = da1_ref[...] + nn(place(rows_ref, 0, where_ref, rows), both(qm_ref, qo_ref))
    da1 = da1 + nn(place(rows_ref, 1, where_ref, rows), both(km_ref, ko_ref))
    da1 = jnp.concatenate(
        [
            da1[:edge] + before_ref[...].astype(F32),
            da1[edge : rows - edge],
            da1[rows - edge :] + after_ref[...].astype(F32),
        ],
        axis=0,
    )
    back, dgain_ref[...] = rms_back(x_ref[...].astype(F32), gains_ref[0:1, :], da1)
    grad = dmid_ref[...] + back
    perm = permutation(src_ref)
    one = low(grad)
    rest = grad - one.astype(F32)
    two = low(rest)
    three = low(rest - two.astype(F32))
    grad_ref[...] = nt(one, perm) + nt(two, perm) + nt(three, perm)


def local(
    inputs, cotangent, lengths, query_index, key_index, token_index,
    light_qkv, light_out, heavy_qkv, heavy_out, light_in, light_down, heavy_in, heavy_down,
    norm_gains, routers,
):
    rows, width = inputs.shape[1], inputs.shape[2]
    extent = rows + 2 * WINDOW
    shard, half = light_qkv.shape[1], width // 2
    dp, tensor = lax.axis_size("dp"), lax.axis_size("tensor")
    dp_index, tensor_index = lax.axis_index("dp"), lax.axis_index("tensor")
    c_lqkv, c_lout = 3 * light_qkv.shape[2], light_out.shape[0]
    c_lin, c_ldown, c_hin = light_in.shape[2], light_down.shape[0], heavy_in.shape[2]
    hw = heavy_out.shape[0]
    order = np.array(relative_order("dp"), np.int32)
    place_of = np.arange(width, dtype=np.int32)
    src = ((dp_index ^ order[place_of // shard]) * shard + place_of % shard)[None].astype(jnp.int32)
    where = jnp.stack([tensor_index * rows, lengths[0]]).astype(jnp.int32)
    index = jnp.concatenate([query_index, key_index, token_index], axis=0).reshape(3, 2, ROUTED // 2)
    index = jnp.where((tensor_index & 1) == 1, index[:, ::-1], index).reshape(3, ROUTED)
    index_cols = index.T

    small = jnp.concatenate([norm_gains, routers], axis=0)
    for bit in (2, 1):
        got = swap(small, "tensor", bit)
        high = (tensor_index & bit) != 0
        small = jnp.concatenate([jnp.where(high, got, small), jnp.where(high, small, got)], axis=0)
    small = small.reshape(2, 2, 5, -1).transpose(1, 0, 2, 3)[None]
    for bit in reversed(bits_of("dp")):
        small = jnp.concatenate([small, swap(small, "dp", bit)], axis=0)
    gains = small.transpose(3, 0, 1, 2, 4).reshape(5, width).astype(F32)

    own = inputs[0]
    before, behind = neighbours(own[:WINDOW], own[rows - WINDOW :])

    def flat(w):
        return w.transpose(1, 0, 2).reshape(shard, -1)

    def tensor_gather(pair):
        pairs = [pair, tuple(swap(w, "tensor", 2) for w in pair)]
        return pairs + [tuple(swap(w, "tensor", 1) for w in p) for p in pairs]

    w_lqkv = gather_halves(flat(light_qkv), "dp")
    piece = jnp.concatenate([flat(heavy_qkv), heavy_out.T], axis=1)
    w_heavy = gather_halves(after(piece, w_lqkv[0]), "dp")
    w_lqkv = tensor_gather(w_lqkv)
    w_lout = gather_halves(after(light_out.T, w_heavy[0]), "dp")
    w_lout = tensor_gather(w_lout)
    piece = jnp.concatenate([flat(light_in), light_down.T], axis=1)
    w_light = gather_halves(after(piece, w_heavy[0]), "dp")
    w_hin = gather_halves(after(flat(heavy_in), w_light[0]), "dp")
    w_hdown = gather_halves(after(heavy_down.T, w_hin[0]), "dp")
    w_light = tensor_gather(w_light)

    rowsb = ((ROUTED // 2, width), BF16)
    wide = ((rows, width), BF16)
    wide32 = ((rows, width), F32)
    x, gfeed, qm, qo, km, ko, fm, fo = call(
        start_body, 4 * rows * width * width, (where, src, index_cols, own, cotangent[0]), [wide, wide] + [rowsb] * 6
    )
    qm, qo = tensor_sum(qm, qo)
    km, ko = tensor_sum(km, ko)
    (a1,) = call(norm_body, rows * width * width, (src, gains, before, x, behind), [((extent, width), BF16)])
    routed, hqkv, ho, hlse, hy, rm, ro = call(
        heavy_forward_body, 2 * ROUTED * width * hw * 4 + 4 * ROUTED * ROUTED * hw * 3,
        (gains, qm, qo, km, ko) + w_heavy,
        [((3, ROUTED, width), BF16), ((3, ROUTED, hw), BF16), ((ROUTED, hw), BF16), ((ROUTED, hw), F32),
         ((ROUTED, width), F32), rowsb, rowsb],
    )
    rm, ro = tensor_sum(rm, ro)
    heads = [
        call(
            local_forward_body, 2 * extent * width * c_lqkv + 8 * rows * 384 * 128,
            (where, a1) + pair,
            [((extent, c_lqkv), BF16), ((rows, c_lout), BF16), ((rows, c_lout), F32)],
        )
        for pair in w_lqkv
    ]
    mid, a2, am, ao = call(
        middle_body, 2 * rows * width * (c_lout * tensor + 2 * ROUTED),
        (where, gains, index_cols, index, x, rm, ro) + sum(((h[1],) + w for h, w in zip(heads, w_lout)), ()),
        [wide32, wide, rowsb, rowsb],
    )

    am, ao = tensor_sum(am, ao)
    fm, fo = tensor_sum(fm, fo)

    def light_feed(done, pairs):
        weights = sum(pairs, ())
        return call(
            functools.partial(light_feed_body, not done), 2 * rows * width * c_lin * 9 * 2,
            (a2, gfeed) + done + weights,
            [wide32, wide32] + [((width, 3 * c_lin), BF16)] * 2,
        )

    feed, da2, g_l0, g_l1 = light_feed((), [w_light[0], w_light[2]])
    feed, da2, g_l2, g_l3 = light_feed((feed, da2), [w_light[1], w_light[3]])
    step = min(c_hin, 256)
    steps = c_hin // step
    col = pl.BlockSpec((half, step), lambda j: (0, j))
    next_col = pl.BlockSpec((half, step), lambda j: (0, j + steps))
    fixed = pl.BlockSpec((ROUTED // 2, width), lambda j: (0, 0))
    one_row = pl.BlockSpec((1, width), lambda j: (0, 0))
    bm, bo, dm, do, grad_router_f, *g_heavy = call(
        heavy_feed_body, 2 * ROUTED * width * c_hin * 9,
        (gains, am, ao, fm, fo) + w_hin + w_hin + w_hdown,
        [rowsb] * 4 + [((1, width), F32)] + [((half, c_hin), BF16)] * 6,
        grid=(steps,),
        in_specs=[pl.BlockSpec((5, width), lambda j: (0, 0))] + [fixed] * 4 + [col, col, next_col, next_col, col, col],
        out_specs=[fixed] * 4 + [one_row] + [col] * 6,
        scratch=[pltpu.VMEM((ROUTED, width), F32)] * 2,
    )
    dm, do = tensor_sum(dm, do)
    dmid, gattn, grad_gain2, gm, go = call(
        turn_body, 4 * rows * width * ROUTED,
        (where, gains, index_cols, index, mid, da2, gfeed, dm, do),
        [wide32, wide, ((1, width), F32), rowsb, rowsb],
    )

    def tensor_reduce(g0, g1, g2, g3):
        g0 = add(g0, swap(g1, "tensor", 1))
        g2 = add(g2, swap(g3, "tensor", 1))
        got = swap(g2, "tensor", 2)
        return add(g0[:half], got[:half]), add(g0[half:], got[half:])

    g_hgate, g_hup, g_hdown = [reduce_halves(g_heavy[i], g_heavy[i + 1], "dp") for i in (0, 2, 4)]
    g_light = reduce_halves(*tensor_reduce(g_l0, g_l1, g_l2, g_l3), "dp")
    bm, bo = tensor_sum(bm, bo)
    (output,) = call(
        output_body, 2 * rows * width * (width + ROUTED), (where, src, index, mid, feed, bm, bo), [wide]
    )

    gm, go = tensor_sum(gm, go)

    def local_backward(which):
        args = sum((tuple(heads[i]) + w_lout[i] for i in which), ())
        outs = [((rows, c_lout), BF16), ((extent, 2 * c_lout), BF16), ((width, c_lqkv + c_lout), BF16)]
        res = call(
            functools.partial(local_backward_body, len(which)),
            len(which) * (2 * extent * width * (c_lqkv + 2 * c_lout) + 20 * rows * 384 * 128),
            (where, gattn, a1) + args, outs * len(which),
            scratch=[pltpu.VMEM((extent, 2 * c_lout), F32), pltpu.VMEM((rows, c_lout), BF16)],
        )
        return [res[3 * i : 3 * i + 3] for i in range(len(which))]

    back2, back3 = local_backward((2, 3))
    (back1,) = local_backward((1,))
    (back0,) = local_backward((0,))
    qm, qo, km, ko, h_keep, h_send, grad_router_qk = call(
        heavy_backward_body, 2 * ROUTED * width * hw * 8 + 10 * ROUTED * ROUTED * hw * 3,
        (gains, gm, go, hy, routed, hqkv, ho, hlse) + w_heavy,
        [rowsb] * 4 + [((half, 4 * hw), BF16)] * 2 + [((2, width), F32)],
    )
    da1, first, last = call(
        functools.partial(local_input_body, tensor), 2 * extent * width * c_lqkv * tensor,
        sum(((b[0], b[1]) + w for b, w in zip((back0, back1, back2, back3), w_lqkv)), ()),
        [wide32, ((WINDOW, width), BF16), ((WINDOW, width), BF16)],
    )
    before, behind = neighbours(first, last)
    qm, qo = tensor_sum(qm, qo)
    km, ko = tensor_sum(km, ko)
    input_grad, grad_gain1 = call(
        finish_body, 2 * rows * width * (3 * width + 2 * ROUTED),
        (where, src, gains, index, x, dmid, da1, before, behind, qm, qo, km, ko),
        [wide32, ((1, width), F32)],
    )
    g_hattn = reduce_halves(h_keep, h_send, "dp")
    g_lattn = reduce_halves(*tensor_reduce(back0[2], back2[2], back1[2], back3[2]), "dp")

    small = jnp.concatenate([grad_gain1, grad_gain2, grad_router_qk, grad_router_f], axis=0)
    small = small.reshape(5, dp, tensor, -1).transpose(1, 2, 0, 3)
    small = reduce_halves(small[: dp // 2], small[dp // 2 :], "dp")[0]
    for bit in (2, 1):
        half_count = small.shape[0] // 2
        high = (tensor_index & bit) != 0
        lower, upper = small[:half_count], small[half_count:]
        small = jnp.where(high, upper, lower) + swap(jnp.where(high, lower, upper), "tensor", bit)
    small = small[0]

    def unflat(grad, count):
        return grad.reshape(shard, count, -1).transpose(1, 0, 2)

    return (
        output[None],
        input_grad[None],
        unflat(g_lattn[:, :c_lqkv], 3),
        g_lattn[:, c_lqkv:].T,
        unflat(g_hattn[:, : 3 * hw], 3),
        g_hattn[:, 3 * hw :].T,
        unflat(g_light[:, : 2 * c_lin], 2),
        g_light[:, 2 * c_lin :].T,
        jnp.stack([g_hgate, g_hup]),
        g_hdown.T,
        small[:2],
        small[2:],
    )


def solution(mesh):
    rows = P("dp", "tensor", None)
    index = P("dp", None)
    cols = P(None, "dp", "tensor")
    back = P("tensor", "dp")
    both = P(None, ("dp", "tensor"))
    weights = (cols, back) * 4
    return jax.shard_map(
        local,
        mesh=mesh,
        in_specs=(rows, rows, P("dp"), index, index, index) + weights + (both, both),
        out_specs=(rows, rows) + weights + (both, both),
        check_vma=False,
    )
```

```python
import functools

import jax
import jax.numpy as jnp
import numpy as np
from jax import lax
from jax.experimental import pallas as pl
from jax.experimental.pallas import tpu as pltpu
from jax.sharding import PartitionSpec as P

HEAD = 64
SLOT = 2048
WINDOW = 128
ROUTED = 256
NORM_EPS = 1e-06
SCALE = 0.125
MASKED = -1e30
F32 = jnp.float32
BF16 = jnp.bfloat16


def mm(left, right, dims):
    return lax.dot_general(left, right, (dims, ((), ())), preferred_element_type=F32)


def nn(left, right):
    return mm(left, right, ((1,), (0,)))


def nt(left, right):
    return mm(left, right, ((1,), (1,)))


def tn(left, right):
    return mm(left, right, ((0,), (0,)))


def low(values):
    return values.astype(BF16)


def swap(values, axis, bit, label="swap"):
    size = lax.axis_size(axis)
    with jax.named_scope(f"{label}_{axis}{bit}"):
        return lax.ppermute(values, axis, [(i, i ^ bit) for i in range(size)])


def bits_of(axis):
    size = lax.axis_size(axis)
    return [1 << b for b in range(size.bit_length() - 1)]


def relative_order(axis):
    order = [0]
    for bit in reversed(bits_of(axis)):
        order = order + [r ^ bit for r in order]
    return order


def after(values, *others):
    return lax.optimization_barrier((values,) + others)[0]


class Order:
    def __init__(self):
        self.last = None

    def __call__(self, values):
        if self.last is None:
            return values
        return lax.optimization_barrier((values, self.last))[0]

    def call(self, body, args, outs, scratch=()):
        first = next(i for i, a in enumerate(args) if a.ndim > 1)
        args = args[:first] + (self(args[first]),) + args[first + 1 :]
        res = call(body, args, outs, scratch)
        self.last = res[0]
        return res

    def add(self, left, right, kind=BF16):
        self.last = (self(left).astype(F32) + right.astype(F32)).astype(kind)
        return self.last

    def join(self, *parts):
        self.last = jnp.concatenate((self(parts[0]),) + parts[1:], axis=0)
        return self.last


class Gather:
    def __init__(self, order, block, axis, label):
        self.order, self.axis, self.label = order, axis, label
        self.bits = list(reversed(bits_of(axis)))
        self.have = block
        self.got = swap(block, axis, self.bits[0], label)

    def step(self):
        self.bits = self.bits[1:]
        self.have = self.order.join(self.have, self.got)
        self.got = swap(self.have, self.axis, self.bits[0], self.label)

    def steps_but_last(self, kept):
        while len(self.bits) > kept:
            self.step()

    def halves(self):
        return self.have, self.got


class Reduce:
    def __init__(self, order, keep, send, bits, label):
        self.order, self.bits, self.label = order, bits, label
        self.keep, self.got = keep, swap(send, "dp", bits[0], label)

    def step(self):
        half = self.keep.shape[0] // 2
        send = self.order.add(self.keep[half:], self.got[half:], self.keep.dtype)
        self.keep = self.order.add(self.keep[:half], self.got[:half], self.keep.dtype)
        self.bits = self.bits[1:]
        self.got = swap(send, "dp", self.bits[0], self.label)

    def steps_but_last(self):
        while len(self.bits) > 1:
            self.step()

    def result(self):
        self.steps_but_last()
        return self.order.add(self.keep, self.got, F32)


class TensorSum:
    def __init__(self, order, mine, other, label):
        self.order, self.mine, self.label = order, mine, label
        self.got = swap(other, "tensor", 1, label)

    def step(self):
        self.mine = self.order.add(self.mine, self.got)
        self.got = swap(self.mine, "tensor", 2, self.label)

    def result(self):
        self.mine = self.order.add(self.mine, self.got)
        return self.mine, swap(self.mine, "tensor", 1, self.label)


class PairSum:
    def __init__(self, order, values, label):
        self.order, self.values, self.label = order, values, label
        self.got = swap(values, "tensor", 1, label)

    def result(self):
        chip = self.order.add(self.values, self.got)
        return chip, swap(chip, "tensor", 2, self.label)


def neighbours(first, last):
    size = lax.axis_size("tensor")
    before = lax.ppermute(last, "tensor", [(i, i + 1) for i in range(size - 1)])
    behind = lax.ppermute(first, "tensor", [(i + 1, i) for i in range(size - 1)])
    return before, behind


VMEM = pl.BlockSpec(memory_space=pltpu.VMEM)
SMEM = pl.BlockSpec(memory_space=pltpu.SMEM)


def call(body, args, outs, scratch=()):
    return pl.pallas_call(
        body,
        in_specs=[SMEM if a.ndim == 1 else VMEM for a in args],
        out_specs=[VMEM] * len(outs),
        out_shape=[jax.ShapeDtypeStruct(shape, dtype) for shape, dtype in outs],
        scratch_shapes=scratch,
        compiler_params=pltpu.CompilerParams(vmem_limit_bytes=48 << 20),
        cost_estimate=pl.CostEstimate(flops=int(2e10), bytes_accessed=0, transcendentals=0),
    )(*args)


def mul(x, first, second):
    half = first.shape[0]
    return nn(x[:, :half], first) + nn(x[:, half:], second)


def mul_t(y, first, second):
    return jnp.concatenate([nt(y, first), nt(y, second)], axis=1)


def sigmoid(v):
    return 1.0 / (1.0 + jnp.exp(-v))


def rms(v, gain):
    return v * lax.rsqrt(jnp.mean(v * v, axis=-1, keepdims=True) + NORM_EPS) * gain


def rms_back(v, gain, grad):
    r = lax.rsqrt(jnp.mean(v * v, axis=-1, keepdims=True) + NORM_EPS)
    n = v * r
    h = grad * gain
    return r * (h - n * jnp.mean(h * n, axis=-1, keepdims=True)), jnp.sum(grad * n, axis=0, keepdims=True)


def gelu_parts(v):
    root = 0.7978845608028654
    th = jnp.tanh(root * (v + 0.044715 * v * v * v))
    value = 0.5 * v * (1.0 + th)
    slope = 0.5 * (1.0 + th) + 0.5 * v * (1.0 - th * th) * root * (1.0 + 3 * 0.044715 * v * v)
    return value, slope


def iota(shape, axis):
    return lax.broadcasted_iota(jnp.int32, shape, axis)


def ones_where(mask):
    return low(jnp.where(mask, 1.0, 0.0))


def permutation(src_ref):
    size = src_ref.shape[1]
    return ones_where(iota((size, size), 0) == src_ref[...])


def valid_rows(where_ref, rows):
    return where_ref[0] + iota((rows, 1), 0) < where_ref[1]


def pick(cols_ref, which, where_ref, rows):
    index = cols_ref[:, which : which + 1]
    return ones_where(index == where_ref[0] + iota((index.shape[0], rows), 1))


def place(rows_ref, which, where_ref, rows):
    index = rows_ref[which : which + 1, :]
    return ones_where(index == where_ref[0] + iota((rows, index.shape[1]), 0))


def core_of(where_ref):
    return where_ref[where_ref.shape[0] - 1]


def split(where_ref, values, mine_ref, other_ref, which):
    size = values.shape[0] // 2
    first = core_of(where_ref) == 0
    lower, upper = values[:size], values[size:]
    mine_ref[which] = jnp.where(first, lower, upper).astype(mine_ref.dtype)
    other_ref[which] = jnp.where(first, upper, lower).astype(other_ref.dtype)


def both(where_ref, mine_ref, other_ref, which):
    first = core_of(where_ref) == 0
    mine, other = mine_ref[which].astype(F32), other_ref[which].astype(F32)
    return jnp.concatenate([jnp.where(first, mine, other), jnp.where(first, other, mine)], axis=0)


def total(one_ref, two_ref, which=0):
    return low(one_ref[which].astype(F32) + two_ref[which].astype(F32))


def start_body(where_ref, src_ref, cols_ref, x_ref, cot_ref, xr_ref, g_ref, mine_ref, other_ref):
    rows = x_ref.shape[0]
    perm = permutation(src_ref)
    xr = low(nn(x_ref[...], perm))
    xr_ref[...] = xr
    g = low(jnp.where(valid_rows(where_ref, rows), nn(cot_ref[...], perm), 0.0))
    g_ref[...] = g
    for which, values in enumerate((xr, xr, g)):
        split(where_ref, nn(pick(cols_ref, which, where_ref, rows), values), mine_ref, other_ref, which)


def norm_body(src_ref, gains_ref, before_ref, x_ref, after_ref, a1_ref, out_ref):
    edge, rows = before_ref.shape[0], x_ref.shape[0]
    perm = permutation(src_ref)
    gains = nn(low(gains_ref[...]), perm)
    out_ref[...] = gains
    gain = gains[0:1, :]
    a1_ref[0:edge, :] = low(rms(nn(before_ref[...], perm), gain))
    a1_ref[edge : edge + rows, :] = low(rms(x_ref[...].astype(F32), gain))
    a1_ref[edge + rows :, :] = low(rms(nn(after_ref[...], perm), gain))


def lane_masks(width):
    lane = iota((1, width), 1) // HEAD
    return [(lane == h).astype(F32) for h in range(width // HEAD)]


def stack_heads(values, masks):
    return jnp.concatenate([values * m.astype(values.dtype) for m in masks], axis=0)


def join_heads(values, masks):
    size = values.shape[0] // len(masks)
    return sum(values[h * size : (h + 1) * size] * m for h, m in enumerate(masks))


def band(i, where_ref):
    start, length = where_ref[0], where_ref[1]
    shape = (2 * WINDOW, 3 * WINDOW)
    q_off = iota(shape, 0) % WINDOW
    k_off = iota(shape, 1)
    q_pos = start + i * WINDOW + q_off
    k_pos = start + (i - 1) * WINDOW + k_off
    ahead = k_off - q_off
    near = (ahead >= 1) & (ahead <= 2 * WINDOW - 1)
    inside = (k_pos >= 0) & (k_pos < SLOT)
    return near & inside & ((k_pos < length) | (q_pos >= length))


def local_forward_body(where_ref, a1_ref, c_ref, d_ref, qkv_ref, lo_ref, lse_ref):
    qkv_ref[...] = low(mul(a1_ref[...], c_ref[:, :384], d_ref[:, :384]))
    masks = lane_masks(2 * HEAD)

    @pl.loop(0, lo_ref.shape[0] // WINDOW)
    def _(i):
        base = pl.multiple_of(i * WINDOW, WINDOW)
        q = qkv_ref[pl.ds(base + WINDOW, WINDOW), 0:128]
        k = qkv_ref[pl.ds(base, 3 * WINDOW), 128:256]
        v = qkv_ref[pl.ds(base, 3 * WINDOW), 256:384]
        s = nt(stack_heads(q, masks), k) * SCALE
        s = jnp.where(band(i, where_ref), s, MASKED)
        top = jnp.max(s, axis=-1, keepdims=True)
        e = jnp.exp(s - top)
        total = jnp.sum(e, axis=-1, keepdims=True)
        o = nn(low(e / total), v)
        lo_ref[pl.ds(base, WINDOW), :] = low(join_heads(o, masks))
        lse_ref[pl.ds(base, WINDOW), :] = join_heads(top + jnp.log(total), masks)


def local_backward_body(count, where_ref, g_ref, a1_ref, *refs):
    per = 5
    ins = [refs[i * per : (i + 1) * per] for i in range(count)]
    outs = [refs[count * per + i * 3 : count * per + (i + 1) * 3] for i in range(count)]
    dkv_acc, dlo_ref = refs[count * (per + 3) :]
    rows = g_ref.shape[0]
    masks = lane_masks(2 * HEAD)
    for (qkv_ref, lo_ref, lse_ref, c_ref, d_ref), (dq_ref, dkv_ref, grad_ref) in zip(ins, outs):
        dlo_ref[...] = low(mul(g_ref[...], c_ref[:, 384:], d_ref[:, 384:]))
        dkv_acc[...] = jnp.zeros_like(dkv_acc)

        @pl.loop(0, rows // WINDOW)
        def _(i, qkv_ref=qkv_ref, lse_ref=lse_ref, dq_ref=dq_ref):
            base = pl.multiple_of(i * WINDOW, WINDOW)
            q = stack_heads(qkv_ref[pl.ds(base + WINDOW, WINDOW), 0:128], masks)
            k = qkv_ref[pl.ds(base, 3 * WINDOW), 128:256]
            v = qkv_ref[pl.ds(base, 3 * WINDOW), 256:384]
            g = stack_heads(dlo_ref[pl.ds(base, WINDOW), :], masks)
            lse = lse_ref[pl.ds(base, WINDOW), :]
            lse = jnp.concatenate([lse[:, 0:1], lse[:, HEAD : HEAD + 1]], axis=0)
            s = jnp.where(band(i, where_ref), nt(q, k) * SCALE, MASKED)
            p = jnp.exp(s - lse)
            dp = nt(g, v)
            ds = low(p * (dp - jnp.sum(p * dp, axis=-1, keepdims=True)))
            dq_ref[pl.ds(base, WINDOW), :] = low(join_heads(nn(ds, k), masks) * SCALE)
            dkv_acc[pl.ds(base, 3 * WINDOW), 0:128] += tn(ds, q) * SCALE
            dkv_acc[pl.ds(base, 3 * WINDOW), 128:256] += tn(low(p), g)

        dkv_ref[...] = low(dkv_acc[...])
        grad_ref[:, 0:128] = low(tn(a1_ref[WINDOW : WINDOW + rows, :], dq_ref[...]))
        grad_ref[:, 128:384] = low(tn(a1_ref[...], dkv_ref[...]))
        grad_ref[:, 384:512] = low(tn(g_ref[...], lo_ref[...]))


def local_input_body(count, *refs):
    ins = [refs[i * 4 : (i + 1) * 4] for i in range(count)]
    da1_ref, first_ref, last_ref = refs[count * 4 :]
    rows, edge = da1_ref.shape[0], first_ref.shape[0]
    half = ins[0][2].shape[0]
    dkv = jnp.concatenate([r[1][...] for r in ins], axis=1)
    dq = jnp.concatenate([r[0][...] for r in ins], axis=1)
    for side in range(2):
        cut = slice(side * half, (side + 1) * half)
        w_kv = jnp.concatenate([r[2 + side][:, 128:384] for r in ins], axis=1)
        w_q = jnp.concatenate([r[2 + side][:, 0:128] for r in ins], axis=1)
        part = nt(dkv, w_kv)
        first_ref[:, cut] = low(part[:edge])
        da1_ref[:, cut] = part[edge : edge + rows] + nt(dq, w_q)
        last_ref[:, cut] = low(part[edge + rows :])


def ordered(where_ref, w_ref, cut):
    return jnp.concatenate([w_ref[where_ref[2 + r], :, cut] for r in range(w_ref.shape[0])], axis=0)


def light_feed_body(first, where_ref, *refs):
    if first:
        a2_ref, g_ref, *refs = refs
    else:
        a2_ref, g_ref, feed_in, da2_in, *refs = refs
    feed_ref, da2_ref, *grads = refs[2:]
    hidden = refs[0].shape[2] // 3
    feed = da2 = None
    a2, g = a2_ref[...], g_ref[...]
    for w_ref, grad_ref in zip(refs[:2], grads):
        w_in = ordered(where_ref, w_ref, slice(0, 2 * hidden))
        w_down = ordered(where_ref, w_ref, slice(2 * hidden, 3 * hidden))
        gu = nn(a2, w_in)
        up = gu[:, hidden:]
        value, slope = gelu_parts(gu[:, :hidden])
        lh = low(value * up)
        dlh = low(nn(g, w_down)).astype(F32)
        dgu = jnp.concatenate([low(dlh * up * slope), low(dlh * value)], axis=1)
        new_feed = nt(lh, w_down)
        new_da2 = nt(dgu, w_in)
        feed = new_feed if feed is None else feed + new_feed
        da2 = new_da2 if da2 is None else da2 + new_da2
        grad_ref[:, : 2 * hidden] = low(tn(a2, dgu))
        grad_ref[:, 2 * hidden :] = low(tn(g, lh))
    if first:
        feed_ref[...] = feed
        da2_ref[...] = da2
    else:
        feed_ref[...] = feed_in[...] + feed
        da2_ref[...] = da2_in[...] + da2


def heavy_feed_body(
    where_ref, gains_ref, one_ref, two_ref, picked_ref, other_ref, w_ref,
    drows_ref, back_ref, drouter_ref, grad_ref
):
    blocks, shard, cols = w_ref.shape
    hidden = cols // 3
    step = min(hidden, 256)
    f = total(one_ref, two_ref)
    f32 = f.astype(F32)
    router = gains_ref[4:5, :]
    sf = scores(f, router)
    g32 = both(where_ref, picked_ref, other_ref, 2)
    tf = low(sf * g32)
    hf = daf = None
    for j in range(hidden // step):
        cuts = [slice(i * hidden + j * step, i * hidden + (j + 1) * step) for i in range(3)]
        w_gate, w_up, w_down = [ordered(where_ref, w_ref, cut) for cut in cuts]
        up = nn(f, w_up)
        value, slope = gelu_parts(nn(f, w_gate))
        hh = low(value * up)
        dhh = low(nn(tf, w_down)).astype(F32)
        dgate, dup = low(dhh * up * slope), low(dhh * value)
        new_hf = nt(hh, w_down)
        new_daf = nt(dgate, w_gate) + nt(dup, w_up)
        hf = new_hf if hf is None else hf + new_hf
        daf = new_daf if daf is None else daf + new_daf
        for x, dy, cut in zip((f, f, tf), (dgate, dup, hh), cuts):
            grad = low(tn(x, dy))
            for r in range(blocks):
                grad_ref[where_ref[2 + r], :, cut] = grad[r * shard : (r + 1) * shard]
    back_ref[0] = low(sf * hf)
    wf = jnp.sum(g32 * hf, axis=-1, keepdims=True) * sf * (1.0 - sf)
    drows_ref[0] = low(daf + wf * router)
    drouter_ref[...] = jnp.sum(wf * f32, axis=0, keepdims=True)


def scores(rows, router):
    return sigmoid(jnp.sum(rows.astype(F32) * router, axis=-1, keepdims=True))


def heavy_forward_body(
    where_ref, gains_ref, mine_ref, other_ref, c_ref, d_ref,
    rows_ref, hqkv_ref, ho_ref, lse_ref, hy_ref, back_ref
):
    width = c_ref.shape[1] // 4
    masks = lane_masks(width)
    gain = gains_ref[0:1, :]
    q_rows = low(rms(both(where_ref, mine_ref, other_ref, 0), gain))
    k_rows = low(rms(both(where_ref, mine_ref, other_ref, 1), gain))
    sq = scores(q_rows, gains_ref[2:3, :])
    kvin = low(scores(k_rows, gains_ref[3:4, :]) * k_rows.astype(F32))
    rows_ref[0] = q_rows
    rows_ref[1] = k_rows
    rows_ref[2] = kvin
    hq = low(mul(q_rows, c_ref[:, 0:width], d_ref[:, 0:width]))
    hk = low(mul(kvin, c_ref[:, width : 2 * width], d_ref[:, width : 2 * width]))
    hv = low(mul(kvin, c_ref[:, 2 * width : 3 * width], d_ref[:, 2 * width : 3 * width]))
    hqkv_ref[0] = hq
    hqkv_ref[1] = hk
    hqkv_ref[2] = hv
    s = nt(stack_heads(hq, masks), hk) * SCALE
    top = jnp.max(s, axis=-1, keepdims=True)
    e = jnp.exp(s - top)
    total = jnp.sum(e, axis=-1, keepdims=True)
    ho = low(join_heads(nn(low(e / total), hv), masks))
    ho_ref[...] = ho
    lse_ref[...] = join_heads(top + jnp.log(total), masks)
    hy = mul_t(ho, c_ref[:, 3 * width :], d_ref[:, 3 * width :])
    hy_ref[...] = hy
    back_ref[0] = low(sq * hy)


def heavy_backward_body(
    where_ref, gains_ref, gm_ref, go_ref, hy_ref, rows_ref, hqkv_ref, ho_ref, lse_ref, c_ref, d_ref,
    dm_ref, do_ref, keep_ref, send_ref, drouter_ref
):
    width, half = c_ref.shape[1] // 4, c_ref.shape[0]
    masks = lane_masks(width)
    q_rows, k_rows, kvin = rows_ref[0], rows_ref[1], rows_ref[2]
    q32, k32 = q_rows.astype(F32), k_rows.astype(F32)
    sq = scores(q_rows, gains_ref[2:3, :])
    sk = scores(k_rows, gains_ref[3:4, :])
    ga = total(gm_ref, go_ref).astype(F32)
    dsq = jnp.sum(ga * hy_ref[...], axis=-1, keepdims=True)
    tq = low(sq * ga)
    cuts = [slice(i * width, (i + 1) * width) for i in range(4)]
    dho = low(mul(tq, c_ref[:, cuts[3]], d_ref[:, cuts[3]]))
    q3 = stack_heads(hqkv_ref[0], masks)
    hk, hv = hqkv_ref[1], hqkv_ref[2]
    g3 = stack_heads(dho, masks)
    lse = lse_ref[...]
    lse3 = jnp.concatenate([lse[:, h * HEAD : h * HEAD + 1] for h in range(len(masks))], axis=0)
    p = jnp.exp(nt(q3, hk) * SCALE - lse3)
    dp = nt(g3, hv)
    ds = low(p * (dp - jnp.sum(p * dp, axis=-1, keepdims=True)))
    dhq = low(join_heads(nn(ds, hk), masks) * SCALE)
    dhk = low(tn(ds, q3) * SCALE)
    dhv = low(tn(low(p), g3))
    dkv = mul_t(dhk, c_ref[:, cuts[1]], d_ref[:, cuts[1]]) + mul_t(dhv, c_ref[:, cuts[2]], d_ref[:, cuts[2]])
    wq = dsq * sq * (1.0 - sq)
    wk = jnp.sum(dkv * k32, axis=-1, keepdims=True) * sk * (1.0 - sk)
    split(where_ref, mul_t(dhq, c_ref[:, cuts[0]], d_ref[:, cuts[0]]) + wq * gains_ref[2:3, :], dm_ref, do_ref, 0)
    split(where_ref, sk * dkv + wk * gains_ref[3:4, :], dm_ref, do_ref, 1)
    drouter_ref[0:1, :] = jnp.sum(wq * q32, axis=0, keepdims=True)
    drouter_ref[1:2, :] = jnp.sum(wk * k32, axis=0, keepdims=True)
    for cut, x, dy in zip(cuts, (q_rows, kvin, kvin, tq), (dhq, dhk, dhv, ho_ref[...])):
        keep_ref[:, cut] = low(tn(x[:, :half], dy))
        send_ref[:, cut] = low(tn(x[:, half:], dy))


def middle_body(where_ref, gains_ref, cols_ref, rows_ref, x_ref, rm_ref, ro_ref, *refs):
    ins = [refs[i * 3 : (i + 1) * 3] for i in range(4)]
    mid_ref, a2_ref, picked_ref = refs[12:]
    rows = x_ref.shape[0]
    lo = jnp.concatenate([r[0][...] for r in ins], axis=1)
    c = jnp.concatenate([r[1][:, 384:] for r in ins], axis=1)
    d = jnp.concatenate([r[2][:, 384:] for r in ins], axis=1)
    attn = mul_t(lo, c, d) + nn(place(rows_ref, 0, where_ref, rows), total(rm_ref, ro_ref))
    mid = x_ref[...].astype(F32) + jnp.where(valid_rows(where_ref, rows), attn, 0.0)
    mid_ref[...] = mid
    a2 = low(rms(mid, gains_ref[1:2, :]))
    a2_ref[...] = a2
    picked_ref[0] = low(nn(pick(cols_ref, 2, where_ref, rows), a2))


def output_body(where_ref, src_ref, rows_ref, mid_ref, feed_ref, gm_ref, go_ref, out_ref):
    rows = mid_ref.shape[0]
    feed = feed_ref[...] + nn(place(rows_ref, 2, where_ref, rows), total(gm_ref, go_ref, 1))
    out = low(mid_ref[...] + jnp.where(valid_rows(where_ref, rows), feed, 0.0))
    out_ref[...] = low(nt(out, permutation(src_ref)))


def turn_body(
    where_ref, gains_ref, cols_ref, rows_ref, mid_ref, da2_ref, g_ref, am_ref, ao_ref, back_ref,
    dmid_ref, gattn_ref, dgain_ref, picked_ref
):
    rows = mid_ref.shape[0]
    da2 = da2_ref[...] + nn(place(rows_ref, 2, where_ref, rows), total(am_ref, ao_ref))
    back, dgain_ref[...] = rms_back(mid_ref[...], gains_ref[1:2, :], da2)
    dmid = g_ref[...].astype(F32) + back
    dmid_ref[...] = dmid
    gattn = low(jnp.where(valid_rows(where_ref, rows), dmid, 0.0))
    gattn_ref[...] = gattn
    picked_ref[0] = low(nn(pick(cols_ref, 0, where_ref, rows), gattn))
    picked_ref[1] = back_ref[0]


def unpermute(values, perm):
    one = low(values)
    rest = values - one.astype(F32)
    two = low(rest)
    three = low(rest - two.astype(F32))
    return nt(one, perm) + nt(two, perm) + nt(three, perm)


def finish_body(
    where_ref, src_ref, gains_ref, rows_ref, x_ref, dmid_ref, da1_ref, before_ref, after_ref,
    dm_ref, do_ref, dgain2_ref, dqk_ref, drf_ref, grad_ref, small_ref
):
    rows, edge = x_ref.shape[0], before_ref.shape[0]
    da1 = da1_ref[...] + nn(place(rows_ref, 0, where_ref, rows), low(both(where_ref, dm_ref, do_ref, 0)))
    da1 = da1 + nn(place(rows_ref, 1, where_ref, rows), low(both(where_ref, dm_ref, do_ref, 1)))
    da1 = jnp.concatenate(
        [
            da1[:edge] + before_ref[...].astype(F32),
            da1[edge : rows - edge],
            da1[rows - edge :] + after_ref[...].astype(F32),
        ],
        axis=0,
    )
    back, dgain1 = rms_back(x_ref[...].astype(F32), gains_ref[0:1, :], da1)
    perm = permutation(src_ref)
    grad_ref[...] = unpermute(dmid_ref[...] + back, perm)
    small = jnp.concatenate([dgain1, dgain2_ref[...], dqk_ref[...], drf_ref[...]], axis=0)
    small_ref[...] = unpermute(small, perm)


def local(
    inputs, cotangent, lengths, query_index, key_index, token_index,
    light_qkv, light_out, heavy_qkv, heavy_out, light_in, light_down, heavy_in, heavy_down,
    norm_gains, routers,
):
    rows, width = inputs.shape[1], inputs.shape[2]
    extent = rows + 2 * WINDOW
    shard, half = light_qkv.shape[1], width // 2
    dp, tensor = lax.axis_size("dp"), lax.axis_size("tensor")
    dp_index, tensor_index = lax.axis_index("dp"), lax.axis_index("tensor")
    c_lqkv, c_lout = 3 * light_qkv.shape[2], light_out.shape[0]
    c_lin, c_ldown, c_hin = light_in.shape[2], light_down.shape[0], heavy_in.shape[2]
    hw = heavy_out.shape[0]
    blocks = np.array(relative_order("dp"), np.int32)
    place_of = np.arange(width, dtype=np.int32)
    src = ((dp_index ^ blocks[place_of // shard]) * shard + place_of % shard)[None].astype(jnp.int32)
    where = jnp.concatenate(
        [jnp.stack([tensor_index * rows, lengths[0]]), dp_index ^ blocks, (tensor_index & 1)[None]]
    ).astype(jnp.int32)
    index = jnp.concatenate([query_index, key_index, token_index], axis=0)
    index_cols = index.T

    order = Order()
    rows1, rows2 = [((n, ROUTED, width), BF16) for n in (1, 2)]
    halves2, halves3 = [((n, ROUTED // 2, width), BF16) for n in (2, 3)]
    wide = ((rows, width), BF16)
    wide32 = ((rows, width), F32)
    gain_row = ((1, width), F32)

    def flat(w):
        return w.transpose(1, 0, 2).reshape(shard, -1)

    own = inputs[0]
    feed_piece = jnp.concatenate([heavy_in[0], heavy_in[1], heavy_down.T], axis=1)
    light_piece = jnp.concatenate([flat(light_in), light_down.T], axis=1)
    light_w = lax.all_gather(light_piece, "dp", axis=0)
    local_piece = jnp.concatenate([flat(light_qkv), light_out.T], axis=1)
    local_w = Gather(order, local_piece, "dp", "local")
    small = jnp.concatenate([norm_gains, routers], axis=0)
    small = jnp.broadcast_to(small[None], (dp * tensor,) + small.shape)
    with jax.named_scope("gains"):
        small = lax.all_to_all(small, ("dp", "tensor"), 0, 0)
    gains = small.transpose(1, 0, 2).reshape(5, width)
    before, behind = neighbours(own[:WINDOW], own[rows - WINDOW :])
    x, gfeed, picked, other = order.call(
        start_body, (where, src, index_cols, own, cotangent[0]), [wide, wide, halves3, halves3]
    )
    picks = TensorSum(order, picked, other, "picked")
    heavy_piece = order(jnp.concatenate([flat(heavy_qkv), heavy_out.T], axis=1))
    local_w.step()
    feed_w = lax.all_gather(after(feed_piece, local_w.have), "dp", axis=0)
    heavy_w = Gather(order, order(heavy_piece), "dp", "heavy")
    local_w.steps_but_last(1)
    local_first, local_second = local_w.halves()
    picks.step()
    gains = order(gains)
    order.last = gains = gains.astype(F32)
    heavy_w.step()

    def across(first, second, bit, label):
        return swap(first, "tensor", bit, label), swap(second, "tensor", bit, label)

    a1, gains = order.call(
        norm_body, (src, gains, before, x, behind), [((extent, width), BF16), ((5, width), F32)]
    )

    def local_forward(pair):
        return order.call(
            local_forward_body, (where, a1) + pair,
            [((extent, c_lqkv), BF16), ((rows, c_lout), BF16), ((rows, c_lout), F32)],
        )

    w0 = (local_first, local_second)
    w2, w1 = across(*w0, 2, "local"), across(*w0, 1, "local")
    head0 = local_forward(w0)
    heavy_w.steps_but_last(1)
    heavy_w = heavy_w.halves()
    head1 = local_forward(w1)
    picked, other = picks.result()
    w3 = across(*w2, 1, "local")
    head2 = local_forward(w2)
    routed, hqkv, ho, hlse, hy, back = order.call(
        heavy_forward_body, (where, gains, picked, other) + heavy_w,
        [((3, ROUTED, width), BF16), ((3, ROUTED, hw), BF16), ((ROUTED, hw), BF16), ((ROUTED, hw), F32),
         ((ROUTED, width), F32), rows1],
    )
    routed_sum = PairSum(order, back, "routed")
    rm, ro = routed_sum.result()
    head3 = local_forward(w3)
    heads = (head0, head1, head2, head3)
    local_w = (w0, w1, w2, w3)
    mid, a2, am = order.call(
        middle_body,
        (where, gains, index_cols, index, x, rm, ro) + sum(((h[1],) + w for h, w in zip(heads, local_w)), ()),
        [wide32, wide, rows1],
    )

    tokens = PairSum(order, am, "tokens")
    l0 = light_w
    l1 = swap(l0, "tensor", 1, "light")
    l2 = swap(after(l0, mid), "tensor", 2, "light")

    def light_feed(done, *pairs):
        return order.call(
            functools.partial(light_feed_body, not done), (where, a2, gfeed) + done + pairs,
            [wide32, wide32] + [((width, 3 * c_lin), BF16)] * 2,
        )

    feed, da2, g_l0, g_l1 = light_feed((), l0, l1)
    g1_got = swap(g_l1, "tensor", 1, "glight")
    am, ao = tokens.result()
    l3 = swap(after(l2, am), "tensor", 1, "light")
    bits = bits_of("dp")
    drows, back, grad_router_f, g_feed = order.call(
        heavy_feed_body, (where, gains, am, ao, picked, other, feed_w),
        [rows1, rows1, gain_row, ((dp, shard, 3 * c_hin), BF16)],
    )
    g_feed = lax.psum_scatter(g_feed, "dp", scatter_dimension=0).astype(F32)
    dtokens = PairSum(order, drows, "dtokens")
    feed, da2, g_l2, g_l3 = light_feed((feed, da2), l2, l3)
    g3_got = swap(g_l3, "tensor", 1, "glight")
    dm, do = dtokens.result()
    g_l2 = order.add(g_l2, g3_got)
    g2_got = swap(g_l2, "tensor", 2, "glight")
    g_l0 = order.add(g_l0, g1_got)
    dmid, gattn, grad_gain2, ga = order.call(
        turn_body, (where, gains, index_cols, index, mid, da2, gfeed, dm, do, back), [wide32, wide, gain_row, rows2]
    )

    dattn = PairSum(order, ga, "dattn")

    def local_backward(which):
        args = sum((tuple(heads[i]) + local_w[i] for i in which), ())
        outs = [((rows, c_lout), BF16), ((extent, 2 * c_lout), BF16), ((width, c_lqkv + c_lout), BF16)]
        res = order.call(
            functools.partial(local_backward_body, len(which)), (where, gattn, a1) + args, outs * len(which),
            scratch=[pltpu.VMEM((extent, 2 * c_lout), F32), pltpu.VMEM((rows, c_lout), BF16)],
        )
        return [res[3 * i : 3 * i + 3] for i in range(len(which))]

    (back3,) = local_backward((3,))
    s3_got = swap(back3[2], "tensor", 1, "glocal")
    gm, go = dattn.result()
    l_send = order.add(g_l0[half:], g2_got[half:])
    l_keep = order.add(g_l0[:half], g2_got[:half])
    g_l = Reduce(order, l_keep, l_send, bits, "glight")
    (back1,) = local_backward((1,))
    s1_got = swap(back1[2], "tensor", 1, "glocal")
    (back2,) = local_backward((2,))
    s2 = order.add(back2[2], s3_got)
    s2_got = swap(s2, "tensor", 2, "glocal")
    (back0,) = local_backward((0,))
    s0 = order.add(back0[2], s1_got)
    dm, do, h_keep, h_send, grad_router_qk = order.call(
        heavy_backward_body, (where, gains, gm, go, hy, routed, hqkv, ho, hlse) + heavy_w,
        [halves2] * 2 + [((half, 4 * hw), BF16)] * 2 + [((2, width), F32)],
    )
    drows = TensorSum(order, dm, do, "drows")
    g_h = Reduce(order, h_keep, h_send, bits, "gheavy")
    da1, first, last = order.call(
        functools.partial(local_input_body, tensor),
        sum(((b[0], b[1]) + w for b, w in zip((back0, back1, back2, back3), local_w)), ()),
        [wide32, ((WINDOW, width), BF16), ((WINDOW, width), BF16)],
    )
    before, behind = neighbours(first, last)
    drows.step()
    s_send = order.add(s0[half:], s2_got[half:])
    s_keep = order.add(s0[:half], s2_got[:half])
    g_s = Reduce(order, s_keep, s_send, bits, "glocal")
    g_l.step()
    (output,) = order.call(output_body, (where, src, index, mid, feed, gm, go), [wide])
    dm, do = drows.result()
    input_grad, small = order.call(
        finish_body, (where, src, gains, index, x, dmid, da1, before, behind, dm, do, grad_gain2, grad_router_qk, grad_router_f),
        [wide32, ((5, width), F32)],
    )

    small = small.reshape(5, dp * tensor, -1).transpose(1, 0, 2)
    with jax.named_scope("small"):
        small = lax.all_to_all(small, ("dp", "tensor"), 0, 0)
    g_l.steps_but_last()
    g_h.step()
    g_s.step()
    g_light = g_l.result()
    g_h.steps_but_last()
    g_s.steps_but_last()
    g_hattn = g_h.result()
    g_lattn = g_s.result()
    small = jnp.sum(order(small), axis=0)

    def unflat(grad, count):
        return grad.reshape(shard, count, -1).transpose(1, 0, 2)

    return (
        output[None],
        input_grad[None],
        unflat(g_lattn[:, :c_lqkv], 3),
        g_lattn[:, c_lqkv:].T,
        unflat(g_hattn[:, : 3 * hw], 3),
        g_hattn[:, 3 * hw :].T,
        unflat(g_light[:, : 2 * c_lin], 2),
        g_light[:, 2 * c_lin :].T,
        jnp.stack([g_feed[:, :c_hin], g_feed[:, c_hin : 2 * c_hin]]),
        g_feed[:, 2 * c_hin :].T,
        small[:2],
        small[2:],
    )


def solution(mesh):
    rows = P("dp", "tensor", None)
    index = P("dp", None)
    cols = P(None, "dp", "tensor")
    back = P("tensor", "dp")
    both = P(None, ("dp", "tensor"))
    weights = (cols, back) * 4
    return jax.shard_map(
        local,
        mesh=mesh,
        in_specs=(rows, rows, P("dp"), index, index, index) + weights + (both, both),
        out_specs=(rows, rows) + weights + (both, both),
        check_vma=False,
    )
```

```python
import functools

import jax
import jax.numpy as jnp
import numpy as np
from jax import lax
from jax.experimental import pallas as pl
from jax.experimental.pallas import tpu as pltpu
from jax.sharding import PartitionSpec as P

HEAD = 64
SLOT = 2048
WINDOW = 128
ROUTED = 256
NORM_EPS = 1e-06
SCALE = 0.125
MASKED = -1e30
F32 = jnp.float32
BF16 = jnp.bfloat16


def mm(left, right, dims):
    return lax.dot_general(left, right, (dims, ((), ())), preferred_element_type=F32)


def nn(left, right):
    return mm(left, right, ((1,), (0,)))


def nt(left, right):
    return mm(left, right, ((1,), (1,)))


def tn(left, right):
    return mm(left, right, ((0,), (0,)))


def low(values):
    return values.astype(BF16)


def swap(values, axis, bit, label="swap"):
    size = lax.axis_size(axis)
    with jax.named_scope(f"{label}_{axis}{bit}"):
        return lax.ppermute(values, axis, [(i, i ^ bit) for i in range(size)])


def bits_of(axis):
    size = lax.axis_size(axis)
    return [1 << b for b in range(size.bit_length() - 1)]


def relative_order(axis):
    order = [0]
    for bit in reversed(bits_of(axis)):
        order = order + [r ^ bit for r in order]
    return order


def after(values, *others):
    return lax.optimization_barrier((values,) + others)[0]


class Order:
    def __init__(self):
        self.last = None

    def __call__(self, values):
        if self.last is None:
            return values
        return lax.optimization_barrier((values, self.last))[0]

    def call(self, body, args, outs, scratch=()):
        first = next(i for i, a in enumerate(args) if a.ndim > 1)
        args = args[:first] + (self(args[first]),) + args[first + 1 :]
        res = call(body, args, outs, scratch)
        self.last = res[0]
        return res

    def add(self, left, right, kind=BF16):
        self.last = (self(left).astype(F32) + right.astype(F32)).astype(kind)
        return self.last

    def join(self, *parts):
        self.last = jnp.concatenate((self(parts[0]),) + parts[1:], axis=0)
        return self.last


class Gather:
    def __init__(self, order, block, axis, label):
        self.order, self.axis, self.label = order, axis, label
        self.bits = list(reversed(bits_of(axis)))
        self.have = block
        self.got = swap(block, axis, self.bits[0], label)

    def step(self):
        self.bits = self.bits[1:]
        self.have = self.order.join(self.have, self.got)
        self.got = swap(self.have, self.axis, self.bits[0], self.label)

    def steps_but_last(self, kept):
        while len(self.bits) > kept:
            self.step()

    def halves(self):
        return self.have, self.got


class Reduce:
    def __init__(self, order, keep, send, bits, label):
        self.order, self.bits, self.label = order, bits, label
        self.keep, self.got = keep, swap(send, "dp", bits[0], label)

    def step(self):
        half = self.keep.shape[0] // 2
        send = self.order.add(self.keep[half:], self.got[half:], self.keep.dtype)
        self.keep = self.order.add(self.keep[:half], self.got[:half], self.keep.dtype)
        self.bits = self.bits[1:]
        self.got = swap(send, "dp", self.bits[0], self.label)

    def steps_but_last(self):
        while len(self.bits) > 1:
            self.step()

    def terms(self):
        self.steps_but_last()
        return self.keep, self.got


class TensorSum:
    def __init__(self, order, mine, other, label):
        self.order, self.mine, self.label = order, mine, label
        self.got = swap(other, "tensor", 1, label)

    def step(self):
        self.mine = self.order.add(self.mine, self.got)
        self.got = swap(self.mine, "tensor", 2, self.label)

    def result(self):
        self.mine = self.order.add(self.mine, self.got)
        return self.mine, swap(self.mine, "tensor", 1, self.label)


class PairSum:
    def __init__(self, order, values, label):
        self.order, self.values, self.label = order, values, label
        self.got = swap(values, "tensor", 1, label)

    def result(self):
        chip = self.order.add(self.values, self.got)
        return chip, swap(chip, "tensor", 2, self.label)


def neighbours(first, last):
    size = lax.axis_size("tensor")
    before = lax.ppermute(last, "tensor", [(i, i + 1) for i in range(size - 1)])
    behind = lax.ppermute(first, "tensor", [(i + 1, i) for i in range(size - 1)])
    return before, behind


VMEM = pl.BlockSpec(memory_space=pltpu.VMEM)
SMEM = pl.BlockSpec(memory_space=pltpu.SMEM)


def call(body, args, outs, scratch=()):
    return pl.pallas_call(
        body,
        in_specs=[SMEM if a.ndim == 1 else VMEM for a in args],
        out_specs=[VMEM] * len(outs),
        out_shape=[jax.ShapeDtypeStruct(shape, dtype) for shape, dtype in outs],
        scratch_shapes=scratch,
        compiler_params=pltpu.CompilerParams(vmem_limit_bytes=48 << 20),
        cost_estimate=pl.CostEstimate(flops=int(2e10), bytes_accessed=0, transcendentals=0),
    )(*args)


def mul(x, first, second):
    half = first.shape[0]
    return nn(x[:, :half], first) + nn(x[:, half:], second)


def mul_t(y, first, second):
    return jnp.concatenate([nt(y, first), nt(y, second)], axis=1)


def sigmoid(v):
    return 1.0 / (1.0 + jnp.exp(-v))


def rms(v, gain):
    return v * lax.rsqrt(jnp.mean(v * v, axis=-1, keepdims=True) + NORM_EPS) * gain


def rms_back(v, gain, grad):
    r = lax.rsqrt(jnp.mean(v * v, axis=-1, keepdims=True) + NORM_EPS)
    n = v * r
    h = grad * gain
    return r * (h - n * jnp.mean(h * n, axis=-1, keepdims=True)), jnp.sum(grad * n, axis=0, keepdims=True)


def gelu_parts(v):
    root = 0.7978845608028654
    th = jnp.tanh(root * (v + 0.044715 * v * v * v))
    value = 0.5 * v * (1.0 + th)
    slope = 0.5 * (1.0 + th) + 0.5 * v * (1.0 - th * th) * root * (1.0 + 3 * 0.044715 * v * v)
    return value, slope


def iota(shape, axis):
    return lax.broadcasted_iota(jnp.int32, shape, axis)


def ones_where(mask):
    return low(jnp.where(mask, 1.0, 0.0))


def permutation(src_ref):
    size = src_ref.shape[1]
    return ones_where(iota((size, size), 0) == src_ref[...])


def valid_rows(where_ref, rows):
    return where_ref[0] + iota((rows, 1), 0) < where_ref[1]


def pick(cols_ref, which, where_ref, rows):
    index = cols_ref[:, which : which + 1]
    return ones_where(index == where_ref[0] + iota((index.shape[0], rows), 1))


def place(rows_ref, which, where_ref, rows):
    index = rows_ref[which : which + 1, :]
    return ones_where(index == where_ref[0] + iota((rows, index.shape[1]), 0))


def core_of(where_ref):
    return where_ref[where_ref.shape[0] - 1]


def split(where_ref, values, mine_ref, other_ref, which):
    size = values.shape[0] // 2
    first = core_of(where_ref) == 0
    lower, upper = values[:size], values[size:]
    mine_ref[which] = jnp.where(first, lower, upper).astype(mine_ref.dtype)
    other_ref[which] = jnp.where(first, upper, lower).astype(other_ref.dtype)


def both(where_ref, mine_ref, other_ref, which):
    first = core_of(where_ref) == 0
    mine, other = mine_ref[which].astype(F32), other_ref[which].astype(F32)
    return jnp.concatenate([jnp.where(first, mine, other), jnp.where(first, other, mine)], axis=0)


def total(one_ref, two_ref, which=0):
    return low(one_ref[which].astype(F32) + two_ref[which].astype(F32))


def start_body(where_ref, src_ref, cols_ref, x_ref, cot_ref, xr_ref, g_ref, mine_ref, other_ref):
    rows = x_ref.shape[0]
    perm = permutation(src_ref)
    xr = low(nn(x_ref[...], perm))
    xr_ref[...] = xr
    g = low(jnp.where(valid_rows(where_ref, rows), nn(cot_ref[...], perm), 0.0))
    g_ref[...] = g
    for which, values in enumerate((xr, xr, g)):
        split(where_ref, nn(pick(cols_ref, which, where_ref, rows), values), mine_ref, other_ref, which)


def norm_body(src_ref, gains_ref, before_ref, x_ref, after_ref, a1_ref, out_ref):
    edge, rows = before_ref.shape[0], x_ref.shape[0]
    perm = permutation(src_ref)
    gains = nn(low(gains_ref[...]), perm)
    out_ref[...] = gains
    gain = gains[0:1, :]
    a1_ref[0:edge, :] = low(rms(nn(before_ref[...], perm), gain))
    a1_ref[edge : edge + rows, :] = low(rms(x_ref[...].astype(F32), gain))
    a1_ref[edge + rows :, :] = low(rms(nn(after_ref[...], perm), gain))


def lane_masks(width):
    lane = iota((1, width), 1) // HEAD
    return [(lane == h).astype(F32) for h in range(width // HEAD)]


def stack_heads(values, masks):
    return jnp.concatenate([values * m.astype(values.dtype) for m in masks], axis=0)


def join_heads(values, masks):
    size = values.shape[0] // len(masks)
    return sum(values[h * size : (h + 1) * size] * m for h, m in enumerate(masks))


def band(i, where_ref):
    start, length = where_ref[0], where_ref[1]
    shape = (2 * WINDOW, 3 * WINDOW)
    q_off = iota(shape, 0) % WINDOW
    k_off = iota(shape, 1)
    q_pos = start + i * WINDOW + q_off
    k_pos = start + (i - 1) * WINDOW + k_off
    ahead = k_off - q_off
    near = (ahead >= 1) & (ahead <= 2 * WINDOW - 1)
    inside = (k_pos >= 0) & (k_pos < SLOT)
    return near & inside & ((k_pos < length) | (q_pos >= length))


def local_forward_body(where_ref, a1_ref, c_ref, d_ref, qkv_ref, lo_ref, lse_ref):
    qkv_ref[...] = low(mul(a1_ref[...], c_ref[:, :384], d_ref[:, :384]))
    masks = lane_masks(2 * HEAD)

    for i in range(lo_ref.shape[0] // WINDOW):
        base = i * WINDOW
        q = qkv_ref[pl.ds(base + WINDOW, WINDOW), 0:128]
        k = qkv_ref[pl.ds(base, 3 * WINDOW), 128:256]
        v = qkv_ref[pl.ds(base, 3 * WINDOW), 256:384]
        s = nt(stack_heads(q, masks), k) * SCALE
        s = jnp.where(band(i, where_ref), s, MASKED)
        top = jnp.max(s, axis=-1, keepdims=True)
        e = jnp.exp(s - top)
        total = jnp.sum(e, axis=-1, keepdims=True)
        o = nn(low(e / total), v)
        lo_ref[pl.ds(base, WINDOW), :] = low(join_heads(o, masks))
        lse_ref[pl.ds(base, WINDOW), :] = join_heads(top + jnp.log(total), masks)


def local_backward_body(count, where_ref, g_ref, a1_ref, *refs):
    per = 5
    ins = [refs[i * per : (i + 1) * per] for i in range(count)]
    outs = [refs[count * per + i * 3 : count * per + (i + 1) * 3] for i in range(count)]
    dkv_acc, dlo_ref = refs[count * (per + 3) :]
    rows = g_ref.shape[0]
    masks = lane_masks(2 * HEAD)
    for (qkv_ref, lo_ref, lse_ref, c_ref, d_ref), (dq_ref, dkv_ref, grad_ref) in zip(ins, outs):
        dlo_ref[...] = low(mul(g_ref[...], c_ref[:, 384:], d_ref[:, 384:]))
        dkv_acc[...] = jnp.zeros_like(dkv_acc)

        for i in range(rows // WINDOW):
            base = i * WINDOW
            q = stack_heads(qkv_ref[pl.ds(base + WINDOW, WINDOW), 0:128], masks)
            k = qkv_ref[pl.ds(base, 3 * WINDOW), 128:256]
            v = qkv_ref[pl.ds(base, 3 * WINDOW), 256:384]
            g = stack_heads(dlo_ref[pl.ds(base, WINDOW), :], masks)
            lse = lse_ref[pl.ds(base, WINDOW), :]
            lse = jnp.concatenate([lse[:, 0:1], lse[:, HEAD : HEAD + 1]], axis=0)
            s = jnp.where(band(i, where_ref), nt(q, k) * SCALE, MASKED)
            p = jnp.exp(s - lse)
            dp = nt(g, v)
            ds = low(p * (dp - jnp.sum(p * dp, axis=-1, keepdims=True)))
            dq_ref[pl.ds(base, WINDOW), :] = low(join_heads(nn(ds, k), masks) * SCALE)
            dkv_acc[pl.ds(base, 3 * WINDOW), 0:128] += tn(ds, q) * SCALE
            dkv_acc[pl.ds(base, 3 * WINDOW), 128:256] += tn(low(p), g)

        dkv_ref[...] = low(dkv_acc[...])
        grad_ref[:, 0:128] = low(tn(a1_ref[WINDOW : WINDOW + rows, :], dq_ref[...]))
        grad_ref[:, 128:384] = low(tn(a1_ref[...], dkv_ref[...]))
        grad_ref[:, 384:512] = low(tn(g_ref[...], lo_ref[...]))


def local_input_body(count, *refs):
    ins = [refs[i * 4 : (i + 1) * 4] for i in range(count)]
    da1_ref, first_ref, last_ref = refs[count * 4 :]
    rows, edge = da1_ref.shape[0], first_ref.shape[0]
    half = ins[0][2].shape[0]
    dkv = jnp.concatenate([r[1][...] for r in ins], axis=1)
    dq = jnp.concatenate([r[0][...] for r in ins], axis=1)
    for side in range(2):
        cut = slice(side * half, (side + 1) * half)
        w_kv = jnp.concatenate([r[2 + side][:, 128:384] for r in ins], axis=1)
        w_q = jnp.concatenate([r[2 + side][:, 0:128] for r in ins], axis=1)
        part = nt(dkv, w_kv)
        first_ref[:, cut] = low(part[:edge])
        da1_ref[:, cut] = part[edge : edge + rows] + nt(dq, w_q)
        last_ref[:, cut] = low(part[edge + rows :])


def ordered(where_ref, w_ref, cut):
    return jnp.concatenate([w_ref[where_ref[2 + r], :, cut] for r in range(w_ref.shape[0])], axis=0)


def light_feed_body(first, where_ref, *refs):
    if first:
        a2_ref, g_ref, *refs = refs
    else:
        a2_ref, g_ref, feed_in, da2_in, *refs = refs
    *weights, feed_ref, da2_ref, grad0_ref, grad1_ref = refs
    hidden = weights[0].shape[2] // 3
    feed = da2 = None
    a2, g = a2_ref[...], g_ref[...]
    for w_ref, grad_ref in zip(weights, (grad0_ref, grad1_ref)):
        w_in = ordered(where_ref, w_ref, slice(0, 2 * hidden))
        w_down = ordered(where_ref, w_ref, slice(2 * hidden, 3 * hidden))
        gu = nn(a2, w_in)
        up = gu[:, hidden:]
        value, slope = gelu_parts(gu[:, :hidden])
        lh = low(value * up)
        dlh = low(nn(g, w_down)).astype(F32)
        dgu = jnp.concatenate([low(dlh * up * slope), low(dlh * value)], axis=1)
        new_feed = nt(lh, w_down)
        new_da2 = nt(dgu, w_in)
        feed = new_feed if feed is None else feed + new_feed
        da2 = new_da2 if da2 is None else da2 + new_da2
        grad_ref[:, : 2 * hidden] = low(tn(a2, dgu))
        grad_ref[:, 2 * hidden :] = low(tn(g, lh))
    if first:
        feed_ref[...] = feed
        da2_ref[...] = da2
    else:
        feed_ref[...] = feed_in[...] + feed
        da2_ref[...] = da2_in[...] + da2


def heavy_feed_body(
    where_ref, gains_ref, one_ref, two_ref, picked_ref, other_ref, w_ref,
    drows_ref, back_ref, drouter_ref, grad_ref
):
    blocks, shard, cols = w_ref.shape
    hidden = cols // 3
    step = min(hidden, 256)
    f = total(one_ref, two_ref)
    f32 = f.astype(F32)
    router = gains_ref[4:5, :]
    sf = scores(f, router)
    g32 = both(where_ref, picked_ref, other_ref, 2)
    tf = low(sf * g32)
    hf = daf = None
    for j in range(hidden // step):
        cuts = [slice(i * hidden + j * step, i * hidden + (j + 1) * step) for i in range(3)]
        w_gate, w_up, w_down = [ordered(where_ref, w_ref, cut) for cut in cuts]
        up = nn(f, w_up)
        value, slope = gelu_parts(nn(f, w_gate))
        hh = low(value * up)
        dhh = low(nn(tf, w_down)).astype(F32)
        dgate, dup = low(dhh * up * slope), low(dhh * value)
        new_hf = nt(hh, w_down)
        new_daf = nt(dgate, w_gate) + nt(dup, w_up)
        hf = new_hf if hf is None else hf + new_hf
        daf = new_daf if daf is None else daf + new_daf
        for x, dy, cut in zip((f, f, tf), (dgate, dup, hh), cuts):
            grad = low(tn(x, dy))
            for r in range(blocks):
                grad_ref[where_ref[2 + r], :, cut] = grad[r * shard : (r + 1) * shard]
    back_ref[0] = low(sf * hf)
    wf = jnp.sum(g32 * hf, axis=-1, keepdims=True) * sf * (1.0 - sf)
    drows_ref[0] = low(daf + wf * router)
    drouter_ref[...] = jnp.sum(wf * f32, axis=0, keepdims=True)


def scores(rows, router):
    return sigmoid(jnp.sum(rows.astype(F32) * router, axis=-1, keepdims=True))


def heavy_forward_body(
    where_ref, gains_ref, mine_ref, other_ref, c_ref, d_ref,
    rows_ref, hqkv_ref, ho_ref, lse_ref, hy_ref, back_ref
):
    width = c_ref.shape[1] // 4
    masks = lane_masks(width)
    gain = gains_ref[0:1, :]
    q_rows = low(rms(both(where_ref, mine_ref, other_ref, 0), gain))
    k_rows = low(rms(both(where_ref, mine_ref, other_ref, 1), gain))
    sq = scores(q_rows, gains_ref[2:3, :])
    kvin = low(scores(k_rows, gains_ref[3:4, :]) * k_rows.astype(F32))
    rows_ref[0] = q_rows
    rows_ref[1] = k_rows
    rows_ref[2] = kvin
    hq = low(mul(q_rows, c_ref[:, 0:width], d_ref[:, 0:width]))
    hk = low(mul(kvin, c_ref[:, width : 2 * width], d_ref[:, width : 2 * width]))
    hv = low(mul(kvin, c_ref[:, 2 * width : 3 * width], d_ref[:, 2 * width : 3 * width]))
    hqkv_ref[0] = hq
    hqkv_ref[1] = hk
    hqkv_ref[2] = hv
    s = nt(stack_heads(hq, masks), hk) * SCALE
    top = jnp.max(s, axis=-1, keepdims=True)
    e = jnp.exp(s - top)
    total = jnp.sum(e, axis=-1, keepdims=True)
    ho = low(join_heads(nn(low(e / total), hv), masks))
    ho_ref[...] = ho
    lse_ref[...] = join_heads(top + jnp.log(total), masks)
    hy = mul_t(ho, c_ref[:, 3 * width :], d_ref[:, 3 * width :])
    hy_ref[...] = hy
    back_ref[0] = low(sq * hy)


def heavy_backward_body(
    where_ref, gains_ref, gm_ref, go_ref, hy_ref, rows_ref, hqkv_ref, ho_ref, lse_ref, c_ref, d_ref,
    dm_ref, do_ref, keep_ref, send_ref, drouter_ref
):
    width, half = c_ref.shape[1] // 4, c_ref.shape[0]
    masks = lane_masks(width)
    q_rows, k_rows, kvin = rows_ref[0], rows_ref[1], rows_ref[2]
    q32, k32 = q_rows.astype(F32), k_rows.astype(F32)
    sq = scores(q_rows, gains_ref[2:3, :])
    sk = scores(k_rows, gains_ref[3:4, :])
    ga = total(gm_ref, go_ref).astype(F32)
    dsq = jnp.sum(ga * hy_ref[...], axis=-1, keepdims=True)
    tq = low(sq * ga)
    cuts = [slice(i * width, (i + 1) * width) for i in range(4)]
    dho = low(mul(tq, c_ref[:, cuts[3]], d_ref[:, cuts[3]]))
    q3 = stack_heads(hqkv_ref[0], masks)
    hk, hv = hqkv_ref[1], hqkv_ref[2]
    g3 = stack_heads(dho, masks)
    lse = lse_ref[...]
    lse3 = jnp.concatenate([lse[:, h * HEAD : h * HEAD + 1] for h in range(len(masks))], axis=0)
    p = jnp.exp(nt(q3, hk) * SCALE - lse3)
    dp = nt(g3, hv)
    ds = low(p * (dp - jnp.sum(p * dp, axis=-1, keepdims=True)))
    dhq = low(join_heads(nn(ds, hk), masks) * SCALE)
    dhk = low(tn(ds, q3) * SCALE)
    dhv = low(tn(low(p), g3))
    dkv = mul_t(dhk, c_ref[:, cuts[1]], d_ref[:, cuts[1]]) + mul_t(dhv, c_ref[:, cuts[2]], d_ref[:, cuts[2]])
    wq = dsq * sq * (1.0 - sq)
    wk = jnp.sum(dkv * k32, axis=-1, keepdims=True) * sk * (1.0 - sk)
    split(where_ref, mul_t(dhq, c_ref[:, cuts[0]], d_ref[:, cuts[0]]) + wq * gains_ref[2:3, :], dm_ref, do_ref, 0)
    split(where_ref, sk * dkv + wk * gains_ref[3:4, :], dm_ref, do_ref, 1)
    drouter_ref[0:1, :] = jnp.sum(wq * q32, axis=0, keepdims=True)
    drouter_ref[1:2, :] = jnp.sum(wk * k32, axis=0, keepdims=True)
    for cut, x, dy in zip(cuts, (q_rows, kvin, kvin, tq), (dhq, dhk, dhv, ho_ref[...])):
        keep_ref[:, cut] = low(tn(x[:, :half], dy))
        send_ref[:, cut] = low(tn(x[:, half:], dy))


def middle_body(where_ref, gains_ref, cols_ref, rows_ref, x_ref, rm_ref, ro_ref, *refs):
    ins = [refs[i * 3 : (i + 1) * 3] for i in range(4)]
    mid_ref, a2_ref, picked_ref = refs[12:]
    rows = x_ref.shape[0]
    lo = jnp.concatenate([r[0][...] for r in ins], axis=1)
    c = jnp.concatenate([r[1][:, 384:] for r in ins], axis=1)
    d = jnp.concatenate([r[2][:, 384:] for r in ins], axis=1)
    attn = mul_t(lo, c, d) + nn(place(rows_ref, 0, where_ref, rows), total(rm_ref, ro_ref))
    mid = x_ref[...].astype(F32) + jnp.where(valid_rows(where_ref, rows), attn, 0.0)
    mid_ref[...] = mid
    a2 = low(rms(mid, gains_ref[1:2, :]))
    a2_ref[...] = a2
    picked_ref[0] = low(nn(pick(cols_ref, 2, where_ref, rows), a2))


def output_body(where_ref, src_ref, rows_ref, mid_ref, feed_ref, gm_ref, go_ref, out_ref):
    rows = mid_ref.shape[0]
    feed = feed_ref[...] + nn(place(rows_ref, 2, where_ref, rows), total(gm_ref, go_ref))
    out = low(mid_ref[...] + jnp.where(valid_rows(where_ref, rows), feed, 0.0))
    out_ref[...] = low(nt(out, permutation(src_ref)))


def turn_body(
    where_ref, gains_ref, cols_ref, rows_ref, mid_ref, da2_ref, g_ref, am_ref, ao_ref,
    dmid_ref, gattn_ref, dgain_ref, picked_ref
):
    rows = mid_ref.shape[0]
    da2 = da2_ref[...] + nn(place(rows_ref, 2, where_ref, rows), total(am_ref, ao_ref))
    back, dgain_ref[...] = rms_back(mid_ref[...], gains_ref[1:2, :], da2)
    dmid = g_ref[...].astype(F32) + back
    dmid_ref[...] = dmid
    gattn = low(jnp.where(valid_rows(where_ref, rows), dmid, 0.0))
    gattn_ref[...] = gattn
    picked_ref[0] = low(nn(pick(cols_ref, 0, where_ref, rows), gattn))


def unpermute(values, perm):
    one = low(values)
    rest = values - one.astype(F32)
    two = low(rest)
    three = low(rest - two.astype(F32))
    return nt(one, perm) + nt(two, perm) + nt(three, perm)


def finish_body(
    where_ref, src_ref, gains_ref, rows_ref, x_ref, dmid_ref, da1_ref, before_ref, after_ref,
    dm_ref, do_ref, dgain2_ref, dqk_ref, drf_ref, grad_ref, small_ref
):
    rows, edge = x_ref.shape[0], before_ref.shape[0]
    da1 = da1_ref[...] + nn(place(rows_ref, 0, where_ref, rows), low(both(where_ref, dm_ref, do_ref, 0)))
    da1 = da1 + nn(place(rows_ref, 1, where_ref, rows), low(both(where_ref, dm_ref, do_ref, 1)))
    da1 = jnp.concatenate(
        [
            da1[:edge] + before_ref[...].astype(F32),
            da1[edge : rows - edge],
            da1[rows - edge :] + after_ref[...].astype(F32),
        ],
        axis=0,
    )
    back, dgain1 = rms_back(x_ref[...].astype(F32), gains_ref[0:1, :], da1)
    perm = permutation(src_ref)
    grad_ref[...] = unpermute(dmid_ref[...] + back, perm)
    small = jnp.concatenate([dgain1, dgain2_ref[...], dqk_ref[...], drf_ref[...]], axis=0)
    small_ref[...] = unpermute(small, perm)


def weights_body(*refs):
    *terms, out_ref, back_ref = refs
    count, cols = out_ref.shape[0], out_ref.shape[2]
    grad = terms[0][...].astype(F32)
    for term in terms[1:]:
        grad = grad + term[...].astype(F32)
    for i in range(count):
        out_ref[i] = grad[:, i * cols : (i + 1) * cols]
    back_ref[...] = grad[:, count * cols :].T


def local(
    inputs, cotangent, lengths, query_index, key_index, token_index,
    light_qkv, light_out, heavy_qkv, heavy_out, light_in, light_down, heavy_in, heavy_down,
    norm_gains, routers,
):
    rows, width = inputs.shape[1], inputs.shape[2]
    extent = rows + 2 * WINDOW
    shard, half = light_qkv.shape[1], width // 2
    dp, tensor = lax.axis_size("dp"), lax.axis_size("tensor")
    dp_index, tensor_index = lax.axis_index("dp"), lax.axis_index("tensor")
    c_lqkv, c_lout = 3 * light_qkv.shape[2], light_out.shape[0]
    c_lin, c_ldown, c_hin = light_in.shape[2], light_down.shape[0], heavy_in.shape[2]
    hw = heavy_out.shape[0]
    blocks = np.array(relative_order("dp"), np.int32)
    place_of = np.arange(width, dtype=np.int32)
    src = ((dp_index ^ blocks[place_of // shard]) * shard + place_of % shard)[None].astype(jnp.int32)
    where = jnp.concatenate(
        [jnp.stack([tensor_index * rows, lengths[0]]), dp_index ^ blocks, (tensor_index & 1)[None]]
    ).astype(jnp.int32)
    index = jnp.concatenate([query_index, key_index, token_index], axis=0)
    index_cols = index.T

    order = Order()
    rows1, rows2 = [((n, ROUTED, width), BF16) for n in (1, 2)]
    halves2, halves3 = [((n, ROUTED // 2, width), BF16) for n in (2, 3)]
    wide = ((rows, width), BF16)
    wide32 = ((rows, width), F32)
    gain_row = ((1, width), F32)

    def flat(w):
        return w.transpose(1, 0, 2).reshape(shard, -1)

    own = inputs[0]
    light_piece = jnp.concatenate([flat(light_in), light_down.T], axis=1)
    light_w = lax.all_gather(light_piece, "dp", axis=0)
    order.last = light_piece
    local_piece = jnp.concatenate([order(flat(light_qkv)), light_out.T], axis=1)
    local_w = Gather(order, local_piece, "dp", "local")
    order.last = local_piece
    feed_piece = jnp.concatenate([heavy_in[0], heavy_in[1], heavy_down.T], axis=1)
    x, gfeed, picked, other = order.call(
        start_body, (where, src, index_cols, own, cotangent[0]), [wide, wide, halves3, halves3]
    )
    picks = TensorSum(order, picked, other, "picked")
    small = order(jnp.concatenate([norm_gains, routers], axis=0))
    small = jnp.broadcast_to(small[None], (dp * tensor,) + small.shape)
    with jax.named_scope("gains"):
        small = lax.all_to_all(small, ("dp", "tensor"), 0, 0)
    gains = small.transpose(1, 0, 2).reshape(5, width)
    edges = order(own)
    before, behind = neighbours(edges[:WINDOW], edges[rows - WINDOW :])
    heavy_piece = order(jnp.concatenate([flat(heavy_qkv), heavy_out.T], axis=1))
    local_w.step()
    feed_w = lax.all_gather(after(feed_piece, local_w.have), "dp", axis=0)
    heavy_w = Gather(order, order(heavy_piece), "dp", "heavy")
    local_w.steps_but_last(1)
    local_first, local_second = local_w.halves()
    picks.step()
    gains = order(gains)
    order.last = gains = gains.astype(F32)
    heavy_w.step()

    def across(first, second, bit, label):
        return swap(first, "tensor", bit, label), swap(second, "tensor", bit, label)

    a1, gains = order.call(
        norm_body, (src, gains, before, x, behind), [((extent, width), BF16), ((5, width), F32)]
    )

    def local_forward(pair):
        return order.call(
            local_forward_body, (where, a1) + pair,
            [((extent, c_lqkv), BF16), ((rows, c_lout), BF16), ((rows, c_lout), F32)],
        )

    w0 = (local_first, local_second)
    w2, w1 = across(*w0, 2, "local"), across(*w0, 1, "local")
    head0 = local_forward(w0)
    heavy_w.steps_but_last(1)
    heavy_w = heavy_w.halves()
    head1 = local_forward(w1)
    picked, other = picks.result()
    w3 = across(*w2, 1, "local")
    head2 = local_forward(w2)
    routed, hqkv, ho, hlse, hy, back = order.call(
        heavy_forward_body, (where, gains, picked, other) + heavy_w,
        [((3, ROUTED, width), BF16), ((3, ROUTED, hw), BF16), ((ROUTED, hw), BF16), ((ROUTED, hw), F32),
         ((ROUTED, width), F32), rows1],
    )
    routed_sum = PairSum(order, back, "routed")
    rm, ro = routed_sum.result()
    head3 = local_forward(w3)
    heads = (head0, head1, head2, head3)
    local_w = (w0, w1, w2, w3)
    l0 = light_w
    l1 = swap(l0, "tensor", 1, "light")
    l2 = swap(after(l0, ro), "tensor", 2, "light")
    mid, a2, am = order.call(
        middle_body,
        (where, gains, index_cols, index, x, rm, ro) + sum(((h[1],) + w for h, w in zip(heads, local_w)), ()),
        [wide32, wide, rows1],
    )

    tokens = PairSum(order, am, "tokens")

    def light_feed(done, *weights):
        return order.call(
            functools.partial(light_feed_body, not done), (where, a2, gfeed) + done + weights,
            [wide32, wide32] + [((width, 3 * c_lin), BF16)] * 2,
        )

    feed, da2, g_l0, g_l1 = light_feed((), l0, l1)
    l1_got = swap(g_l1, "tensor", 1, "glight")
    am, ao = tokens.result()
    bits = bits_of("dp")
    drows, back, grad_router_f, g_feed = order.call(
        heavy_feed_body, (where, gains, am, ao, picked, other, feed_w),
        [rows1, rows1, gain_row, ((dp, shard, 3 * c_hin), BF16)],
    )
    g_feed = lax.psum_scatter(g_feed, "dp", scatter_dimension=0)
    dtokens = PairSum(order, drows, "dtokens")
    l3 = swap(after(l2, drows), "tensor", 1, "light")
    dm, do = dtokens.result()
    feed, da2, g_l2, g_l3 = light_feed((feed, da2), l2, l3)
    l3_got = swap(g_l3, "tensor", 1, "glight")
    dmid, gattn, grad_gain2, ga = order.call(
        turn_body, (where, gains, index_cols, index, mid, da2, gfeed, dm, do), [wide32, wide, gain_row, rows1]
    )

    dattn = PairSum(order, ga, "dattn")
    g_l0 = order.add(g_l0, l1_got)
    g_l2 = order.add(g_l2, l3_got)
    l2_got = swap(after(g_l2, ga), "tensor", 2, "glight")

    def local_backward(which):
        args = sum((tuple(heads[i]) + local_w[i] for i in which), ())
        outs = [((rows, c_lout), BF16), ((extent, 2 * c_lout), BF16), ((width, c_lqkv + c_lout), BF16)]
        res = order.call(
            functools.partial(local_backward_body, len(which)), (where, gattn, a1) + args, outs * len(which),
            scratch=[pltpu.VMEM((extent, 2 * c_lout), F32), pltpu.VMEM((rows, c_lout), BF16)],
        )
        return [res[3 * i : 3 * i + 3] for i in range(len(which))]

    (back3,) = local_backward((3,))
    s3_got = swap(back3[2], "tensor", 1, "glocal")
    gm, go = dattn.result()
    (back1,) = local_backward((1,))
    s1_got = swap(back1[2], "tensor", 1, "glocal")
    (back2,) = local_backward((2,))
    s2 = order.add(back2[2], s3_got)
    s2_got = swap(s2, "tensor", 2, "glocal")
    dm, do, h_keep, h_send, grad_router_qk = order.call(
        heavy_backward_body, (where, gains, gm, go, hy, routed, hqkv, ho, hlse) + heavy_w,
        [halves2] * 2 + [((half, 4 * hw), BF16)] * 2 + [((2, width), F32)],
    )
    drows = TensorSum(order, dm, do, "drows")
    g_h = Reduce(order, h_keep, h_send, bits, "gheavy")
    (back0,) = local_backward((0,))
    drows.step()
    s0 = order.add(back0[2], s1_got)
    da1, first, last = order.call(
        functools.partial(local_input_body, tensor),
        sum(((b[0], b[1]) + w for b, w in zip((back0, back1, back2, back3), local_w)), ()),
        [wide32, ((WINDOW, width), BF16), ((WINDOW, width), BF16)],
    )
    before, behind = neighbours(first, last)
    l_send = order.add(g_l0[half:], l2_got[half:])
    l_keep = order.add(g_l0[:half], l2_got[:half])
    g_l = Reduce(order, l_keep, l_send, bits, "glight")
    dm, do = drows.result()
    g_h.step()
    s_send = order.add(s0[half:], s2_got[half:])
    s_keep = order.add(s0[:half], s2_got[:half])
    g_s = Reduce(order, s_keep, s_send, bits, "glocal")
    input_grad, small = order.call(
        finish_body, (where, src, gains, index, x, dmid, da1, before, behind, dm, do, grad_gain2, grad_router_qk, grad_router_f),
        [wide32, ((5, width), F32)],
    )
    small = small.reshape(5, dp * tensor, -1).transpose(1, 0, 2)
    with jax.named_scope("small"):
        small = lax.all_to_all(small, ("dp", "tensor"), 0, 0)

    def as_weights(terms, count, cols, back_rows):
        return order.call(weights_body, terms, [((count, shard, cols), F32), ((back_rows, shard), F32)])

    g_l.step()
    back_sum = PairSum(order, order(back), "back")
    g_h.steps_but_last()
    g_s.step()
    back = back_sum.result()
    g_l.steps_but_last()
    (output,) = order.call(output_body, (where, src, index, mid, feed) + back, [wide])
    heavy_grads = as_weights(g_h.terms(), 3, hw, hw)
    g_s.steps_but_last()
    light_grads = as_weights(g_l.terms(), 2, c_lin, c_ldown)
    feed_grads = as_weights((g_feed,), 2, c_hin, c_hin)
    local_grads = as_weights(g_s.terms(), 3, c_lout, c_lout)
    small = jnp.sum(order(small), axis=0)

    return (
        output[None],
        input_grad[None],
        *local_grads,
        *heavy_grads,
        *light_grads,
        *feed_grads,
        small[:2],
        small[2:],
    )


def solution(mesh):
    rows = P("dp", "tensor", None)
    index = P("dp", None)
    cols = P(None, "dp", "tensor")
    back = P("tensor", "dp")
    both = P(None, ("dp", "tensor"))
    weights = (cols, back) * 4
    return jax.shard_map(
        local,
        mesh=mesh,
        in_specs=(rows, rows, P("dp"), index, index, index) + weights + (both, both),
        out_specs=(rows, rows) + weights + (both, both),
        check_vma=False,
    )
```

```python
import functools

import jax
import jax.numpy as jnp
import numpy as np
from jax import lax
from jax.experimental import pallas as pl
from jax.experimental.pallas import tpu as pltpu
from jax.sharding import PartitionSpec as P

HEAD = 64
SLOT = 2048
WINDOW = 128
ROUTED = 256
NORM_EPS = 1e-06
SCALE = 0.125
MASKED = -1e30
F32 = jnp.float32
BF16 = jnp.bfloat16


def mm(left, right, dims):
    return lax.dot_general(left, right, (dims, ((), ())), preferred_element_type=F32)


def nn(left, right):
    return mm(left, right, ((1,), (0,)))


def nt(left, right):
    return mm(left, right, ((1,), (1,)))


def tn(left, right):
    return mm(left, right, ((0,), (0,)))


def low(values):
    return values.astype(BF16)


def swap(values, axis, bit, label="swap"):
    size = lax.axis_size(axis)
    with jax.named_scope(f"{label}_{axis}{bit}"):
        return lax.ppermute(values, axis, [(i, i ^ bit) for i in range(size)])


def bits_of(axis):
    size = lax.axis_size(axis)
    return [1 << b for b in range(size.bit_length() - 1)]


def relative_order(axis):
    order = [0]
    for bit in reversed(bits_of(axis)):
        order = order + [r ^ bit for r in order]
    return order


def after(values, *others):
    return lax.optimization_barrier((values,) + others)[0]


class Order:
    def __init__(self):
        self.last = None

    def __call__(self, values):
        if self.last is None:
            return values
        return lax.optimization_barrier((values, self.last))[0]

    def call(self, body, args, outs, scratch=()):
        first = next(i for i, a in enumerate(args) if a.ndim > 1)
        args = args[:first] + (self(args[first]),) + args[first + 1 :]
        res = call(body, args, outs, scratch)
        self.last = res[0]
        return res

    def add(self, left, right, kind=BF16):
        self.last = (self(left).astype(F32) + right.astype(F32)).astype(kind)
        return self.last

    def join(self, *parts):
        self.last = jnp.concatenate((self(parts[0]),) + parts[1:], axis=0)
        return self.last


class Gather:
    def __init__(self, order, block, axis, label):
        self.order, self.axis, self.label = order, axis, label
        self.bits = list(reversed(bits_of(axis)))
        self.have = block
        self.got = swap(block, axis, self.bits[0], label)

    def step(self):
        self.bits = self.bits[1:]
        self.have = self.order.join(self.have, self.got)
        self.got = swap(self.have, self.axis, self.bits[0], self.label)

    def steps_but_last(self, kept):
        while len(self.bits) > kept:
            self.step()

    def halves(self):
        return self.have, self.got


class Reduce:
    def __init__(self, order, keep, send, bits, label):
        self.order, self.bits, self.label = order, bits, label
        self.keep, self.got = keep, swap(send, "dp", bits[0], label)

    def step(self):
        half = self.keep.shape[0] // 2
        send = self.order.add(self.keep[half:], self.got[half:], self.keep.dtype)
        self.keep = self.order.add(self.keep[:half], self.got[:half], self.keep.dtype)
        self.bits = self.bits[1:]
        self.got = swap(send, "dp", self.bits[0], self.label)

    def steps_but_last(self):
        while len(self.bits) > 1:
            self.step()

    def terms(self):
        self.steps_but_last()
        return self.keep, self.got


class TensorSum:
    def __init__(self, order, mine, other, label):
        self.order, self.mine, self.label = order, mine, label
        self.got = swap(other, "tensor", 1, label)

    def step(self):
        self.mine = self.order.add(self.mine, self.got)
        self.got = swap(self.mine, "tensor", 2, self.label)

    def result(self):
        self.mine = self.order.add(self.mine, self.got)
        return self.mine, swap(self.mine, "tensor", 1, self.label)


class PairSum:
    def __init__(self, order, values, label):
        self.order, self.values, self.label = order, values, label
        self.got = swap(values, "tensor", 1, label)

    def result(self):
        chip = self.order.add(self.values, self.got)
        return chip, swap(chip, "tensor", 2, self.label)


def neighbours(first, last):
    size = lax.axis_size("tensor")
    before = lax.ppermute(last, "tensor", [(i, i + 1) for i in range(size - 1)])
    behind = lax.ppermute(first, "tensor", [(i + 1, i) for i in range(size - 1)])
    return before, behind


COST = {"local_forward_body": 20, "heavy_forward_body": 20, "middle_body": 20, "light_feed_body": 20, "heavy_feed_body": 20, "turn_body": 20, "local_backward_body": 20, "heavy_backward_body": 20, "local_input_body": 20, "finish_body": 20, "start_body": 20, "norm_body": 20, "output_body": 20, "weights_body": 20}

VMEM = pl.BlockSpec(memory_space=pltpu.VMEM)
SMEM = pl.BlockSpec(memory_space=pltpu.SMEM)


def call(body, args, outs, scratch=()):
    return pl.pallas_call(
        body,
        in_specs=[SMEM if a.ndim == 1 else VMEM for a in args],
        out_specs=[VMEM] * len(outs),
        out_shape=[jax.ShapeDtypeStruct(shape, dtype) for shape, dtype in outs],
        scratch_shapes=scratch,
        compiler_params=pltpu.CompilerParams(vmem_limit_bytes=48 << 20),
        cost_estimate=pl.CostEstimate(flops=int(COST.get(getattr(body, "func", body).__name__, 20) * 1e9), bytes_accessed=0, transcendentals=0),
    )(*args)


def mul(x, first, second):
    half = first.shape[0]
    return nn(x[:, :half], first) + nn(x[:, half:], second)


def mul_t(y, first, second):
    return jnp.concatenate([nt(y, first), nt(y, second)], axis=1)


def sigmoid(v):
    return 1.0 / (1.0 + jnp.exp(-v))


def rms(v, gain):
    return v * lax.rsqrt(jnp.mean(v * v, axis=-1, keepdims=True) + NORM_EPS) * gain


def rms_back(v, gain, grad):
    r = lax.rsqrt(jnp.mean(v * v, axis=-1, keepdims=True) + NORM_EPS)
    n = v * r
    h = grad * gain
    return r * (h - n * jnp.mean(h * n, axis=-1, keepdims=True)), jnp.sum(grad * n, axis=0, keepdims=True)


def gelu_parts(v):
    root = 0.7978845608028654
    th = jnp.tanh(root * (v + 0.044715 * v * v * v))
    value = 0.5 * v * (1.0 + th)
    slope = 0.5 * (1.0 + th) + 0.5 * v * (1.0 - th * th) * root * (1.0 + 3 * 0.044715 * v * v)
    return value, slope


def iota(shape, axis):
    return lax.broadcasted_iota(jnp.int32, shape, axis)


def ones_where(mask):
    return low(jnp.where(mask, 1.0, 0.0))


def permutation(src_ref):
    size = src_ref.shape[1]
    return ones_where(iota((size, size), 0) == src_ref[...])


def valid_rows(where_ref, rows):
    return where_ref[0] + iota((rows, 1), 0) < where_ref[1]


def pick(cols_ref, which, where_ref, rows):
    index = cols_ref[:, which : which + 1]
    return ones_where(index == where_ref[0] + iota((index.shape[0], rows), 1))


def place(rows_ref, which, where_ref, rows):
    index = rows_ref[which : which + 1, :]
    return ones_where(index == where_ref[0] + iota((rows, index.shape[1]), 0))


def core_of(where_ref):
    return where_ref[where_ref.shape[0] - 1]


def split(where_ref, values, mine_ref, other_ref, which):
    size = values.shape[0] // 2
    first = core_of(where_ref) == 0
    lower, upper = values[:size], values[size:]
    mine_ref[which] = jnp.where(first, lower, upper).astype(mine_ref.dtype)
    other_ref[which] = jnp.where(first, upper, lower).astype(other_ref.dtype)


def both(where_ref, mine_ref, other_ref, which):
    first = core_of(where_ref) == 0
    mine, other = mine_ref[which].astype(F32), other_ref[which].astype(F32)
    return jnp.concatenate([jnp.where(first, mine, other), jnp.where(first, other, mine)], axis=0)


def total(one_ref, two_ref, which=0):
    return low(one_ref[which].astype(F32) + two_ref[which].astype(F32))


def start_body(where_ref, src_ref, cols_ref, x_ref, cot_ref, xr_ref, g_ref, mine_ref, other_ref):
    rows = x_ref.shape[0]
    perm = permutation(src_ref)
    xr = low(nn(x_ref[...], perm))
    xr_ref[...] = xr
    g = low(jnp.where(valid_rows(where_ref, rows), nn(cot_ref[...], perm), 0.0))
    g_ref[...] = g
    for which, values in enumerate((xr, xr, g)):
        split(where_ref, nn(pick(cols_ref, which, where_ref, rows), values), mine_ref, other_ref, which)


def norm_body(src_ref, gains_ref, before_ref, x_ref, after_ref, a1_ref, out_ref):
    edge, rows = before_ref.shape[0], x_ref.shape[0]
    perm = permutation(src_ref)
    gains = nn(low(gains_ref[...]), perm)
    out_ref[...] = gains
    gain = gains[0:1, :]
    a1_ref[0:edge, :] = low(rms(nn(before_ref[...], perm), gain))
    a1_ref[edge : edge + rows, :] = low(rms(x_ref[...].astype(F32), gain))
    a1_ref[edge + rows :, :] = low(rms(nn(after_ref[...], perm), gain))


def lane_masks(width):
    lane = iota((1, width), 1) // HEAD
    return [(lane == h).astype(F32) for h in range(width // HEAD)]


def stack_heads(values, masks):
    return jnp.concatenate([values * m.astype(values.dtype) for m in masks], axis=0)


def join_heads(values, masks):
    size = values.shape[0] // len(masks)
    return sum(values[h * size : (h + 1) * size] * m for h, m in enumerate(masks))


def band(i, where_ref):
    start, length = where_ref[0], where_ref[1]
    shape = (2 * WINDOW, 3 * WINDOW)
    q_off = iota(shape, 0) % WINDOW
    k_off = iota(shape, 1)
    q_pos = start + i * WINDOW + q_off
    k_pos = start + (i - 1) * WINDOW + k_off
    ahead = k_off - q_off
    near = (ahead >= 1) & (ahead <= 2 * WINDOW - 1)
    inside = (k_pos >= 0) & (k_pos < SLOT)
    return near & inside & ((k_pos < length) | (q_pos >= length))


def local_forward_body(where_ref, a1_ref, c_ref, d_ref, qkv_ref, lo_ref, lse_ref):
    qkv_ref[...] = low(mul(a1_ref[...], c_ref[:, :384], d_ref[:, :384]))
    masks = lane_masks(2 * HEAD)

    for i in range(lo_ref.shape[0] // WINDOW):
        base = i * WINDOW
        q = qkv_ref[pl.ds(base + WINDOW, WINDOW), 0:128]
        k = qkv_ref[pl.ds(base, 3 * WINDOW), 128:256]
        v = qkv_ref[pl.ds(base, 3 * WINDOW), 256:384]
        s = nt(stack_heads(q, masks), k) * SCALE
        s = jnp.where(band(i, where_ref), s, MASKED)
        top = jnp.max(s, axis=-1, keepdims=True)
        e = jnp.exp(s - top)
        total = jnp.sum(e, axis=-1, keepdims=True)
        o = nn(low(e / total), v)
        lo_ref[pl.ds(base, WINDOW), :] = low(join_heads(o, masks))
        lse_ref[pl.ds(base, WINDOW), :] = join_heads(top + jnp.log(total), masks)


def local_backward_body(count, where_ref, g_ref, a1_ref, *refs):
    per = 5
    ins = [refs[i * per : (i + 1) * per] for i in range(count)]
    outs = [refs[count * per + i * 3 : count * per + (i + 1) * 3] for i in range(count)]
    dkv_acc, dlo_ref = refs[count * (per + 3) :]
    rows = g_ref.shape[0]
    masks = lane_masks(2 * HEAD)
    for (qkv_ref, lo_ref, lse_ref, c_ref, d_ref), (dq_ref, dkv_ref, grad_ref) in zip(ins, outs):
        dlo_ref[...] = low(mul(g_ref[...], c_ref[:, 384:], d_ref[:, 384:]))
        dkv_acc[...] = jnp.zeros_like(dkv_acc)

        for i in range(rows // WINDOW):
            base = i * WINDOW
            q = stack_heads(qkv_ref[pl.ds(base + WINDOW, WINDOW), 0:128], masks)
            k = qkv_ref[pl.ds(base, 3 * WINDOW), 128:256]
            v = qkv_ref[pl.ds(base, 3 * WINDOW), 256:384]
            g = stack_heads(dlo_ref[pl.ds(base, WINDOW), :], masks)
            lse = lse_ref[pl.ds(base, WINDOW), :]
            lse = jnp.concatenate([lse[:, 0:1], lse[:, HEAD : HEAD + 1]], axis=0)
            s = jnp.where(band(i, where_ref), nt(q, k) * SCALE, MASKED)
            p = jnp.exp(s - lse)
            dp = nt(g, v)
            ds = low(p * (dp - jnp.sum(p * dp, axis=-1, keepdims=True)))
            dq_ref[pl.ds(base, WINDOW), :] = low(join_heads(nn(ds, k), masks) * SCALE)
            dkv_acc[pl.ds(base, 3 * WINDOW), 0:128] += tn(ds, q) * SCALE
            dkv_acc[pl.ds(base, 3 * WINDOW), 128:256] += tn(low(p), g)

        dkv_ref[...] = low(dkv_acc[...])
        grad_ref[:, 0:128] = low(tn(a1_ref[WINDOW : WINDOW + rows, :], dq_ref[...]))
        grad_ref[:, 128:384] = low(tn(a1_ref[...], dkv_ref[...]))
        grad_ref[:, 384:512] = low(tn(g_ref[...], lo_ref[...]))


def local_input_body(count, *refs):
    ins = [refs[i * 4 : (i + 1) * 4] for i in range(count)]
    da1_ref, first_ref, last_ref = refs[count * 4 :]
    rows, edge = da1_ref.shape[0], first_ref.shape[0]
    half = ins[0][2].shape[0]
    dkv = jnp.concatenate([r[1][...] for r in ins], axis=1)
    dq = jnp.concatenate([r[0][...] for r in ins], axis=1)
    for side in range(2):
        cut = slice(side * half, (side + 1) * half)
        w_kv = jnp.concatenate([r[2 + side][:, 128:384] for r in ins], axis=1)
        w_q = jnp.concatenate([r[2 + side][:, 0:128] for r in ins], axis=1)
        part = nt(dkv, w_kv)
        first_ref[:, cut] = low(part[:edge])
        da1_ref[:, cut] = part[edge : edge + rows] + nt(dq, w_q)
        last_ref[:, cut] = low(part[edge + rows :])


def ordered(where_ref, w_ref, cut):
    return jnp.concatenate([w_ref[where_ref[2 + r], :, cut] for r in range(w_ref.shape[0])], axis=0)


def light_feed_body(first, where_ref, *refs):
    if first:
        a2_ref, g_ref, *refs = refs
    else:
        a2_ref, g_ref, feed_in, da2_in, *refs = refs
    *weights, feed_ref, da2_ref, grad0_ref, grad1_ref = refs
    hidden = weights[0].shape[2] // 3
    feed = da2 = None
    a2, g = a2_ref[...], g_ref[...]
    for w_ref, grad_ref in zip(weights, (grad0_ref, grad1_ref)):
        w_in = ordered(where_ref, w_ref, slice(0, 2 * hidden))
        w_down = ordered(where_ref, w_ref, slice(2 * hidden, 3 * hidden))
        gu = nn(a2, w_in)
        up = gu[:, hidden:]
        value, slope = gelu_parts(gu[:, :hidden])
        lh = low(value * up)
        dlh = low(nn(g, w_down)).astype(F32)
        dgu = jnp.concatenate([low(dlh * up * slope), low(dlh * value)], axis=1)
        new_feed = nt(lh, w_down)
        new_da2 = nt(dgu, w_in)
        feed = new_feed if feed is None else feed + new_feed
        da2 = new_da2 if da2 is None else da2 + new_da2
        grad_ref[:, : 2 * hidden] = low(tn(a2, dgu))
        grad_ref[:, 2 * hidden :] = low(tn(g, lh))
    if first:
        feed_ref[...] = feed
        da2_ref[...] = da2
    else:
        feed_ref[...] = feed_in[...] + feed
        da2_ref[...] = da2_in[...] + da2


def heavy_feed_body(
    where_ref, gains_ref, one_ref, two_ref, picked_ref, other_ref, w_ref,
    drows_ref, back_ref, drouter_ref, grad_ref
):
    blocks, shard, cols = w_ref.shape
    hidden = cols // 3
    step = min(hidden, 256)
    f = total(one_ref, two_ref)
    f32 = f.astype(F32)
    router = gains_ref[4:5, :]
    sf = scores(f, router)
    g32 = both(where_ref, picked_ref, other_ref, 2)
    tf = low(sf * g32)
    hf = daf = None
    for j in range(hidden // step):
        cuts = [slice(i * hidden + j * step, i * hidden + (j + 1) * step) for i in range(3)]
        w_gate, w_up, w_down = [ordered(where_ref, w_ref, cut) for cut in cuts]
        up = nn(f, w_up)
        value, slope = gelu_parts(nn(f, w_gate))
        hh = low(value * up)
        dhh = low(nn(tf, w_down)).astype(F32)
        dgate, dup = low(dhh * up * slope), low(dhh * value)
        new_hf = nt(hh, w_down)
        new_daf = nt(dgate, w_gate) + nt(dup, w_up)
        hf = new_hf if hf is None else hf + new_hf
        daf = new_daf if daf is None else daf + new_daf
        for x, dy, cut in zip((f, f, tf), (dgate, dup, hh), cuts):
            grad = low(tn(x, dy))
            for r in range(blocks):
                grad_ref[where_ref[2 + r], :, cut] = grad[r * shard : (r + 1) * shard]
    back_ref[0] = low(sf * hf)
    wf = jnp.sum(g32 * hf, axis=-1, keepdims=True) * sf * (1.0 - sf)
    drows_ref[0] = low(daf + wf * router)
    drouter_ref[...] = jnp.sum(wf * f32, axis=0, keepdims=True)


def scores(rows, router):
    return sigmoid(jnp.sum(rows.astype(F32) * router, axis=-1, keepdims=True))


def heavy_forward_body(
    where_ref, gains_ref, mine_ref, other_ref, c_ref, d_ref,
    rows_ref, hqkv_ref, ho_ref, lse_ref, hy_ref, back_ref
):
    width = c_ref.shape[1] // 4
    masks = lane_masks(width)
    gain = gains_ref[0:1, :]
    q_rows = low(rms(both(where_ref, mine_ref, other_ref, 0), gain))
    k_rows = low(rms(both(where_ref, mine_ref, other_ref, 1), gain))
    sq = scores(q_rows, gains_ref[2:3, :])
    kvin = low(scores(k_rows, gains_ref[3:4, :]) * k_rows.astype(F32))
    rows_ref[0] = q_rows
    rows_ref[1] = k_rows
    rows_ref[2] = kvin
    hq = low(mul(q_rows, c_ref[:, 0:width], d_ref[:, 0:width]))
    hk = low(mul(kvin, c_ref[:, width : 2 * width], d_ref[:, width : 2 * width]))
    hv = low(mul(kvin, c_ref[:, 2 * width : 3 * width], d_ref[:, 2 * width : 3 * width]))
    hqkv_ref[0] = hq
    hqkv_ref[1] = hk
    hqkv_ref[2] = hv
    s = nt(stack_heads(hq, masks), hk) * SCALE
    top = jnp.max(s, axis=-1, keepdims=True)
    e = jnp.exp(s - top)
    total = jnp.sum(e, axis=-1, keepdims=True)
    ho = low(join_heads(nn(low(e / total), hv), masks))
    ho_ref[...] = ho
    lse_ref[...] = join_heads(top + jnp.log(total), masks)
    hy = mul_t(ho, c_ref[:, 3 * width :], d_ref[:, 3 * width :])
    hy_ref[...] = hy
    back_ref[0] = low(sq * hy)


def heavy_backward_body(
    where_ref, gains_ref, gm_ref, go_ref, hy_ref, rows_ref, hqkv_ref, ho_ref, lse_ref, c_ref, d_ref,
    dm_ref, do_ref, keep_ref, send_ref, drouter_ref
):
    width, half = c_ref.shape[1] // 4, c_ref.shape[0]
    masks = lane_masks(width)
    q_rows, k_rows, kvin = rows_ref[0], rows_ref[1], rows_ref[2]
    q32, k32 = q_rows.astype(F32), k_rows.astype(F32)
    sq = scores(q_rows, gains_ref[2:3, :])
    sk = scores(k_rows, gains_ref[3:4, :])
    ga = total(gm_ref, go_ref).astype(F32)
    dsq = jnp.sum(ga * hy_ref[...], axis=-1, keepdims=True)
    tq = low(sq * ga)
    cuts = [slice(i * width, (i + 1) * width) for i in range(4)]
    dho = low(mul(tq, c_ref[:, cuts[3]], d_ref[:, cuts[3]]))
    q3 = stack_heads(hqkv_ref[0], masks)
    hk, hv = hqkv_ref[1], hqkv_ref[2]
    g3 = stack_heads(dho, masks)
    lse = lse_ref[...]
    lse3 = jnp.concatenate([lse[:, h * HEAD : h * HEAD + 1] for h in range(len(masks))], axis=0)
    p = jnp.exp(nt(q3, hk) * SCALE - lse3)
    dp = nt(g3, hv)
    ds = low(p * (dp - jnp.sum(p * dp, axis=-1, keepdims=True)))
    dhq = low(join_heads(nn(ds, hk), masks) * SCALE)
    dhk = low(tn(ds, q3) * SCALE)
    dhv = low(tn(low(p), g3))
    dkv = mul_t(dhk, c_ref[:, cuts[1]], d_ref[:, cuts[1]]) + mul_t(dhv, c_ref[:, cuts[2]], d_ref[:, cuts[2]])
    wq = dsq * sq * (1.0 - sq)
    wk = jnp.sum(dkv * k32, axis=-1, keepdims=True) * sk * (1.0 - sk)
    split(where_ref, mul_t(dhq, c_ref[:, cuts[0]], d_ref[:, cuts[0]]) + wq * gains_ref[2:3, :], dm_ref, do_ref, 0)
    split(where_ref, sk * dkv + wk * gains_ref[3:4, :], dm_ref, do_ref, 1)
    drouter_ref[0:1, :] = jnp.sum(wq * q32, axis=0, keepdims=True)
    drouter_ref[1:2, :] = jnp.sum(wk * k32, axis=0, keepdims=True)
    for cut, x, dy in zip(cuts, (q_rows, kvin, kvin, tq), (dhq, dhk, dhv, ho_ref[...])):
        keep_ref[:, cut] = low(tn(x[:, :half], dy))
        send_ref[:, cut] = low(tn(x[:, half:], dy))


def middle_body(where_ref, gains_ref, cols_ref, rows_ref, x_ref, rm_ref, ro_ref, *refs):
    ins = [refs[i * 3 : (i + 1) * 3] for i in range(4)]
    mid_ref, a2_ref, picked_ref = refs[12:]
    rows = x_ref.shape[0]
    lo = jnp.concatenate([r[0][...] for r in ins], axis=1)
    c = jnp.concatenate([r[1][:, 384:] for r in ins], axis=1)
    d = jnp.concatenate([r[2][:, 384:] for r in ins], axis=1)
    attn = mul_t(lo, c, d) + nn(place(rows_ref, 0, where_ref, rows), total(rm_ref, ro_ref))
    mid = x_ref[...].astype(F32) + jnp.where(valid_rows(where_ref, rows), attn, 0.0)
    mid_ref[...] = mid
    a2 = low(rms(mid, gains_ref[1:2, :]))
    a2_ref[...] = a2
    picked_ref[0] = low(nn(pick(cols_ref, 2, where_ref, rows), a2))


def output_body(where_ref, src_ref, rows_ref, mid_ref, feed_ref, gm_ref, go_ref, out_ref):
    rows = mid_ref.shape[0]
    feed = feed_ref[...] + nn(place(rows_ref, 2, where_ref, rows), total(gm_ref, go_ref))
    out = low(mid_ref[...] + jnp.where(valid_rows(where_ref, rows), feed, 0.0))
    out_ref[...] = low(nt(out, permutation(src_ref)))


def turn_body(
    where_ref, gains_ref, cols_ref, rows_ref, mid_ref, da2_ref, g_ref, am_ref, ao_ref,
    dmid_ref, gattn_ref, dgain_ref, picked_ref
):
    rows = mid_ref.shape[0]
    da2 = da2_ref[...] + nn(place(rows_ref, 2, where_ref, rows), total(am_ref, ao_ref))
    back, dgain_ref[...] = rms_back(mid_ref[...], gains_ref[1:2, :], da2)
    dmid = g_ref[...].astype(F32) + back
    dmid_ref[...] = dmid
    gattn = low(jnp.where(valid_rows(where_ref, rows), dmid, 0.0))
    gattn_ref[...] = gattn
    picked_ref[0] = low(nn(pick(cols_ref, 0, where_ref, rows), gattn))


def unpermute(values, perm):
    one = low(values)
    rest = values - one.astype(F32)
    two = low(rest)
    three = low(rest - two.astype(F32))
    return nt(one, perm) + nt(two, perm) + nt(three, perm)


def finish_body(
    where_ref, src_ref, gains_ref, rows_ref, x_ref, dmid_ref, da1_ref, before_ref, after_ref,
    dm_ref, do_ref, dgain2_ref, dqk_ref, drf_ref, grad_ref, small_ref
):
    rows, edge = x_ref.shape[0], before_ref.shape[0]
    da1 = da1_ref[...] + nn(place(rows_ref, 0, where_ref, rows), low(both(where_ref, dm_ref, do_ref, 0)))
    da1 = da1 + nn(place(rows_ref, 1, where_ref, rows), low(both(where_ref, dm_ref, do_ref, 1)))
    da1 = jnp.concatenate(
        [
            da1[:edge] + before_ref[...].astype(F32),
            da1[edge : rows - edge],
            da1[rows - edge :] + after_ref[...].astype(F32),
        ],
        axis=0,
    )
    back, dgain1 = rms_back(x_ref[...].astype(F32), gains_ref[0:1, :], da1)
    perm = permutation(src_ref)
    grad_ref[...] = unpermute(dmid_ref[...] + back, perm)
    small = jnp.concatenate([dgain1, dgain2_ref[...], dqk_ref[...], drf_ref[...]], axis=0)
    small_ref[...] = unpermute(small, perm)


def weights_body(*refs):
    *terms, out_ref, back_ref = refs
    count, cols = out_ref.shape[0], out_ref.shape[2]
    grad = terms[0][...].astype(F32)
    for term in terms[1:]:
        grad = grad + term[...].astype(F32)
    for i in range(count):
        out_ref[i] = grad[:, i * cols : (i + 1) * cols]
    back_ref[...] = grad[:, count * cols :].T


def local(
    inputs, cotangent, lengths, query_index, key_index, token_index,
    light_qkv, light_out, heavy_qkv, heavy_out, light_in, light_down, heavy_in, heavy_down,
    norm_gains, routers,
):
    rows, width = inputs.shape[1], inputs.shape[2]
    extent = rows + 2 * WINDOW
    shard, half = light_qkv.shape[1], width // 2
    dp, tensor = lax.axis_size("dp"), lax.axis_size("tensor")
    dp_index, tensor_index = lax.axis_index("dp"), lax.axis_index("tensor")
    c_lqkv, c_lout = 3 * light_qkv.shape[2], light_out.shape[0]
    c_lin, c_ldown, c_hin = light_in.shape[2], light_down.shape[0], heavy_in.shape[2]
    hw = heavy_out.shape[0]
    blocks = np.array(relative_order("dp"), np.int32)
    place_of = np.arange(width, dtype=np.int32)
    src = ((dp_index ^ blocks[place_of // shard]) * shard + place_of % shard)[None].astype(jnp.int32)
    where = jnp.concatenate(
        [jnp.stack([tensor_index * rows, lengths[0]]), dp_index ^ blocks, (tensor_index & 1)[None]]
    ).astype(jnp.int32)
    index = jnp.concatenate([query_index, key_index, token_index], axis=0)
    index_cols = index.T

    order = Order()
    rows1, rows2 = [((n, ROUTED, width), BF16) for n in (1, 2)]
    halves2, halves3 = [((n, ROUTED // 2, width), BF16) for n in (2, 3)]
    wide = ((rows, width), BF16)
    wide32 = ((rows, width), F32)
    gain_row = ((1, width), F32)

    def flat(w):
        return w.transpose(1, 0, 2).reshape(shard, -1)

    own = inputs[0]
    light_piece = jnp.concatenate([flat(light_in), light_down.T], axis=1)
    light_w = lax.all_gather(light_piece, "dp", axis=0)
    order.last = light_piece
    local_piece = jnp.concatenate([order(flat(light_qkv)), light_out.T], axis=1)
    local_w = Gather(order, local_piece, "dp", "local")
    order.last = local_piece
    feed_piece = jnp.concatenate([heavy_in[0], heavy_in[1], heavy_down.T], axis=1)
    x, gfeed, picked, other = order.call(
        start_body, (where, src, index_cols, own, cotangent[0]), [wide, wide, halves3, halves3]
    )
    picks = TensorSum(order, picked, other, "picked")
    small = order(jnp.concatenate([norm_gains, routers], axis=0))
    small = jnp.broadcast_to(small[None], (dp * tensor,) + small.shape)
    with jax.named_scope("gains"):
        small = lax.all_to_all(small, ("dp", "tensor"), 0, 0)
    gains = small.transpose(1, 0, 2).reshape(5, width)
    edges = order(own)
    before, behind = neighbours(edges[:WINDOW], edges[rows - WINDOW :])
    heavy_piece = order(jnp.concatenate([flat(heavy_qkv), heavy_out.T], axis=1))
    local_w.step()
    feed_w = lax.all_gather(after(feed_piece, local_w.have), "dp", axis=0)
    heavy_w = Gather(order, order(heavy_piece), "dp", "heavy")
    local_w.steps_but_last(1)
    local_first, local_second = local_w.halves()
    picks.step()
    gains = order(gains)
    order.last = gains = gains.astype(F32)
    heavy_w.step()

    def across(first, second, bit, label):
        return swap(first, "tensor", bit, label), swap(second, "tensor", bit, label)

    a1, gains = order.call(
        norm_body, (src, gains, before, x, behind), [((extent, width), BF16), ((5, width), F32)]
    )

    def local_forward(pair):
        return order.call(
            local_forward_body, (where, a1) + pair,
            [((extent, c_lqkv), BF16), ((rows, c_lout), BF16), ((rows, c_lout), F32)],
        )

    w0 = (local_first, local_second)
    w2, w1 = across(*w0, 2, "local"), across(*w0, 1, "local")
    head0 = local_forward(w0)
    heavy_w.steps_but_last(1)
    heavy_w = heavy_w.halves()
    head1 = local_forward(w1)
    picked, other = picks.result()
    w3 = across(*w2, 1, "local")
    head2 = local_forward(w2)
    routed, hqkv, ho, hlse, hy, back = order.call(
        heavy_forward_body, (where, gains, picked, other) + heavy_w,
        [((3, ROUTED, width), BF16), ((3, ROUTED, hw), BF16), ((ROUTED, hw), BF16), ((ROUTED, hw), F32),
         ((ROUTED, width), F32), rows1],
    )
    routed_sum = PairSum(order, back, "routed")
    rm, ro = routed_sum.result()
    head3 = local_forward(w3)
    heads = (head0, head1, head2, head3)
    local_w = (w0, w1, w2, w3)
    l0 = light_w
    l1 = swap(l0, "tensor", 1, "light")
    l2 = swap(after(l0, ro), "tensor", 2, "light")
    mid, a2, am = order.call(
        middle_body,
        (where, gains, index_cols, index, x, rm, ro) + sum(((h[1],) + w for h, w in zip(heads, local_w)), ()),
        [wide32, wide, rows1],
    )

    tokens = PairSum(order, am, "tokens")

    def light_feed(done, *weights):
        return order.call(
            functools.partial(light_feed_body, not done), (where, a2, gfeed) + done + weights,
            [wide32, wide32] + [((width, 3 * c_lin), BF16)] * 2,
        )

    feed, da2, g_l0, g_l1 = light_feed((), l0, l1)
    l1_got = swap(g_l1, "tensor", 1, "glight")
    am, ao = tokens.result()
    bits = bits_of("dp")
    drows, back, grad_router_f, g_feed = order.call(
        heavy_feed_body, (where, gains, am, ao, picked, other, feed_w),
        [rows1, rows1, gain_row, ((dp, shard, 3 * c_hin), BF16)],
    )
    g_feed = lax.psum_scatter(g_feed, "dp", scatter_dimension=0)
    dtokens = PairSum(order, drows, "dtokens")
    l3 = swap(after(l2, drows), "tensor", 1, "light")
    dm, do = dtokens.result()
    feed, da2, g_l2, g_l3 = light_feed((feed, da2), l2, l3)
    l3_got = swap(g_l3, "tensor", 1, "glight")
    dmid, gattn, grad_gain2, ga = order.call(
        turn_body, (where, gains, index_cols, index, mid, da2, gfeed, dm, do), [wide32, wide, gain_row, rows1]
    )

    dattn = PairSum(order, ga, "dattn")
    g_l0 = order.add(g_l0, l1_got)
    g_l2 = order.add(g_l2, l3_got)
    l2_got = swap(after(g_l2, ga), "tensor", 2, "glight")

    def local_backward(which):
        args = sum((tuple(heads[i]) + local_w[i] for i in which), ())
        outs = [((rows, c_lout), BF16), ((extent, 2 * c_lout), BF16), ((width, c_lqkv + c_lout), BF16)]
        res = order.call(
            functools.partial(local_backward_body, len(which)), (where, gattn, a1) + args, outs * len(which),
            scratch=[pltpu.VMEM((extent, 2 * c_lout), F32), pltpu.VMEM((rows, c_lout), BF16)],
        )
        return [res[3 * i : 3 * i + 3] for i in range(len(which))]

    (back3,) = local_backward((3,))
    s3_got = swap(back3[2], "tensor", 1, "glocal")
    gm, go = dattn.result()
    (back1,) = local_backward((1,))
    s1_got = swap(back1[2], "tensor", 1, "glocal")
    (back2,) = local_backward((2,))
    s2 = order.add(back2[2], s3_got)
    dm, do, h_keep, h_send, grad_router_qk = order.call(
        heavy_backward_body, (where, gains, gm, go, hy, routed, hqkv, ho, hlse) + heavy_w,
        [halves2] * 2 + [((half, 4 * hw), BF16)] * 2 + [((2, width), F32)],
    )
    drows = TensorSum(order, dm, do, "drows")
    g_h = Reduce(order, h_keep, h_send, bits, "gheavy")
    (back0,) = local_backward((0,))
    drows.step()
    s0 = order.add(back0[2], s1_got)
    da1, first, last = order.call(
        functools.partial(local_input_body, tensor),
        sum(((b[0], b[1]) + w for b, w in zip((back0, back1, back2, back3), local_w)), ()),
        [wide32, ((WINDOW, width), BF16), ((WINDOW, width), BF16)],
    )
    before, behind = neighbours(first, last)
    s2_got = swap(after(s2, da1), "tensor", 2, "glocal")
    dm, do = drows.result()
    l_send = order.add(g_l0[half:], l2_got[half:])
    l_keep = order.add(g_l0[:half], l2_got[:half])
    g_l = Reduce(order, l_keep, l_send, bits, "glight")
    g_h.step()
    input_grad, small = order.call(
        finish_body, (where, src, gains, index, x, dmid, da1, before, behind, dm, do, grad_gain2, grad_router_qk, grad_router_f),
        [wide32, ((5, width), F32)],
    )
    small = small.reshape(5, dp * tensor, -1).transpose(1, 0, 2)
    with jax.named_scope("small"):
        small = lax.all_to_all(small, ("dp", "tensor"), 0, 0)

    def as_weights(terms, count, cols, back_rows):
        return order.call(weights_body, terms, [((count, shard, cols), F32), ((back_rows, shard), F32)])

    s_send = order.add(s0[half:], s2_got[half:])
    s_keep = order.add(s0[:half], s2_got[:half])
    g_s = Reduce(order, s_keep, s_send, bits, "glocal")
    g_l.step()
    back_sum = PairSum(order, order(back), "back")
    g_h.steps_but_last()
    g_s.step()
    back = back_sum.result()
    g_l.steps_but_last()
    (output,) = order.call(output_body, (where, src, index, mid, feed) + back, [wide])
    heavy_grads = as_weights(g_h.terms(), 3, hw, hw)
    g_s.steps_but_last()
    light_grads = as_weights(g_l.terms(), 2, c_lin, c_ldown)
    feed_grads = as_weights((g_feed,), 2, c_hin, c_hin)
    local_grads = as_weights(g_s.terms(), 3, c_lout, c_lout)
    small = jnp.sum(order(small), axis=0)

    return (
        output[None],
        input_grad[None],
        *local_grads,
        *heavy_grads,
        *light_grads,
        *feed_grads,
        small[:2],
        small[2:],
    )


def solution(mesh):
    rows = P("dp", "tensor", None)
    index = P("dp", None)
    cols = P(None, "dp", "tensor")
    back = P("tensor", "dp")
    both = P(None, ("dp", "tensor"))
    weights = (cols, back) * 4
    return jax.shard_map(
        local,
        mesh=mesh,
        in_specs=(rows, rows, P("dp"), index, index, index) + weights + (both, both),
        out_specs=(rows, rows) + weights + (both, both),
        check_vma=False,
    )
```

```python
import functools

import jax
import jax.numpy as jnp
import numpy as np
from jax import lax
from jax.experimental import pallas as pl
from jax.experimental.pallas import tpu as pltpu
from jax.sharding import PartitionSpec as P

HEAD = 64
SLOT = 2048
WINDOW = 128
ROUTED = 256
NORM_EPS = 1e-06
SCALE = 0.125
MASKED = -1e30
F32 = jnp.float32
BF16 = jnp.bfloat16


def mm(left, right, dims):
    return lax.dot_general(left, right, (dims, ((), ())), preferred_element_type=F32)


def nn(left, right):
    return mm(left, right, ((1,), (0,)))


def nt(left, right):
    return mm(left, right, ((1,), (1,)))


def tn(left, right):
    return mm(left, right, ((0,), (0,)))


def low(values):
    return values.astype(BF16)


def swap(values, axis, bit, label="swap"):
    size = lax.axis_size(axis)
    with jax.named_scope(f"{label}_{axis}{bit}"):
        return lax.ppermute(values, axis, [(i, i ^ bit) for i in range(size)])


def bits_of(axis):
    size = lax.axis_size(axis)
    return [1 << b for b in range(size.bit_length() - 1)]


def relative_order(axis):
    order = [0]
    for bit in reversed(bits_of(axis)):
        order = order + [r ^ bit for r in order]
    return order


def after(values, *others):
    return lax.optimization_barrier((values,) + others)[0]


class Order:
    def __init__(self):
        self.last = None

    def __call__(self, values):
        if self.last is None:
            return values
        return lax.optimization_barrier((values, self.last))[0]

    def call(self, body, args, outs, scratch=()):
        first = next(i for i, a in enumerate(args) if a.ndim > 1)
        args = args[:first] + (self(args[first]),) + args[first + 1 :]
        res = call(body, args, outs, scratch)
        self.last = res[0]
        return res

    def add(self, left, right, kind=BF16):
        self.last = (self(left).astype(F32) + right.astype(F32)).astype(kind)
        return self.last

    def join(self, *parts):
        self.last = jnp.concatenate((self(parts[0]),) + parts[1:], axis=0)
        return self.last


class Gather:
    def __init__(self, order, block, axis, label):
        self.order, self.axis, self.label = order, axis, label
        self.bits = list(reversed(bits_of(axis)))
        self.have = block
        self.got = swap(block, axis, self.bits[0], label)

    def step(self):
        self.bits = self.bits[1:]
        self.have = self.order.join(self.have, self.got)
        self.got = swap(self.have, self.axis, self.bits[0], self.label)

    def steps_but_last(self, kept):
        while len(self.bits) > kept:
            self.step()

    def halves(self):
        return self.have, self.got


class Reduce:
    def __init__(self, order, keep, send, bits, label):
        self.order, self.bits, self.label = order, bits, label
        self.keep, self.got = keep, swap(send, "dp", bits[0], label)

    def step(self):
        half = self.keep.shape[0] // 2
        send = self.order.add(self.keep[half:], self.got[half:], self.keep.dtype)
        self.keep = self.order.add(self.keep[:half], self.got[:half], self.keep.dtype)
        self.bits = self.bits[1:]
        self.got = swap(send, "dp", self.bits[0], self.label)

    def steps_but_last(self):
        while len(self.bits) > 1:
            self.step()

    def terms(self):
        self.steps_but_last()
        return self.keep, self.got


class TensorSum:
    def __init__(self, order, mine, other, label):
        self.order, self.mine, self.label = order, mine, label
        self.got = swap(other, "tensor", 1, label)

    def step(self):
        self.mine = self.order.add(self.mine, self.got)
        self.got = swap(self.mine, "tensor", 2, self.label)

    def result(self):
        self.mine = self.order.add(self.mine, self.got)
        return self.mine, swap(self.mine, "tensor", 1, self.label)


class PairSum:
    def __init__(self, order, values, label):
        self.order, self.values, self.label = order, values, label
        self.got = swap(values, "tensor", 1, label)

    def result(self):
        chip = self.order.add(self.values, self.got)
        return chip, swap(chip, "tensor", 2, self.label)


def neighbours(first, last):
    size = lax.axis_size("tensor")
    before = lax.ppermute(last, "tensor", [(i, i + 1) for i in range(size - 1)])
    behind = lax.ppermute(first, "tensor", [(i + 1, i) for i in range(size - 1)])
    return before, behind


COST = {"local_forward_body": 20, "heavy_forward_body": 20, "middle_body": 20, "light_feed_body": 20, "heavy_feed_body": 20, "turn_body": 20, "local_backward_body": 20, "heavy_backward_body": 20, "local_input_body": 20, "finish_body": 20, "start_body": 5, "norm_body": 5, "output_body": 20, "weights_body": 20}

VMEM = pl.BlockSpec(memory_space=pltpu.VMEM)
SMEM = pl.BlockSpec(memory_space=pltpu.SMEM)


def call(body, args, outs, scratch=()):
    return pl.pallas_call(
        body,
        in_specs=[SMEM if a.ndim == 1 else VMEM for a in args],
        out_specs=[VMEM] * len(outs),
        out_shape=[jax.ShapeDtypeStruct(shape, dtype) for shape, dtype in outs],
        scratch_shapes=scratch,
        compiler_params=pltpu.CompilerParams(vmem_limit_bytes=48 << 20),
        cost_estimate=pl.CostEstimate(flops=int(COST.get(getattr(body, "func", body).__name__, 20) * 1e9), bytes_accessed=0, transcendentals=0),
    )(*args)


def mul(x, first, second):
    half = first.shape[0]
    return nn(x[:, :half], first) + nn(x[:, half:], second)


def mul_t(y, first, second):
    return jnp.concatenate([nt(y, first), nt(y, second)], axis=1)


def sigmoid(v):
    return 1.0 / (1.0 + jnp.exp(-v))


def rms(v, gain):
    return v * lax.rsqrt(jnp.mean(v * v, axis=-1, keepdims=True) + NORM_EPS) * gain


def rms_back(v, gain, grad):
    r = lax.rsqrt(jnp.mean(v * v, axis=-1, keepdims=True) + NORM_EPS)
    n = v * r
    h = grad * gain
    return r * (h - n * jnp.mean(h * n, axis=-1, keepdims=True)), jnp.sum(grad * n, axis=0, keepdims=True)


def gelu_parts(v):
    root = 0.7978845608028654
    th = jnp.tanh(root * (v + 0.044715 * v * v * v))
    value = 0.5 * v * (1.0 + th)
    slope = 0.5 * (1.0 + th) + 0.5 * v * (1.0 - th * th) * root * (1.0 + 3 * 0.044715 * v * v)
    return value, slope


def iota(shape, axis):
    return lax.broadcasted_iota(jnp.int32, shape, axis)


def ones_where(mask):
    return low(jnp.where(mask, 1.0, 0.0))


def permutation(src_ref):
    size = src_ref.shape[1]
    return ones_where(iota((size, size), 0) == src_ref[...])


def valid_rows(where_ref, rows):
    return where_ref[0] + iota((rows, 1), 0) < where_ref[1]


def pick(cols_ref, which, where_ref, rows):
    index = cols_ref[:, which : which + 1]
    return ones_where(index == where_ref[0] + iota((index.shape[0], rows), 1))


def place(rows_ref, which, where_ref, rows):
    index = rows_ref[which : which + 1, :]
    return ones_where(index == where_ref[0] + iota((rows, index.shape[1]), 0))


def core_of(where_ref):
    return where_ref[where_ref.shape[0] - 1]


def split(where_ref, values, mine_ref, other_ref, which):
    size = values.shape[0] // 2
    first = core_of(where_ref) == 0
    lower, upper = values[:size], values[size:]
    mine_ref[which] = jnp.where(first, lower, upper).astype(mine_ref.dtype)
    other_ref[which] = jnp.where(first, upper, lower).astype(other_ref.dtype)


def both(where_ref, mine_ref, other_ref, which):
    first = core_of(where_ref) == 0
    mine, other = mine_ref[which].astype(F32), other_ref[which].astype(F32)
    return jnp.concatenate([jnp.where(first, mine, other), jnp.where(first, other, mine)], axis=0)


def total(one_ref, two_ref, which=0):
    return low(one_ref[which].astype(F32) + two_ref[which].astype(F32))


def start_body(where_ref, src_ref, cols_ref, x_ref, cot_ref, xr_ref, g_ref, mine_ref, other_ref):
    rows = x_ref.shape[0]
    perm = permutation(src_ref)
    xr = low(nn(x_ref[...], perm))
    xr_ref[...] = xr
    g = low(jnp.where(valid_rows(where_ref, rows), nn(cot_ref[...], perm), 0.0))
    g_ref[...] = g
    for which, values in enumerate((xr, xr, g)):
        split(where_ref, nn(pick(cols_ref, which, where_ref, rows), values), mine_ref, other_ref, which)


def norm_body(src_ref, gains_ref, before_ref, x_ref, after_ref, a1_ref, out_ref):
    edge, rows = before_ref.shape[0], x_ref.shape[0]
    perm = permutation(src_ref)
    gains = nn(low(gains_ref[...]), perm)
    out_ref[...] = gains
    gain = gains[0:1, :]
    a1_ref[0:edge, :] = low(rms(nn(before_ref[...], perm), gain))
    a1_ref[edge : edge + rows, :] = low(rms(x_ref[...].astype(F32), gain))
    a1_ref[edge + rows :, :] = low(rms(nn(after_ref[...], perm), gain))


def lane_masks(width):
    lane = iota((1, width), 1) // HEAD
    return [(lane == h).astype(F32) for h in range(width // HEAD)]


def stack_heads(values, masks):
    return jnp.concatenate([values * m.astype(values.dtype) for m in masks], axis=0)


def join_heads(values, masks):
    size = values.shape[0] // len(masks)
    return sum(values[h * size : (h + 1) * size] * m for h, m in enumerate(masks))


def band(i, where_ref):
    start, length = where_ref[0], where_ref[1]
    shape = (2 * WINDOW, 3 * WINDOW)
    q_off = iota(shape, 0) % WINDOW
    k_off = iota(shape, 1)
    q_pos = start + i * WINDOW + q_off
    k_pos = start + (i - 1) * WINDOW + k_off
    ahead = k_off - q_off
    near = (ahead >= 1) & (ahead <= 2 * WINDOW - 1)
    inside = (k_pos >= 0) & (k_pos < SLOT)
    return near & inside & ((k_pos < length) | (q_pos >= length))


def local_forward_body(where_ref, a1_ref, c_ref, d_ref, qkv_ref, lo_ref, lse_ref):
    qkv_ref[...] = low(mul(a1_ref[...], c_ref[:, :384], d_ref[:, :384]))
    masks = lane_masks(2 * HEAD)

    for i in range(lo_ref.shape[0] // WINDOW):
        base = i * WINDOW
        q = qkv_ref[pl.ds(base + WINDOW, WINDOW), 0:128]
        k = qkv_ref[pl.ds(base, 3 * WINDOW), 128:256]
        v = qkv_ref[pl.ds(base, 3 * WINDOW), 256:384]
        s = nt(stack_heads(q, masks), k) * SCALE
        s = jnp.where(band(i, where_ref), s, MASKED)
        top = jnp.max(s, axis=-1, keepdims=True)
        e = jnp.exp(s - top)
        total = jnp.sum(e, axis=-1, keepdims=True)
        o = nn(low(e / total), v)
        lo_ref[pl.ds(base, WINDOW), :] = low(join_heads(o, masks))
        lse_ref[pl.ds(base, WINDOW), :] = join_heads(top + jnp.log(total), masks)


def local_backward_body(count, where_ref, g_ref, a1_ref, *refs):
    per = 5
    ins = [refs[i * per : (i + 1) * per] for i in range(count)]
    outs = [refs[count * per + i * 3 : count * per + (i + 1) * 3] for i in range(count)]
    dkv_acc, dlo_ref = refs[count * (per + 3) :]
    rows = g_ref.shape[0]
    masks = lane_masks(2 * HEAD)
    for (qkv_ref, lo_ref, lse_ref, c_ref, d_ref), (dq_ref, dkv_ref, grad_ref) in zip(ins, outs):
        dlo_ref[...] = low(mul(g_ref[...], c_ref[:, 384:], d_ref[:, 384:]))
        dkv_acc[...] = jnp.zeros_like(dkv_acc)

        for i in range(rows // WINDOW):
            base = i * WINDOW
            q = stack_heads(qkv_ref[pl.ds(base + WINDOW, WINDOW), 0:128], masks)
            k = qkv_ref[pl.ds(base, 3 * WINDOW), 128:256]
            v = qkv_ref[pl.ds(base, 3 * WINDOW), 256:384]
            g = stack_heads(dlo_ref[pl.ds(base, WINDOW), :], masks)
            lse = lse_ref[pl.ds(base, WINDOW), :]
            lse = jnp.concatenate([lse[:, 0:1], lse[:, HEAD : HEAD + 1]], axis=0)
            s = jnp.where(band(i, where_ref), nt(q, k) * SCALE, MASKED)
            p = jnp.exp(s - lse)
            dp = nt(g, v)
            ds = low(p * (dp - jnp.sum(p * dp, axis=-1, keepdims=True)))
            dq_ref[pl.ds(base, WINDOW), :] = low(join_heads(nn(ds, k), masks) * SCALE)
            dkv_acc[pl.ds(base, 3 * WINDOW), 0:128] += tn(ds, q) * SCALE
            dkv_acc[pl.ds(base, 3 * WINDOW), 128:256] += tn(low(p), g)

        dkv_ref[...] = low(dkv_acc[...])
        grad_ref[:, 0:128] = low(tn(a1_ref[WINDOW : WINDOW + rows, :], dq_ref[...]))
        grad_ref[:, 128:384] = low(tn(a1_ref[...], dkv_ref[...]))
        grad_ref[:, 384:512] = low(tn(g_ref[...], lo_ref[...]))


def local_input_body(count, *refs):
    ins = [refs[i * 4 : (i + 1) * 4] for i in range(count)]
    da1_ref, first_ref, last_ref = refs[count * 4 :]
    rows, edge = da1_ref.shape[0], first_ref.shape[0]
    half = ins[0][2].shape[0]
    dkv = jnp.concatenate([r[1][...] for r in ins], axis=1)
    dq = jnp.concatenate([r[0][...] for r in ins], axis=1)
    for side in range(2):
        cut = slice(side * half, (side + 1) * half)
        w_kv = jnp.concatenate([r[2 + side][:, 128:384] for r in ins], axis=1)
        w_q = jnp.concatenate([r[2 + side][:, 0:128] for r in ins], axis=1)
        part = nt(dkv, w_kv)
        first_ref[:, cut] = low(part[:edge])
        da1_ref[:, cut] = part[edge : edge + rows] + nt(dq, w_q)
        last_ref[:, cut] = low(part[edge + rows :])


def ordered(where_ref, w_ref, cut):
    return jnp.concatenate([w_ref[where_ref[2 + r], :, cut] for r in range(w_ref.shape[0])], axis=0)


def light_feed_body(first, where_ref, *refs):
    if first:
        a2_ref, g_ref, *refs = refs
    else:
        a2_ref, g_ref, feed_in, da2_in, *refs = refs
    *weights, feed_ref, da2_ref, grad0_ref, grad1_ref = refs
    hidden = weights[0].shape[2] // 3
    feed = da2 = None
    a2, g = a2_ref[...], g_ref[...]
    for w_ref, grad_ref in zip(weights, (grad0_ref, grad1_ref)):
        w_in = ordered(where_ref, w_ref, slice(0, 2 * hidden))
        w_down = ordered(where_ref, w_ref, slice(2 * hidden, 3 * hidden))
        gu = nn(a2, w_in)
        up = gu[:, hidden:]
        value, slope = gelu_parts(gu[:, :hidden])
        lh = low(value * up)
        dlh = low(nn(g, w_down)).astype(F32)
        dgu = jnp.concatenate([low(dlh * up * slope), low(dlh * value)], axis=1)
        new_feed = nt(lh, w_down)
        new_da2 = nt(dgu, w_in)
        feed = new_feed if feed is None else feed + new_feed
        da2 = new_da2 if da2 is None else da2 + new_da2
        grad_ref[:, : 2 * hidden] = low(tn(a2, dgu))
        grad_ref[:, 2 * hidden :] = low(tn(g, lh))
    if first:
        feed_ref[...] = feed
        da2_ref[...] = da2
    else:
        feed_ref[...] = feed_in[...] + feed
        da2_ref[...] = da2_in[...] + da2


def heavy_feed_body(
    where_ref, gains_ref, one_ref, two_ref, picked_ref, other_ref, w_ref,
    drows_ref, back_ref, drouter_ref, grad_ref
):
    blocks, shard, cols = w_ref.shape
    hidden = cols // 3
    step = min(hidden, 256)
    f = total(one_ref, two_ref)
    f32 = f.astype(F32)
    router = gains_ref[4:5, :]
    sf = scores(f, router)
    g32 = both(where_ref, picked_ref, other_ref, 2)
    tf = low(sf * g32)
    hf = daf = None
    for j in range(hidden // step):
        cuts = [slice(i * hidden + j * step, i * hidden + (j + 1) * step) for i in range(3)]
        w_gate, w_up, w_down = [ordered(where_ref, w_ref, cut) for cut in cuts]
        up = nn(f, w_up)
        value, slope = gelu_parts(nn(f, w_gate))
        hh = low(value * up)
        dhh = low(nn(tf, w_down)).astype(F32)
        dgate, dup = low(dhh * up * slope), low(dhh * value)
        new_hf = nt(hh, w_down)
        new_daf = nt(dgate, w_gate) + nt(dup, w_up)
        hf = new_hf if hf is None else hf + new_hf
        daf = new_daf if daf is None else daf + new_daf
        for x, dy, cut in zip((f, f, tf), (dgate, dup, hh), cuts):
            grad = low(tn(x, dy))
            for r in range(blocks):
                grad_ref[where_ref[2 + r], :, cut] = grad[r * shard : (r + 1) * shard]
    back_ref[0] = low(sf * hf)
    wf = jnp.sum(g32 * hf, axis=-1, keepdims=True) * sf * (1.0 - sf)
    drows_ref[0] = low(daf + wf * router)
    drouter_ref[...] = jnp.sum(wf * f32, axis=0, keepdims=True)


def scores(rows, router):
    return sigmoid(jnp.sum(rows.astype(F32) * router, axis=-1, keepdims=True))


def heavy_forward_body(
    where_ref, gains_ref, mine_ref, other_ref, c_ref, d_ref,
    rows_ref, hqkv_ref, ho_ref, lse_ref, hy_ref, back_ref
):
    width = c_ref.shape[1] // 4
    masks = lane_masks(width)
    gain = gains_ref[0:1, :]
    q_rows = low(rms(both(where_ref, mine_ref, other_ref, 0), gain))
    k_rows = low(rms(both(where_ref, mine_ref, other_ref, 1), gain))
    sq = scores(q_rows, gains_ref[2:3, :])
    kvin = low(scores(k_rows, gains_ref[3:4, :]) * k_rows.astype(F32))
    rows_ref[0] = q_rows
    rows_ref[1] = k_rows
    rows_ref[2] = kvin
    hq = low(mul(q_rows, c_ref[:, 0:width], d_ref[:, 0:width]))
    hk = low(mul(kvin, c_ref[:, width : 2 * width], d_ref[:, width : 2 * width]))
    hv = low(mul(kvin, c_ref[:, 2 * width : 3 * width], d_ref[:, 2 * width : 3 * width]))
    hqkv_ref[0] = hq
    hqkv_ref[1] = hk
    hqkv_ref[2] = hv
    s = nt(stack_heads(hq, masks), hk) * SCALE
    top = jnp.max(s, axis=-1, keepdims=True)
    e = jnp.exp(s - top)
    total = jnp.sum(e, axis=-1, keepdims=True)
    ho = low(join_heads(nn(low(e / total), hv), masks))
    ho_ref[...] = ho
    lse_ref[...] = join_heads(top + jnp.log(total), masks)
    hy = mul_t(ho, c_ref[:, 3 * width :], d_ref[:, 3 * width :])
    hy_ref[...] = hy
    back_ref[0] = low(sq * hy)


def heavy_backward_body(
    where_ref, gains_ref, gm_ref, go_ref, hy_ref, rows_ref, hqkv_ref, ho_ref, lse_ref, c_ref, d_ref,
    dm_ref, do_ref, keep_ref, send_ref, drouter_ref
):
    width, half = c_ref.shape[1] // 4, c_ref.shape[0]
    masks = lane_masks(width)
    q_rows, k_rows, kvin = rows_ref[0], rows_ref[1], rows_ref[2]
    q32, k32 = q_rows.astype(F32), k_rows.astype(F32)
    sq = scores(q_rows, gains_ref[2:3, :])
    sk = scores(k_rows, gains_ref[3:4, :])
    ga = total(gm_ref, go_ref).astype(F32)
    dsq = jnp.sum(ga * hy_ref[...], axis=-1, keepdims=True)
    tq = low(sq * ga)
    cuts = [slice(i * width, (i + 1) * width) for i in range(4)]
    dho = low(mul(tq, c_ref[:, cuts[3]], d_ref[:, cuts[3]]))
    q3 = stack_heads(hqkv_ref[0], masks)
    hk, hv = hqkv_ref[1], hqkv_ref[2]
    g3 = stack_heads(dho, masks)
    lse = lse_ref[...]
    lse3 = jnp.concatenate([lse[:, h * HEAD : h * HEAD + 1] for h in range(len(masks))], axis=0)
    p = jnp.exp(nt(q3, hk) * SCALE - lse3)
    dp = nt(g3, hv)
    ds = low(p * (dp - jnp.sum(p * dp, axis=-1, keepdims=True)))
    dhq = low(join_heads(nn(ds, hk), masks) * SCALE)
    dhk = low(tn(ds, q3) * SCALE)
    dhv = low(tn(low(p), g3))
    dkv = mul_t(dhk, c_ref[:, cuts[1]], d_ref[:, cuts[1]]) + mul_t(dhv, c_ref[:, cuts[2]], d_ref[:, cuts[2]])
    wq = dsq * sq * (1.0 - sq)
    wk = jnp.sum(dkv * k32, axis=-1, keepdims=True) * sk * (1.0 - sk)
    split(where_ref, mul_t(dhq, c_ref[:, cuts[0]], d_ref[:, cuts[0]]) + wq * gains_ref[2:3, :], dm_ref, do_ref, 0)
    split(where_ref, sk * dkv + wk * gains_ref[3:4, :], dm_ref, do_ref, 1)
    drouter_ref[0:1, :] = jnp.sum(wq * q32, axis=0, keepdims=True)
    drouter_ref[1:2, :] = jnp.sum(wk * k32, axis=0, keepdims=True)
    for cut, x, dy in zip(cuts, (q_rows, kvin, kvin, tq), (dhq, dhk, dhv, ho_ref[...])):
        keep_ref[:, cut] = low(tn(x[:, :half], dy))
        send_ref[:, cut] = low(tn(x[:, half:], dy))


def middle_body(where_ref, gains_ref, cols_ref, rows_ref, x_ref, rm_ref, ro_ref, *refs):
    ins = [refs[i * 3 : (i + 1) * 3] for i in range(4)]
    mid_ref, a2_ref, picked_ref = refs[12:]
    rows = x_ref.shape[0]
    lo = jnp.concatenate([r[0][...] for r in ins], axis=1)
    c = jnp.concatenate([r[1][:, 384:] for r in ins], axis=1)
    d = jnp.concatenate([r[2][:, 384:] for r in ins], axis=1)
    attn = mul_t(lo, c, d) + nn(place(rows_ref, 0, where_ref, rows), total(rm_ref, ro_ref))
    mid = x_ref[...].astype(F32) + jnp.where(valid_rows(where_ref, rows), attn, 0.0)
    mid_ref[...] = mid
    a2 = low(rms(mid, gains_ref[1:2, :]))
    a2_ref[...] = a2
    picked_ref[0] = low(nn(pick(cols_ref, 2, where_ref, rows), a2))


def output_body(where_ref, src_ref, rows_ref, mid_ref, feed_ref, gm_ref, go_ref, out_ref):
    rows = mid_ref.shape[0]
    feed = feed_ref[...] + nn(place(rows_ref, 2, where_ref, rows), total(gm_ref, go_ref))
    out = low(mid_ref[...] + jnp.where(valid_rows(where_ref, rows), feed, 0.0))
    out_ref[...] = low(nt(out, permutation(src_ref)))


def turn_body(
    where_ref, gains_ref, cols_ref, rows_ref, mid_ref, da2_ref, g_ref, am_ref, ao_ref,
    dmid_ref, gattn_ref, dgain_ref, picked_ref
):
    rows = mid_ref.shape[0]
    da2 = da2_ref[...] + nn(place(rows_ref, 2, where_ref, rows), total(am_ref, ao_ref))
    back, dgain_ref[...] = rms_back(mid_ref[...], gains_ref[1:2, :], da2)
    dmid = g_ref[...].astype(F32) + back
    dmid_ref[...] = dmid
    gattn = low(jnp.where(valid_rows(where_ref, rows), dmid, 0.0))
    gattn_ref[...] = gattn
    picked_ref[0] = low(nn(pick(cols_ref, 0, where_ref, rows), gattn))


def unpermute(values, perm):
    one = low(values)
    rest = values - one.astype(F32)
    two = low(rest)
    three = low(rest - two.astype(F32))
    return nt(one, perm) + nt(two, perm) + nt(three, perm)


def finish_body(
    where_ref, src_ref, gains_ref, rows_ref, x_ref, dmid_ref, da1_ref, before_ref, after_ref,
    dm_ref, do_ref, dgain2_ref, dqk_ref, drf_ref, grad_ref, small_ref
):
    rows, edge = x_ref.shape[0], before_ref.shape[0]
    da1 = da1_ref[...] + nn(place(rows_ref, 0, where_ref, rows), low(both(where_ref, dm_ref, do_ref, 0)))
    da1 = da1 + nn(place(rows_ref, 1, where_ref, rows), low(both(where_ref, dm_ref, do_ref, 1)))
    da1 = jnp.concatenate(
        [
            da1[:edge] + before_ref[...].astype(F32),
            da1[edge : rows - edge],
            da1[rows - edge :] + after_ref[...].astype(F32),
        ],
        axis=0,
    )
    back, dgain1 = rms_back(x_ref[...].astype(F32), gains_ref[0:1, :], da1)
    perm = permutation(src_ref)
    grad_ref[...] = unpermute(dmid_ref[...] + back, perm)
    small = jnp.concatenate([dgain1, dgain2_ref[...], dqk_ref[...], drf_ref[...]], axis=0)
    small_ref[...] = unpermute(small, perm)


def weights_body(*refs):
    *terms, out_ref, back_ref = refs
    count, cols = out_ref.shape[0], out_ref.shape[2]
    grad = terms[0][...].astype(F32)
    for term in terms[1:]:
        grad = grad + term[...].astype(F32)
    for i in range(count):
        out_ref[i] = grad[:, i * cols : (i + 1) * cols]
    back_ref[...] = grad[:, count * cols :].T


def local(
    inputs, cotangent, lengths, query_index, key_index, token_index,
    light_qkv, light_out, heavy_qkv, heavy_out, light_in, light_down, heavy_in, heavy_down,
    norm_gains, routers,
):
    rows, width = inputs.shape[1], inputs.shape[2]
    extent = rows + 2 * WINDOW
    shard, half = light_qkv.shape[1], width // 2
    dp, tensor = lax.axis_size("dp"), lax.axis_size("tensor")
    dp_index, tensor_index = lax.axis_index("dp"), lax.axis_index("tensor")
    c_lqkv, c_lout = 3 * light_qkv.shape[2], light_out.shape[0]
    c_lin, c_ldown, c_hin = light_in.shape[2], light_down.shape[0], heavy_in.shape[2]
    hw = heavy_out.shape[0]
    blocks = np.array(relative_order("dp"), np.int32)
    place_of = np.arange(width, dtype=np.int32)
    src = ((dp_index ^ blocks[place_of // shard]) * shard + place_of % shard)[None].astype(jnp.int32)
    where = jnp.concatenate(
        [jnp.stack([tensor_index * rows, lengths[0]]), dp_index ^ blocks, (tensor_index & 1)[None]]
    ).astype(jnp.int32)
    index = jnp.concatenate([query_index, key_index, token_index], axis=0)
    index_cols = index.T

    order = Order()
    rows1, rows2 = [((n, ROUTED, width), BF16) for n in (1, 2)]
    halves2, halves3 = [((n, ROUTED // 2, width), BF16) for n in (2, 3)]
    wide = ((rows, width), BF16)
    wide32 = ((rows, width), F32)
    gain_row = ((1, width), F32)

    def flat(w):
        return w.transpose(1, 0, 2).reshape(shard, -1)

    own = inputs[0]
    light_piece = jnp.concatenate([flat(light_in), light_down.T], axis=1)
    light_w = lax.all_gather(light_piece, "dp", axis=0)
    order.last = light_piece
    local_piece = jnp.concatenate([order(flat(light_qkv)), light_out.T], axis=1)
    local_w = Gather(order, local_piece, "dp", "local")
    order.last = local_piece
    feed_piece = jnp.concatenate([heavy_in[0], heavy_in[1], heavy_down.T], axis=1)
    x, gfeed, picked, other = order.call(
        start_body, (where, src, index_cols, own, cotangent[0]), [wide, wide, halves3, halves3]
    )
    picks = TensorSum(order, picked, other, "picked")
    small = order(jnp.concatenate([norm_gains, routers], axis=0))
    small = jnp.broadcast_to(small[None], (dp * tensor,) + small.shape)
    with jax.named_scope("gains"):
        small = lax.all_to_all(small, ("dp", "tensor"), 0, 0)
    gains = small.transpose(1, 0, 2).reshape(5, width)
    edges = order(own)
    before, behind = neighbours(edges[:WINDOW], edges[rows - WINDOW :])
    heavy_piece = order(jnp.concatenate([flat(heavy_qkv), heavy_out.T], axis=1))
    local_w.step()
    feed_w = lax.all_gather(after(feed_piece, local_w.have), "dp", axis=0)
    heavy_w = Gather(order, order(heavy_piece), "dp", "heavy")
    local_w.steps_but_last(1)
    local_first, local_second = local_w.halves()
    picks.step()
    gains = order(gains)
    order.last = gains = gains.astype(F32)
    heavy_w.step()

    def across(first, second, bit, label):
        return swap(first, "tensor", bit, label), swap(second, "tensor", bit, label)

    a1, gains = order.call(
        norm_body, (src, gains, before, x, behind), [((extent, width), BF16), ((5, width), F32)]
    )

    def local_forward(pair):
        return order.call(
            local_forward_body, (where, a1) + pair,
            [((extent, c_lqkv), BF16), ((rows, c_lout), BF16), ((rows, c_lout), F32)],
        )

    w0 = (local_first, local_second)
    w2, w1 = across(*w0, 2, "local"), across(*w0, 1, "local")
    head0 = local_forward(w0)
    heavy_w.steps_but_last(1)
    heavy_w = heavy_w.halves()
    head1 = local_forward(w1)
    picked, other = picks.result()
    w3 = across(*w2, 1, "local")
    head2 = local_forward(w2)
    routed, hqkv, ho, hlse, hy, back = order.call(
        heavy_forward_body, (where, gains, picked, other) + heavy_w,
        [((3, ROUTED, width), BF16), ((3, ROUTED, hw), BF16), ((ROUTED, hw), BF16), ((ROUTED, hw), F32),
         ((ROUTED, width), F32), rows1],
    )
    routed_sum = PairSum(order, back, "routed")
    rm, ro = routed_sum.result()
    head3 = local_forward(w3)
    heads = (head0, head1, head2, head3)
    local_w = (w0, w1, w2, w3)
    l0 = light_w
    l1 = swap(l0, "tensor", 1, "light")
    l2 = swap(after(l0, ro), "tensor", 2, "light")
    mid, a2, am = order.call(
        middle_body,
        (where, gains, index_cols, index, x, rm, ro) + sum(((h[1],) + w for h, w in zip(heads, local_w)), ()),
        [wide32, wide, rows1],
    )

    tokens = PairSum(order, am, "tokens")

    def light_feed(done, *weights):
        return order.call(
            functools.partial(light_feed_body, not done), (where, a2, gfeed) + done + weights,
            [wide32, wide32] + [((width, 3 * c_lin), BF16)] * 2,
        )

    feed, da2, g_l0, g_l1 = light_feed((), l0, l1)
    l1_got = swap(g_l1, "tensor", 1, "glight")
    am, ao = tokens.result()
    bits = bits_of("dp")
    drows, back, grad_router_f, g_feed = order.call(
        heavy_feed_body, (where, gains, am, ao, picked, other, feed_w),
        [rows1, rows1, gain_row, ((dp, shard, 3 * c_hin), BF16)],
    )
    g_feed = lax.psum_scatter(g_feed, "dp", scatter_dimension=0)
    dtokens = PairSum(order, drows, "dtokens")
    l3 = swap(after(l2, drows), "tensor", 1, "light")
    dm, do = dtokens.result()
    feed, da2, g_l2, g_l3 = light_feed((feed, da2), l2, l3)
    l3_got = swap(g_l3, "tensor", 1, "glight")
    dmid, gattn, grad_gain2, ga = order.call(
        turn_body, (where, gains, index_cols, index, mid, da2, gfeed, dm, do), [wide32, wide, gain_row, rows1]
    )

    dattn = PairSum(order, ga, "dattn")
    g_l0 = order.add(g_l0, l1_got)
    g_l2 = order.add(g_l2, l3_got)
    l2_got = swap(after(g_l2, ga), "tensor", 2, "glight")

    def local_backward(which):
        args = sum((tuple(heads[i]) + local_w[i] for i in which), ())
        outs = [((rows, c_lout), BF16), ((extent, 2 * c_lout), BF16), ((width, c_lqkv + c_lout), BF16)]
        res = order.call(
            functools.partial(local_backward_body, len(which)), (where, gattn, a1) + args, outs * len(which),
            scratch=[pltpu.VMEM((extent, 2 * c_lout), F32), pltpu.VMEM((rows, c_lout), BF16)],
        )
        return [res[3 * i : 3 * i + 3] for i in range(len(which))]

    (back3,) = local_backward((3,))
    s3_got = swap(back3[2], "tensor", 1, "glocal")
    gm, go = dattn.result()
    (back1,) = local_backward((1,))
    s1_got = swap(back1[2], "tensor", 1, "glocal")
    (back2,) = local_backward((2,))
    s2 = order.add(back2[2], s3_got)
    dm, do, h_keep, h_send, grad_router_qk = order.call(
        heavy_backward_body, (where, gains, gm, go, hy, routed, hqkv, ho, hlse) + heavy_w,
        [halves2] * 2 + [((half, 4 * hw), BF16)] * 2 + [((2, width), F32)],
    )
    drows = TensorSum(order, dm, do, "drows")
    g_h = Reduce(order, h_keep, h_send, bits, "gheavy")
    (back0,) = local_backward((0,))
    drows.step()
    s0 = order.add(back0[2], s1_got)
    da1, first, last = order.call(
        functools.partial(local_input_body, tensor),
        sum(((b[0], b[1]) + w for b, w in zip((back0, back1, back2, back3), local_w)), ()),
        [wide32, ((WINDOW, width), BF16), ((WINDOW, width), BF16)],
    )
    before, behind = neighbours(first, last)
    s2_got = swap(after(s2, da1), "tensor", 2, "glocal")
    dm, do = drows.result()
    l_send = order.add(g_l0[half:], l2_got[half:])
    l_keep = order.add(g_l0[:half], l2_got[:half])
    g_l = Reduce(order, l_keep, l_send, bits, "glight")
    input_grad, small = order.call(
        finish_body, (where, src, gains, index, x, dmid, da1, before, behind, dm, do, grad_gain2, grad_router_qk, grad_router_f),
        [wide32, ((5, width), F32)],
    )
    small = small.reshape(5, dp * tensor, -1).transpose(1, 0, 2)
    with jax.named_scope("small"):
        small = lax.all_to_all(small, ("dp", "tensor"), 0, 0)

    def as_weights(terms, count, cols, back_rows):
        return order.call(weights_body, terms, [((count, shard, cols), F32), ((back_rows, shard), F32)])

    g_h.step()
    s_send = order.add(s0[half:], s2_got[half:])
    s_keep = order.add(s0[:half], s2_got[:half])
    g_s = Reduce(order, s_keep, s_send, bits, "glocal")
    g_l.step()
    back_sum = PairSum(order, order(back), "back")
    g_h.steps_but_last()
    g_s.step()
    back = back_sum.result()
    g_l.steps_but_last()
    (output,) = order.call(output_body, (where, src, index, mid, feed) + back, [wide])
    heavy_grads = as_weights(g_h.terms(), 3, hw, hw)
    g_s.steps_but_last()
    light_grads = as_weights(g_l.terms(), 2, c_lin, c_ldown)
    feed_grads = as_weights((g_feed,), 2, c_hin, c_hin)
    local_grads = as_weights(g_s.terms(), 3, c_lout, c_lout)
    small = jnp.sum(order(small), axis=0)

    return (
        output[None],
        input_grad[None],
        *local_grads,
        *heavy_grads,
        *light_grads,
        *feed_grads,
        small[:2],
        small[2:],
    )


def solution(mesh):
    rows = P("dp", "tensor", None)
    index = P("dp", None)
    cols = P(None, "dp", "tensor")
    back = P("tensor", "dp")
    both = P(None, ("dp", "tensor"))
    weights = (cols, back) * 4
    return jax.shard_map(
        local,
        mesh=mesh,
        in_specs=(rows, rows, P("dp"), index, index, index) + weights + (both, both),
        out_specs=(rows, rows) + weights + (both, both),
        check_vma=False,
    )
```
